32 devices in a mesh: dp: 4 (over y, core), mp: 8 (over z, x).
Axes of the slice: x: 2, y: 2, z: 4, core: 2. Of those that a mesh axis runs over, the one named last changes fastest.
Arguments:
- inputs: bfloat16 [32, 1024, 1024], P('dp', 'mp'), may hold values from -6 to 6
- seg_lengths: int32 [32, 8], P('dp'), may hold values from 1 to 512, 1024 in all within a row
- group_counts: int32 [4], P('dp'), may hold values from 2048 to 8192
- out_grad: bfloat16 [32, 1024, 1024], P('dp', 'mp'), may hold values from -6 to 6
- ln_gain: float32 [1024], replicated, may hold values from 0.1 to 1.9
- ln_bias: float32 [1024], replicated, may hold values from -3 to 3
- w_query: bfloat16 [1024, 1024], P(None, 'mp'), may hold values from -0.1875 to 0.1875
- w_key: bfloat16 [1024, 1024], P(None, 'mp'), may hold values from -0.1875 to 0.1875
- w_value: bfloat16 [1024, 1024], P(None, 'mp'), may hold values from -0.1875 to 0.1875
- w_output: bfloat16 [1024, 1024], P('mp'), may hold values from -0.75 to 0.75
- w_in: bfloat16 [4096, 1024], P('mp'), may hold values from -0.1875 to 0.1875
- b_in: bfloat16 [4096], P('mp'), may hold values from -3 to 3
- w_out: bfloat16 [4096, 1024], P('mp'), may hold values from -0.09375 to 0.09375
- b_out: bfloat16 [1024], replicated, may hold values from -3 to 3
Outputs:
- layer_out: bfloat16 [32, 1024, 1024], P('dp', 'mp')
- input_grad: bfloat16 [32, 1024, 1024], P('dp', 'mp')
- ln_gain_grad: float32 [1024], P(('dp', 'mp'))
- ln_bias_grad: float32 [1024], P(('dp', 'mp'))
- w_query_grad: float32 [1024, 1024], P('dp', 'mp')
- w_key_grad: float32 [1024, 1024], P('dp', 'mp')
- w_value_grad: float32 [1024, 1024], P('dp', 'mp')
- w_output_grad: float32 [1024, 1024], P('mp', 'dp')
- w_in_grad: float32 [4096, 1024], P('mp', 'dp')
- b_in_grad: float32 [4096], P('mp')
- w_out_grad: float32 [4096, 1024], P('mp', 'dp')
- b_out_grad: float32 [1024], P(('dp', 'mp'))
The draws below stay inside these ranges and needn't reach their ends.
Inputs may be any that keep to these rules, and one draw needn't show every extreme that they name: `seg_lengths`: each row's 8 lengths sum to 1024.
All inputs are finite; a program needn't handle non-finite values.
Results may differ from the reference program's by a relative error of at most 0.014.
Values may be sent and summed in bfloat16 or wider, within the bound.
A program may use at most 256 MiB of HBM per device.

```python
import math
import jax
import jax.numpy as jnp
import numpy as np
from jax import lax

D = 1024
H = 16
HD = 64
ROT = 32
FF = 4096
SEQ = 1024
SEGS = 8
MAXSEG = 512
ROWS_GRP = 8
ROWS = 32


def draw_group_counts(key, part):
    groups = ROWS // ROWS_GRP
    lowest = ROWS_GRP * SEQ // 4
    index_row = jnp.arange(groups, dtype=jnp.int32)
    ramp = lowest + 3 * lowest * index_row // max(groups - 1, 1)
    jitter = jax.random.randint(key, (groups,), 0, 2 * lowest + 1, dtype=jnp.int32)
    middle = jnp.where((index_row > 0) & (index_row < groups - 1), jitter, 0)
    return jnp.minimum(ramp + middle, 4 * lowest).astype(jnp.int32)


def steps_of(own_key, dims, pieces, low, high):
    loudness = 1.0
    for axis_at, blocks in pieces:
        draws = jax.random.uniform(jax.random.fold_in(jax.random.fold_in(own_key, 6), axis_at), (blocks,), jnp.float32, low / len(pieces), high / len(pieces))
        loudness = loudness * jnp.repeat(jnp.exp(draws), dims[axis_at] // blocks).reshape((-1,) + (1,) * (len(dims) - 1 - axis_at))
    return loudness


def split_up(number_of, total, most, slope):
    loads = [(1 << 20) // math.isqrt(grade ** slope) + 1 for grade in range(2, number_of + 1)]
    surplus, holding = total - most - (number_of - 1), [1] * (number_of - 1)
    while surplus > 0:
        free = [i for i in range(number_of - 1) if holding[i] < most]
        mass, left = sum([loads[i] for i in free]), surplus
        for i in free:
            more = min(most - holding[i], max(1, left * loads[i] // mass), surplus)
            holding[i] = holding[i] + more
            surplus = surplus - more
    return np.array([most] + holding)


def uneven(stream_key, amount, total, limit, lean):
    if amount == 2:
        one = jax.random.randint(stream_key, (), max(1, total - limit), min(limit, total - 1) + 1)
        return jnp.stack([one, total - one])
    lengths = jnp.asarray(split_up(amount, total, limit, lean), jnp.int32)
    twos = (amount - 1) // 2
    giver, taker = lengths[1:1 + 2 * twos:2], lengths[2:2 + 2 * twos:2]
    margin = jnp.minimum(giver - 1, limit - taker)
    shifted = jax.random.randint(jax.random.fold_in(stream_key, 1), (twos,), 0, 1 << 20) % (margin + 1)
    lengths = lengths.at[1:1 + 2 * twos:2].set(giver - shifted).at[2:2 + 2 * twos:2].set(taker + shifted)
    return lengths[jax.random.permutation(jax.random.fold_in(stream_key, 2), amount)]


def noise(rng, extent, deviation, limit, split=(), held_as=jnp.bfloat16):
    level = steps_of(rng, extent, split, -0.22, 0.18) if split else 1.0
    drawn = jax.random.normal(rng, extent, jnp.float32) * deviation * level
    return jnp.minimum(jnp.maximum(drawn, -limit), limit).astype(held_as)


def setup_inputs(seed: int = 0) -> dict:
    splits = jax.random.split(jax.random.key(seed), 15)
    inputs = noise(splits[0], (ROWS, SEQ, D), 1.0, 6.0, ((0, 4), (1, 8)))
    seg_lengths = jax.vmap(lambda own: uneven(own, SEGS, SEQ, MAXSEG, 2))(jax.random.split(splits[1], ROWS)).reshape((ROWS, SEGS)).astype(jnp.int32)
    group_counts = draw_group_counts(jax.random.fold_in(splits[14], 71), 0)
    out_grad = noise(splits[3], (ROWS, SEQ, D), 1.0, 6.0, ((0, 4), (1, 8)))
    ln_gain = jnp.clip(1.0 + 0.18 * jax.random.normal(splits[4], (D,), jnp.float32), 0.1, 1.9)
    ln_bias = noise(splits[5], (D,), 0.5, 3.0, (), jnp.float32)
    w_query = noise(splits[6], (D, D), D ** -0.5, 0.1875, ((1, 8),))
    w_key = noise(splits[7], (D, D), D ** -0.5, 0.1875, ((1, 8),))
    w_value = noise(splits[8], (D, D), D ** -0.5, 0.1875, ((1, 8),))
    w_output = noise(splits[9], (D, D), (D // 16) ** -0.5, 0.75, ((0, 8),))
    w_in = noise(splits[10], (FF, D), D ** -0.5, 0.1875, ((0, 8),))
    b_in = noise(splits[11], (FF,), 0.5, 3.0, ((0, 8),))
    w_out = noise(splits[12], (FF, D), FF ** -0.5, 0.09375, ((0, 8),))
    b_out = noise(splits[13], (D,), 0.5, 3.0)
    return {"inputs": inputs, "seg_lengths": seg_lengths, "group_counts": group_counts, "out_grad": out_grad, "ln_gain": ln_gain, "ln_bias": ln_bias, "w_query": w_query, "w_key": w_key, "w_value": w_value, "w_output": w_output, "w_in": w_in, "b_in": b_in, "w_out": w_out, "b_out": b_out}


@jax.custom_vjp
def low(v):
    return lax.optimization_barrier(v.astype(jnp.bfloat16)).astype(jnp.float32)

@jax.custom_vjp
def low_back(v):
    return v

def low_keep(v):
    return (low(v), None)

def low_pass(kept, grad):
    return (grad,)

def back_keep(v):
    return (v, None)

def back_low(kept, grad):
    return (low(grad),)
low.defvjp(low_keep, low_pass)
low_back.defvjp(back_keep, back_low)
EPSILON = 1e-05
HIGHEST = lax.Precision.HIGHEST

def segment_layout(seg_lengths):
    lengths_now = seg_lengths.astype(jnp.int32)
    seg_ends = jnp.cumsum(lengths_now, axis=-1).astype(jnp.int32)
    seg_starts = (seg_ends - lengths_now).astype(jnp.int32)
    places = jnp.arange(SEQ, dtype=jnp.int32)
    passed = places[None, :, None] >= seg_ends[:, None, :]
    seg_ids = lax.optimization_barrier(jnp.sum(passed.astype(jnp.int32), axis=-1)).astype(jnp.int32)
    inside = (places[None, :, None] >= seg_starts[:, None, :]) & jnp.logical_not(passed)
    begins = lax.optimization_barrier(jnp.sum(jnp.where(inside, seg_starts[:, None, :], 0), axis=-1)).astype(jnp.int32)
    return (seg_ids, (places[None, :] - begins).astype(jnp.int32))

def rotary_tables(positions):
    exponents = jnp.arange(0, ROT, 2, dtype=jnp.float32) / ROT
    freqs = jnp.power(10000.0, -exponents)
    angles = positions.astype(jnp.float32)[..., None] * freqs
    return (jnp.cos(angles)[..., None, :], jnp.sin(angles)[..., None, :])

def turn_pairs(tensor, cosines, sines):
    rotary = tensor[..., :ROT]
    passive = tensor[..., ROT:]
    paired = rotary.reshape(rotary.shape[:-1] + (ROT // 2, 2))
    evens = paired[..., 0]
    odd_part = paired[..., 1]
    turned = jnp.stack([evens * cosines - odd_part * sines, evens * sines + odd_part * cosines], axis=-1)
    return jnp.concatenate([turned.reshape(rotary.shape), passive], axis=-1)

def attend_row(operands):
    queries, keys_rot, values, seg_ids = operands
    places = jnp.arange(SEQ, dtype=jnp.int32)
    allowed = (seg_ids[:, None] == seg_ids[None, :]) & (places[:, None] >= places[None, :])
    scores = jnp.einsum('qhd,khd->hqk', queries, keys_rot, precision=HIGHEST) * (1.0 / math.sqrt(HD))
    scores = low_back(scores)
    scores = jnp.where(allowed[None], scores, -1e+30)
    probs = low(jax.nn.softmax(scores, axis=-1))
    return jnp.einsum('hqk,khd->qhd', probs, values, precision=HIGHEST)

def layer(inputs, seg_ids, cosines, sines, ln_gain, ln_bias, w_query, w_key, w_value, w_output, w_in, b_in, w_out, b_out):
    row_count = inputs.shape[0]
    mean_in = lax.optimization_barrier(jnp.mean(inputs, axis=-1, keepdims=True))
    centred = inputs - mean_in
    normed = centred * lax.rsqrt(lax.optimization_barrier(jnp.mean(centred * centred, axis=-1, keepdims=True)) + EPSILON) * ln_gain + ln_bias
    flat_rows = low(normed).reshape(row_count * SEQ, D)

    def project_heads(matrix):
        return low_back(jnp.dot(flat_rows, matrix, precision=HIGHEST)).reshape(row_count, SEQ, H, HD)
    queries = low(turn_pairs(project_heads(w_query), cosines, sines))
    keys_rot = low(turn_pairs(project_heads(w_key), cosines, sines))
    values = low(project_heads(w_value))
    context = lax.map(jax.checkpoint(attend_row), (queries, keys_rot, values, seg_ids))
    context = low(low_back(context.reshape(row_count * SEQ, D)))
    attended = low_back(jnp.dot(context, w_output, precision=HIGHEST))
    hidden = low_back(jnp.dot(flat_rows, w_in.T, precision=HIGHEST) + b_in)
    activated = low(jax.nn.gelu(hidden, approximate=True))
    mlp_out = low_back(jnp.dot(activated, w_out, precision=HIGHEST) + b_out)
    return inputs + (attended + mlp_out).reshape(row_count, SEQ, D)

def reference(inputs, seg_lengths, group_counts, out_grad, ln_gain, ln_bias, w_query, w_key, w_value, w_output, w_in, b_in, w_out, b_out):
    params = tuple((param_value.astype(jnp.float32) for param_value in (ln_gain, ln_bias, w_query, w_key, w_value, w_output, w_in, b_in, w_out, b_out)))
    groups = group_counts.shape[0]
    counted = group_counts.astype(jnp.float32)
    weights = groups * counted / jnp.sum(counted)
    seg_ids, positions = segment_layout(seg_lengths)
    cosines, sines = rotary_tables(positions)

    def regroup(tensor):
        return tensor.reshape((groups, ROWS_GRP) + tensor.shape[1:])

    def group_step(running, operands):
        block_in, block_ids, block_cos, block_sin, block_grad, block_weight = operands

        def forward(block_value, *weights_now):
            return layer(block_value, block_ids, block_cos, block_sin, *weights_now)
        result, pull_back = jax.vjp(forward, block_in.astype(jnp.float32), *params)
        pulled = pull_back(block_grad.astype(jnp.float32) * block_weight)
        running = tuple((old_sum + new_term for old_sum, new_term in zip(running, pulled[1:])))
        return (running, (result.astype(jnp.bfloat16), pulled[0].astype(jnp.bfloat16)))
    initial = tuple((jnp.zeros_like(param_value) for param_value in params))
    running, (layer_out, input_grad) = lax.scan(group_step, initial, (regroup(inputs), regroup(seg_ids), regroup(cosines), regroup(sines), regroup(out_grad), weights))
    layer_out = layer_out.reshape(inputs.shape)
    input_grad = input_grad.reshape(inputs.shape)
    return (layer_out, input_grad, running[0], running[1], running[2], running[3], running[4], running[5], running[6], running[7], running[8], running[9])
```

```python
from functools import partial
import math
import jax
import jax.numpy as jnp
from jax import lax
from jax.sharding import PartitionSpec as P
from jax.experimental import pallas as pl
from jax.experimental.pallas import tpu as pltpu


D = 1024
HD = 64
ROT = 32
SEQ = 1024


EPSILON = 1e-05


def segment_layout(seg_lengths):
    seg_ends = jnp.cumsum(seg_lengths, axis=-1)
    seg_starts = seg_ends - seg_lengths
    places = jnp.arange(SEQ, dtype=jnp.int32)
    passed = places[None, :, None] >= seg_ends[:, None, :]
    seg_ids = jnp.sum(passed.astype(jnp.int32), axis=-1)
    inside = (places[None, :, None] >= seg_starts[:, None, :]) & jnp.logical_not(passed)
    begins = jnp.sum(jnp.where(inside, seg_starts[:, None, :], 0), axis=-1)
    return (seg_ids, places[None, :] - begins)


def rotary_tables(positions):
    exponents = jnp.arange(0, ROT, 2, dtype=jnp.float32) / ROT
    freqs = jnp.power(10000.0, -exponents)
    angles = positions.astype(jnp.float32)[..., None] * freqs
    return (jnp.cos(angles)[..., None, :], jnp.sin(angles)[..., None, :])


def turn_pairs(tensor, cosines, sines):
    rotary = tensor[..., :ROT]
    passive = tensor[..., ROT:]
    paired = rotary.reshape(rotary.shape[:-1] + (ROT // 2, 2))
    evens = paired[..., 0]
    odd_part = paired[..., 1]
    turned = jnp.stack(
        [evens * cosines - odd_part * sines, evens * sines + odd_part * cosines], axis=-1
    )
    return jnp.concatenate([turned.reshape(rotary.shape), passive], axis=-1)


def norm_rows(inputs, ln_gain, ln_bias):
    values_in = inputs.astype(jnp.float32)
    centred = values_in - jnp.mean(values_in, axis=-1, keepdims=True)
    inverse = lax.rsqrt(jnp.mean(centred * centred, axis=-1, keepdims=True) + EPSILON)
    standard = centred * inverse
    return (standard, inverse, (standard * ln_gain + ln_bias).astype(jnp.bfloat16))


def masked_scores(queries, keys_rot, seg_ids):
    places = jnp.arange(SEQ, dtype=jnp.int32)
    allowed = (seg_ids[:, None] == seg_ids[None, :]) & (places[:, None] >= places[None, :])
    scores = jnp.einsum("qhd,khd->hqk", queries, keys_rot, preferred_element_type=jnp.float32) * (
        1.0 / math.sqrt(HD)
    )
    return jnp.where(allowed[None], scores, -1e30)


def attend_forward(operands):
    queries, keys_rot, values, seg_ids = operands
    scores = masked_scores(queries, keys_rot, seg_ids)
    row_peak = jnp.max(scores, axis=-1, keepdims=True)
    lifted = jnp.exp(scores - row_peak)
    row_mass = jnp.sum(lifted, axis=-1, keepdims=True)
    probs = (lifted / row_mass).astype(jnp.bfloat16)
    context = jnp.einsum("hqk,khd->qhd", probs, values, preferred_element_type=jnp.float32)
    return (context.astype(jnp.bfloat16), (row_peak + jnp.log(row_mass))[..., 0])


def attend_backward(operands):
    queries, keys_rot, values, seg_ids, log_mass, ctx_grad = operands
    score_scale = 1.0 / math.sqrt(HD)
    scores = masked_scores(queries, keys_rot, seg_ids)
    probs = jnp.exp(scores - log_mass[..., None])
    rounded = probs.astype(jnp.bfloat16)
    value_grad = jnp.einsum("hqk,qhd->khd", rounded, ctx_grad, preferred_element_type=jnp.float32)
    prob_grad = jnp.einsum("qhd,khd->hqk", ctx_grad, values, preferred_element_type=jnp.float32)
    score_grad = (probs * (prob_grad - jnp.sum(probs * prob_grad, axis=-1, keepdims=True))).astype(
        jnp.bfloat16
    )
    query_grad = (
        jnp.einsum("hqk,khd->qhd", score_grad, keys_rot, preferred_element_type=jnp.float32)
        * score_scale
    )
    key_grad = (
        jnp.einsum("hqk,qhd->khd", score_grad, queries, preferred_element_type=jnp.float32)
        * score_scale
    )
    return (query_grad, key_grad, value_grad)


def project_heads(flat_rows, matrix, row_count):
    local_heads = matrix.shape[1] // HD
    return jnp.dot(flat_rows, matrix, preferred_element_type=jnp.float32).reshape(
        row_count, -1, local_heads, HD
    )


def attention_inputs(flat_rows, w_query, w_key, w_value, cosines, sines, row_count):
    queries = turn_pairs(project_heads(flat_rows, w_query, row_count), cosines, sines).astype(
        jnp.bfloat16
    )
    keys_rot = turn_pairs(project_heads(flat_rows, w_key, row_count), cosines, sines).astype(
        jnp.bfloat16
    )
    values = project_heads(flat_rows, w_value, row_count).astype(jnp.bfloat16)
    return (queries, keys_rot, values)


def mlp_inputs(flat_rows, w_in, b_in):
    hidden = jnp.dot(flat_rows, w_in.T, preferred_element_type=jnp.float32) + b_in.astype(
        jnp.float32
    )
    return (hidden, jax.nn.gelu(hidden, approximate=True).astype(jnp.bfloat16))


def gelu_grad(hidden, act_grad):
    pulled = jax.vjp(partial(jax.nn.gelu, approximate=True), hidden)[1](act_grad)[0]
    return pulled.astype(jnp.bfloat16)


def head_products(flat_rows, query_back, key_back, value_back, w_query, w_key, w_value):
    normed_part = (
        jnp.dot(query_back, w_query.T, preferred_element_type=jnp.float32)
        + jnp.dot(key_back, w_key.T, preferred_element_type=jnp.float32)
        + jnp.dot(value_back, w_value.T, preferred_element_type=jnp.float32)
    )
    w_query_part = jnp.dot(flat_rows.T, query_back, preferred_element_type=jnp.float32)
    w_key_part = jnp.dot(flat_rows.T, key_back, preferred_element_type=jnp.float32)
    w_value_part = jnp.dot(flat_rows.T, value_back, preferred_element_type=jnp.float32)
    return (normed_part, w_query_part, w_key_part, w_value_part)


def on_device_gathered(
    inputs,
    seg_lengths,
    group_counts,
    out_grad,
    ln_gain,
    ln_bias,
    w_query,
    w_key,
    w_value,
    w_output,
    w_in,
    b_in,
    w_out,
    b_out,
):
    row_count = inputs.shape[0]
    own_tokens = inputs.shape[1]
    local_width = w_query.shape[1]
    local_heads = local_width // HD
    seg_ids, positions = segment_layout(seg_lengths)
    cosines, sines = rotary_tables(positions)
    standard, inverse, normed = norm_rows(inputs, ln_gain, ln_bias)
    base_out = inputs.astype(jnp.float32) + b_out.astype(jnp.float32)
    gathered = lax.all_gather(normed, "mp", axis=1, tiled=True)
    flat_rows = gathered.reshape(row_count * SEQ, D)
    queries, keys_rot, values = attention_inputs(
        flat_rows, w_query, w_key, w_value, cosines, sines, row_count
    )
    context, log_mass = lax.map(attend_forward, (queries, keys_rot, values, seg_ids))
    ctx_flat = context.reshape(row_count * SEQ, local_width)
    hidden, activated = mlp_inputs(flat_rows, w_in, b_in)
    partial_out = jnp.dot(ctx_flat, w_output, preferred_element_type=jnp.float32) + jnp.dot(
        activated, w_out, preferred_element_type=jnp.float32
    )
    summed = lax.psum_scatter(
        partial_out.reshape(row_count, SEQ, D).astype(jnp.bfloat16),
        "mp",
        scatter_dimension=1,
        tiled=True,
    ).astype(jnp.float32)
    layer_out = (base_out + summed).astype(jnp.bfloat16)
    counts_now = group_counts.astype(jnp.float32)
    total_count = lax.psum(counts_now, "dp")
    weight_now = lax.axis_size("dp") * counts_now[0] / total_count[0]
    own_grad = out_grad.astype(jnp.float32) * weight_now
    own_rounded = own_grad.astype(jnp.bfloat16).reshape(row_count * own_tokens, D)
    cot_rows = lax.all_gather(out_grad, "mp", axis=1, tiled=True)
    branch_grad = (
        (cot_rows.astype(jnp.float32) * weight_now).astype(jnp.bfloat16).reshape(row_count * SEQ, D)
    )
    act_grad = jnp.dot(branch_grad, w_out.T, preferred_element_type=jnp.float32)
    hidden_grad = gelu_grad(hidden, act_grad)
    w_out_part = jnp.dot(activated.T, branch_grad, preferred_element_type=jnp.float32)
    w_in_part = jnp.dot(hidden_grad.T, flat_rows, preferred_element_type=jnp.float32)
    b_in_part = jnp.sum(hidden_grad.astype(jnp.float32), axis=0)
    ctx_grad = jnp.dot(branch_grad, w_output.T, preferred_element_type=jnp.float32).astype(
        jnp.bfloat16
    )
    w_output_part = jnp.dot(ctx_flat.T, branch_grad, preferred_element_type=jnp.float32)
    rot_query_grad, rot_key_grad, value_grad = lax.map(
        attend_backward,
        (
            queries,
            keys_rot,
            values,
            seg_ids,
            log_mass,
            ctx_grad.reshape(row_count, SEQ, local_heads, HD),
        ),
    )
    query_back = (
        turn_pairs(rot_query_grad, cosines, -sines)
        .astype(jnp.bfloat16)
        .reshape(row_count, SEQ, local_width)
    )
    key_back = (
        turn_pairs(rot_key_grad, cosines, -sines)
        .astype(jnp.bfloat16)
        .reshape(row_count, SEQ, local_width)
    )
    value_back = value_grad.astype(jnp.bfloat16).reshape(row_count, SEQ, local_width)
    normed_part, w_query_part, w_key_part, w_value_part = head_products(
        flat_rows,
        query_back.reshape(row_count * SEQ, local_width),
        key_back.reshape(row_count * SEQ, local_width),
        value_back.reshape(row_count * SEQ, local_width),
        w_query,
        w_key,
        w_value,
    )
    normed_part = normed_part + jnp.dot(hidden_grad, w_in, preferred_element_type=jnp.float32)
    normed_grad = lax.psum_scatter(
        normed_part.reshape(row_count, SEQ, D).astype(jnp.bfloat16),
        "mp",
        scatter_dimension=1,
        tiled=True,
    ).astype(jnp.float32)
    scaled = normed_grad * ln_gain
    input_part = inverse * (
        scaled
        - jnp.mean(scaled, axis=-1, keepdims=True)
        - standard * jnp.mean(scaled * standard, axis=-1, keepdims=True)
    )
    input_grad = (own_grad + input_part).astype(jnp.bfloat16)
    gain_part = jnp.sum(normed_grad * standard, axis=(0, 1))
    bias_part = jnp.sum(normed_grad, axis=(0, 1))
    out_bias_part = jnp.sum(own_rounded.astype(jnp.float32), axis=0)
    ln_gain_grad, ln_bias_grad, b_out_grad = (
        lax.psum_scatter(gain_part, ("dp", "mp"), scatter_dimension=0, tiled=True),
        lax.psum_scatter(bias_part, ("dp", "mp"), scatter_dimension=0, tiled=True),
        lax.psum_scatter(out_bias_part, ("dp", "mp"), scatter_dimension=0, tiled=True),
    )
    w_query_grad, w_key_grad, w_value_grad = (
        lax.psum_scatter(
            w_query_part.astype(jnp.bfloat16), "dp", scatter_dimension=0, tiled=True
        ).astype(jnp.float32),
        lax.psum_scatter(
            w_key_part.astype(jnp.bfloat16), "dp", scatter_dimension=0, tiled=True
        ).astype(jnp.float32),
        lax.psum_scatter(
            w_value_part.astype(jnp.bfloat16), "dp", scatter_dimension=0, tiled=True
        ).astype(jnp.float32),
    )
    w_output_grad, w_in_grad, w_out_grad = (
        lax.psum_scatter(
            w_output_part.astype(jnp.bfloat16), "dp", scatter_dimension=1, tiled=True
        ).astype(jnp.float32),
        lax.psum_scatter(
            w_in_part.astype(jnp.bfloat16), "dp", scatter_dimension=1, tiled=True
        ).astype(jnp.float32),
        lax.psum_scatter(
            w_out_part.astype(jnp.bfloat16), "dp", scatter_dimension=1, tiled=True
        ).astype(jnp.float32),
    )
    b_in_grad = lax.psum(b_in_part, "dp")
    return (
        layer_out,
        input_grad,
        ln_gain_grad,
        ln_bias_grad,
        w_query_grad,
        w_key_grad,
        w_value_grad,
        w_output_grad,
        w_in_grad,
        b_in_grad,
        w_out_grad,
        b_out_grad,
    )


QB = 256

NT = (((1,), (1,)), ((), ()))
NN = (((1,), (0,)), ((), ()))


def mm(a, b, dims=NN):
    return lax.dot_general(a, b, dims, preferred_element_type=jnp.float32)


def lane_turn(x, cosines, sines):
    width = x.shape[1]
    lanes = lax.broadcasted_iota(jnp.int32, x.shape, 1)
    swapped = jnp.where(lanes % 2 == 0, pltpu.roll(x, width - 1, 1), pltpu.roll(x, 1, 1))
    return x * cosines + swapped * sines


def attn_kernel(kb_ref, start_ref, q_ref, k_ref, v_ref, do_ref, cosq_ref, sinq_ref, cos_ref, sin_ref,
                ctx_ref, dq_ref, dk_ref, dv_ref, dk_acc, dv_acc, bias_ref):
    i, hp = pl.program_id(0), pl.program_id(1)
    kb = kb_ref[i]

    @pl.when(i == 0)
    def _():
        dk_acc[hp] = jnp.zeros(dk_acc.shape[1:], jnp.float32)
        dv_acc[hp] = jnp.zeros(dv_acc.shape[1:], jnp.float32)

    def body(blocks):
        w = blocks * QB
        k0 = pl.multiple_of(kb * QB, QB)

        @pl.when(hp == 0)
        def _():
            keys = lax.broadcasted_iota(jnp.int32, (w, QB), 0) + k0
            queries = lax.broadcasted_iota(jnp.int32, (w, QB), 1) + i * QB
            fine = (keys >= start_ref[...]) & (keys <= queries)
            bias_ref[:w] = jnp.where(fine, 0.0, -1e30)

        q, do = q_ref[...], do_ref[...]
        low = lax.broadcasted_iota(jnp.int32, q.shape, 1) < HD
        zero = jnp.zeros_like(q)
        k, v = k_ref[pl.ds(k0, w), :], v_ref[pl.ds(k0, w), :]
        kt, vt = k.T, v.T
        outs, dqs = [], []
        dk_new, dv_new = dk_acc[hp, pl.ds(k0, w), :], dv_acc[hp, pl.ds(k0, w), :]
        for head in range(2):
            qh = jnp.where(low, q, zero) if head == 0 else jnp.where(low, zero, q)
            doh = jnp.where(low, do, zero) if head == 0 else jnp.where(low, zero, do)
            s = mm(k, qh, NT) + bias_ref[:w]
            e = jnp.exp(s - jnp.max(s, axis=0, keepdims=True))
            p = e * (1.0 / jnp.sum(e, axis=0, keepdims=True))
            pb = p.astype(jnp.bfloat16)
            pd = p * mm(v, doh, NT)
            ds = (pd - p * jnp.sum(pd, axis=0, keepdims=True)).astype(jnp.bfloat16)
            dv_new = dv_new + mm(pb, doh)
            dk_new = dk_new + mm(ds, qh)
            outs.append(mm(vt[head * HD:(head + 1) * HD], pb))
            dqs.append(mm(kt[head * HD:(head + 1) * HD], ds))
        dk_acc[hp, pl.ds(k0, w), :] = dk_new
        dv_acc[hp, pl.ds(k0, w), :] = dv_new
        ctx_ref[...] = jnp.concatenate(outs, axis=0).T.astype(jnp.bfloat16)
        dq = jnp.concatenate(dqs, axis=0).T * 0.125
        dq_ref[...] = lane_turn(dq, cosq_ref[...], -sinq_ref[...]).astype(jnp.bfloat16)

    for blocks in range(1, 4):
        pl.when(i - kb + 1 == blocks)(partial(body, blocks))

    @pl.when(i == pl.num_programs(0) - 1)
    def _():
        dk_ref[...] = lane_turn(dk_acc[hp], cos_ref[...], -sin_ref[...]).astype(jnp.bfloat16)
        dv_ref[...] = dv_acc[hp].astype(jnp.bfloat16)


def attention(qkv, do, starts, cosines, sines):
    width = do.shape[1]
    pairs, steps = width // 128, SEQ // QB
    kb = starts[::QB] // QB
    last = steps - 1
    qspec = pl.BlockSpec((QB, 128), lambda i, h, kb: (i, h))
    kspec = pl.BlockSpec((SEQ, 128), lambda i, h, kb: (0, pairs + h))
    vspec = pl.BlockSpec((SEQ, 128), lambda i, h, kb: (0, 2 * pairs + h))
    outk = pl.BlockSpec((SEQ, 128), lambda i, h, kb: (0, jnp.where(i == last, h, 0)))
    shape = jax.ShapeDtypeStruct((SEQ, width), jnp.bfloat16)
    ctx, dq, dk, dv = pl.pallas_call(
        attn_kernel,
        grid_spec=pltpu.PrefetchScalarGridSpec(
            num_scalar_prefetch=1, grid=(steps, pairs),
            in_specs=[pl.BlockSpec((1, QB), lambda i, h, kb: (0, i)), qspec, kspec, vspec, qspec,
                      pl.BlockSpec((QB, 128), lambda i, h, kb: (i, 0)), pl.BlockSpec((QB, 128), lambda i, h, kb: (i, 0)),
                      pl.BlockSpec((SEQ, 128), lambda i, h, kb: (0, 0)), pl.BlockSpec((SEQ, 128), lambda i, h, kb: (0, 0))],
            out_specs=[qspec, qspec, outk, outk],
            scratch_shapes=[pltpu.VMEM((pairs, SEQ, 128), jnp.float32), pltpu.VMEM((pairs, SEQ, 128), jnp.float32),
                            pltpu.VMEM((3 * QB, QB), jnp.float32)]),
        out_shape=[shape] * 4,
        compiler_params=pltpu.CompilerParams(vmem_limit_bytes=48 << 20),
        cost_estimate=pl.CostEstimate(flops=30 << 30, bytes_accessed=16 << 20, transcendentals=8 << 20),
        name="attention",
    )(kb, starts[None], qkv, qkv, qkv, do, cosines, sines, cosines, sines)
    return ctx, jnp.concatenate([dq, dk, dv], axis=1)


def lane_tables(positions):
    lanes = jnp.arange(128, dtype=jnp.int32) % HD
    exponents = (lanes // 2 * 2).astype(jnp.float32) / ROT
    angles = positions.astype(jnp.float32)[:, None] * jnp.power(10000.0, -exponents)
    turned = (lanes < ROT)[None]
    signs = jnp.where(lanes % 2 == 0, -1.0, 1.0)[None]
    return jnp.where(turned, jnp.cos(angles), 1.0), jnp.where(turned, jnp.sin(angles) * signs, 0.0)


def weight_block(ref):
    half = ref.shape[0] // 2
    rows = half * ref.shape[2]
    return jnp.concatenate(
        [ref[:half, 0].reshape(rows, 128), ref[half:, 0].reshape(rows, 128)], axis=1
    )


def qkv_kernel(x_ref, w_ref, cos_ref, sin_ref, o_ref):
    j = pl.program_id(0)
    out = mm(x_ref[...], weight_block(w_ref))

    @pl.when(j < 2)
    def _():
        cosines = jnp.concatenate([cos_ref[...]] * 2, axis=1)
        sines = jnp.concatenate([sin_ref[...]] * 2, axis=1)
        scale = jnp.where(j == 0, 0.125, 1.0)
        o_ref[...] = (lane_turn(out, cosines, sines).astype(jnp.bfloat16) * scale.astype(jnp.bfloat16))

    @pl.when(j == 2)
    def _():
        o_ref[...] = out.astype(jnp.bfloat16)


MESH_ID = pl.DeviceIdType.MESH
ZS, XS, YS, CS = 4, 2, 2, 2
G1_ROWS = 1024
G2_ROWS = 2064
SPLITS = ((0, 512), (512, 512), (0, 1024), (1024, 1040))


def place_of(z, x, y, c):
    return (z * XS + x) * (YS * CS) + y * CS + c


def gather_kernel(x_ref, gain_ref, bias_ref, count_ref, g1_ref, g2_ref,
                  normed_ref, turned_ref, row_ref, g1_out, g2_out, counts_ref,
                  nv, tv, send_sem, recv_sem, own_sem, a2a_send, a2a_recv, row_sem, turn_sem, count_send, count_recv):
    dp, mp = lax.axis_index("dp"), lax.axis_index("mp")
    y, c, z, x = dp // CS, dp % CS, mp // XS, mp % XS
    members, own = ZS * XS, x_ref.shape[1]

    def device(z, x, y, c):
        return (y * CS + c, z * XS + x)

    barrier = pltpu.get_barrier_semaphore()
    others = [(dp, lax.rem(mp + k, members)) for k in range(1, members)]
    others += [(lax.rem(dp + k, YS * CS), mp) for k in range(1, YS * CS)]
    for other in others:
        pl.semaphore_signal(barrier, inc=1, device_id=other, device_id_type=MESH_ID)
    pl.semaphore_wait(barrier, len(others))

    copies = []

    def send(block, slot, piece, target, local=False):
        src, out = (g1_ref, g1_out) if block < 2 else (g2_ref, g2_out)
        first, rows = SPLITS[block]
        spot = place_of(*piece)
        at = out.at[spot, pl.ds(first, rows)]
        copy = pltpu.make_async_remote_copy(
            src_ref=src.at[pl.ds(first, rows)] if local else at, dst_ref=at,
            send_sem=send_sem.at[block, slot], recv_sem=recv_sem.at[block, slot],
            device_id=device(*target), device_id_type=MESH_ID)
        copy.start()
        copies.append(copy)
        return copy

    recv = {}

    def hop(block, slot, piece, target, local=False):
        recv[block, slot] = send(block, slot, piece, target, local)

    flip = {"x": (z, 1 - x, y, c), "y": (z, x, 1 - y, c), "c": (z, x, y, 1 - c)}

    def orders(block):
        return ("x", "y") if block % 2 == 0 else ("y", "x")

    def begin(block):
        me = (z, x, y, c)
        for k in range(1, ZS):
            hop(block, k - 1, me, (lax.rem(z + k, ZS), x, y, c), True)
        one, two = orders(block)
        hop(block, 3, me, flip[one], True)
        hop(block, 7, me, flip[two], True)
        hop(block, 15, me, flip["c"], True)

    counts_ref[dp] = count_ref[...]
    count_copies = []
    for k in range(1, YS * CS):
        copy = pltpu.make_async_remote_copy(
            src_ref=count_ref, dst_ref=counts_ref.at[dp], send_sem=count_send.at[k], recv_sem=count_recv.at[k],
            device_id=(lax.rem(dp + k, YS * CS), mp), device_id_type=MESH_ID)
        copy.start()
        count_copies.append(copy)

    for block in range(4):
        begin(block)
    me_spot = place_of(z, x, y, c)
    own_copies = [pltpu.make_async_copy(g1_ref, g1_out.at[me_spot], own_sem.at[0]),
                  pltpu.make_async_copy(g2_ref, g2_out.at[me_spot], own_sem.at[1])]

    def normalise(k, carry):
        row = lax.rem(mp + k, members)
        value = x_ref[row].astype(jnp.float32)
        centred = value - jnp.mean(value, axis=-1, keepdims=True)
        inverse = lax.rsqrt(jnp.mean(centred * centred, axis=-1, keepdims=True) + EPSILON)
        nv[k] = (centred * inverse * gain_ref[...] + bias_ref[...]).astype(jnp.bfloat16)
        pltpu.make_async_copy(nv.at[k], normed_ref.at[row], row_sem.at[k]).start()
        return carry

    lax.fori_loop(0, members, normalise, 0)
    mine = pl.ds(pl.multiple_of(mp * own, own), own)
    row_copies = []
    for k in range(1, members):
        row = lax.rem(mp + k, members)
        pltpu.make_async_copy(nv.at[k], normed_ref.at[row], row_sem.at[k]).wait()
        copy = pltpu.make_async_remote_copy(
            src_ref=normed_ref.at[row], dst_ref=row_ref.at[mine], send_sem=a2a_send.at[k], recv_sem=a2a_recv.at[k],
            device_id=(dp, row), device_id_type=MESH_ID)
        copy.start()
        row_copies.append(copy)
    pltpu.make_async_copy(nv.at[0], normed_ref.at[mp], row_sem.at[0]).wait()
    own_row = pltpu.make_async_copy(nv.at[0], row_ref.at[mine], row_sem.at[0])
    own_row.start()
    for copy in own_copies:
        copy.start()

    def turn(k, carry):
        row = lax.rem(mp + k, members)
        tv[:, pl.ds(pl.multiple_of(row * own, own), own)] = nv[k].T
        return carry

    lax.fori_loop(0, members, turn, 0)
    width = tv.shape[0] // (YS * CS)
    turn_copies = []
    for rel in range(YS * CS):
        yr, cr = rel % YS, rel // YS
        from_block = lax.rem(y + yr, YS) * CS + lax.rem(c + cr, CS)
        copy = pltpu.make_async_copy(
            tv.at[pl.ds(pl.multiple_of(from_block * width, width), width)], turned_ref.at[rel], turn_sem.at[rel])
        copy.start()
        turn_copies.append(copy)

    for blocks in ((0, 1), (2, 3)):
        for kz in range(1, ZS):
            for block in blocks:
                one, two = orders(block)
                recv[block, kz - 1].wait_recv()
                piece = (lax.rem(z + ZS - kz, ZS), x, y, c)
                hop(block, 3 + kz, piece, flip[one])
                hop(block, 7 + kz, piece, flip[two])
                hop(block, 15 + kz, piece, flip["c"])
        for kz in range(ZS):
            for block in blocks:
                one, two = orders(block)
                recv[block, 3 + kz].wait_recv()
                zz = lax.rem(z + ZS - kz, ZS)
                piece = (zz, 1 - x, y, c) if one == "x" else (zz, x, 1 - y, c)
                hop(block, 11 + kz, piece, flip[two])
                hop(block, 19 + kz, piece, flip["c"])
        for half in range(2):
            for kz in range(ZS):
                for block in blocks:
                    one, two = orders(block)
                    recv[block, 7 + half * ZS + kz].wait_recv()
                    zz = lax.rem(z + ZS - kz, ZS)
                    if half == 0:
                        piece = (zz, x, 1 - y, c) if two == "y" else (zz, 1 - x, y, c)
                    else:
                        piece = (zz, 1 - x, 1 - y, c)
                    hop(block, 23 + half * ZS + kz, piece, flip["c"])
    for block in range(4):
        for slot in range(15, 31):
            recv[block, slot].wait_recv()
    for copy in copies:
        copy.wait_send()
    for copy in own_copies + turn_copies:
        copy.wait()
    own_row.wait()
    for copy in row_copies + count_copies:
        copy.wait()


def gather_all(inputs, ln_gain, ln_bias, counts, g1, g2):
    rows, own, width = inputs.shape
    places = ZS * XS * YS * CS
    any_space = pl.BlockSpec(memory_space=pl.ANY)
    vmem = pl.BlockSpec(memory_space=pltpu.VMEM)
    shape = jax.ShapeDtypeStruct
    half = jnp.bfloat16
    dma = pltpu.SemaphoreType.DMA
    return pl.pallas_call(
        gather_kernel,
        in_specs=[vmem, vmem, vmem, vmem, any_space, any_space],
        out_specs=[any_space] * 5 + [vmem],
        out_shape=[
            shape((rows, own, width), half),
            shape((YS * CS, width // (YS * CS), rows * own), half),
            shape((rows * own, width), half),
            shape((places,) + g1.shape, half),
            shape((places,) + g2.shape, half),
            shape((YS * CS, 8, 128), jnp.float32),
        ],
        scratch_shapes=[
            pltpu.VMEM((rows, own, width), half), pltpu.VMEM((width, rows * own), half),
            dma((4, 31)), dma((4, 31)), dma((2,)), dma((rows,)), dma((rows,)), dma((rows,)), dma((YS * CS,)),
            dma((YS * CS,)), dma((YS * CS,)),
        ],
        compiler_params=pltpu.CompilerParams(collective_id=0, has_side_effects=True, vmem_limit_bytes=40 << 20),
        name="gather_weights",
    )(inputs, ln_gain[None], ln_bias[None], counts, g1, g2)


PLACES = ZS * XS * YS * CS
PIECE = 256


def relative(dp, rel):
    return lax.rem(dp // CS + rel % YS, YS) * CS + lax.rem(dp % CS + rel // YS, CS)


def wide(ref, at, first, rows, count):
    return jnp.concatenate(
        [ref[at + (slice(first + b * rows, first + (b + 1) * rows),)] for b in range(count)], axis=-1
    )


def cotangent_kernel(place_ref, grad_ref, weight_ref, piece_ref, branch_ref, turned_ref, ctx_ref, w_ref, sum_ref):
    scaled = grad_ref[...].astype(jnp.float32) * weight_ref[...]
    branch = scaled.astype(jnp.bfloat16)
    branch_ref[...] = branch
    sum_ref[...] = jnp.sum(branch.astype(jnp.float32), axis=0, keepdims=True)
    for b in range(D // 128):
        w_ref[:, b * 128:(b + 1) * 128] = piece_ref[:, 0, b * 32:(b + 1) * 32, :].reshape(D, 128)
    ctx_ref[...] = mm(branch, w_ref[...], NT).astype(jnp.bfloat16)
    for rel in range(YS * CS):
        block = relative(place_ref[0], rel)
        turned_ref[rel] = branch_ref[:, pl.ds(pl.multiple_of(block * PIECE, PIECE), PIECE)].T


def cotangent(place, out_grad, weight, g1):
    tokens = out_grad.shape[0]
    half = jnp.bfloat16
    shape = jax.ShapeDtypeStruct
    whole = lambda *dims: pl.BlockSpec(dims, lambda i, p: (0,) * len(dims))
    return pl.pallas_call(
        cotangent_kernel,
        grid_spec=pltpu.PrefetchScalarGridSpec(
            num_scalar_prefetch=1, grid=(1,),
            in_specs=[whole(tokens, D), whole(1, 1),
                      pl.BlockSpec((PLACES, 1, 256, 128), lambda i, p: (0, 3, 0, 0))],
            out_specs=[whole(tokens, D), whole(4, PIECE, tokens), whole(tokens, D), whole(D, D), whole(1, D)]),
        out_shape=[shape((tokens, D), half), shape((4, PIECE, tokens), half), shape((tokens, D), half),
                   shape((D, D), half), shape((1, D), jnp.float32)],
        compiler_params=pltpu.CompilerParams(vmem_limit_bytes=48 << 20),
        cost_estimate=pl.CostEstimate(flops=2 << 30, bytes_accessed=14 << 20, transcendentals=0),
        name="cotangent",
    )(place, out_grad, weight, g1.reshape(PLACES, 4, 256, 128))


def project(rows, g1, cosines, sines):
    return pl.pallas_call(
        qkv_kernel,
        grid=(3, ZS),
        in_specs=[
            pl.BlockSpec((SEQ, D), lambda j, c: (0, 0)),
            pl.BlockSpec((8, 1, 256, 128), lambda j, c: (c, j, 0, 0)),
            pl.BlockSpec((SEQ, 128), lambda j, c: (0, 0)),
            pl.BlockSpec((SEQ, 128), lambda j, c: (0, 0)),
        ],
        out_specs=pl.BlockSpec((SEQ, 256), lambda j, c: (0, j * ZS + c)),
        out_shape=jax.ShapeDtypeStruct((SEQ, 3 * D), jnp.bfloat16),
        compiler_params=pltpu.CompilerParams(vmem_limit_bytes=40 << 20),
        cost_estimate=pl.CostEstimate(flops=6 << 30, bytes_accessed=14 << 20, transcendentals=0),
        name="qkv",
    )(rows, g1.reshape(PLACES, 4, 256, 128), cosines, sines)


def put_tiles(values, keep_ref, send_ref):
    for xr in range(XS):
        for yr in range(YS):
            keep_ref[yr, xr, 0] = values[xr][yr * PIECE:(yr + 1) * PIECE]
            send_ref[yr, xr, 0] = values[xr][(YS + yr) * PIECE:(YS + yr + 1) * PIECE]


def tile_specs(n, index):
    spec = pl.BlockSpec((YS, XS, 1, PIECE, n), index)
    return [spec, spec]


def tile_shapes(n):
    shape = jax.ShapeDtypeStruct((YS, XS, ZS, PIECE, n), jnp.bfloat16)
    return [shape, shape]


def by_x(x, value):
    low, high = value[:, :128], value[:, 128:]
    first = jnp.where(x == 0, low, high)
    return [first, jnp.where(x == 0, high, low)]


def back_kernel(place_ref, x_ref, w_ref, d_ref, n_ref, keep_ref, send_ref, xt_ref, acc_ref):
    step = pl.program_id(0) * pl.num_programs(1) + pl.program_id(1)

    @pl.when(step == 0)
    def _():
        for rel in range(YS * CS):
            block = relative(place_ref[0], rel)
            xt_ref[rel * PIECE:(rel + 1) * PIECE] = x_ref[:, pl.ds(pl.multiple_of(block * PIECE, PIECE), PIECE)].T
        acc_ref[...] = jnp.zeros_like(acc_ref)

    d = d_ref[...]
    acc_ref[...] += mm(d, weight_block(w_ref), NT)
    put_tiles(by_x(place_ref[1] % XS, mm(xt_ref[...], d).astype(jnp.bfloat16)), keep_ref, send_ref)

    @pl.when(step == pl.num_programs(0) * pl.num_programs(1) - 1)
    def _():
        n_ref[...] = acc_ref[...].astype(jnp.bfloat16)


def z_of(place, k):
    return lax.rem(place[1] // XS + k, ZS)


def back(place, rows, g1, grads):
    return pl.pallas_call(
        back_kernel,
        grid_spec=pltpu.PrefetchScalarGridSpec(
            num_scalar_prefetch=1, grid=(ZS, 3),
            in_specs=[
                pl.BlockSpec((SEQ, D), lambda k, j, p: (0, 0)),
                pl.BlockSpec((8, 1, 256, 128), lambda k, j, p: (z_of(p, k), j, 0, 0)),
                pl.BlockSpec((SEQ, 256), lambda k, j, p: (0, j * ZS + z_of(p, k))),
            ],
            out_specs=[pl.BlockSpec((SEQ, D), lambda k, j, p: (0, 0))]
            + tile_specs(128, lambda k, j, p: (0, 0, k, 0, j)),
            scratch_shapes=[pltpu.VMEM((D, SEQ), jnp.bfloat16), pltpu.VMEM((SEQ, D), jnp.float32)]),
        out_shape=[jax.ShapeDtypeStruct((SEQ, D), jnp.bfloat16)] + tile_shapes(384),
        compiler_params=pltpu.CompilerParams(vmem_limit_bytes=48 << 20),
        cost_estimate=pl.CostEstimate(flops=12 << 30, bytes_accessed=22 << 20, transcendentals=0),
        name="attention_back",
    )(place, rows, g1.reshape(PLACES, 4, 256, 128), grads)


C0 = math.sqrt(2.0 / math.pi)


def mlp_kernel(first, place_ref, x_ref, xt_ref, g_ref, gt_ref, wa_ref, wb_ref, *refs):
    if first:
        out_ref, dn_ref, keep_ref, send_ref, bsum_ref, out_acc, dn_acc = refs
    else:
        out_in, dn_in, out_ref, dn_ref, keep_ref, send_ref, bsum_ref, out_acc, dn_acc = refs
    step = pl.program_id(0)

    @pl.when(step == 0)
    def _():
        out_acc[...] = jnp.zeros_like(out_acc) if first else out_in[...]
        dn_acc[...] = jnp.zeros_like(dn_acc) if first else dn_in[...]

    w_in = jnp.concatenate([wide(r, (0, 0, p), 0, 128, 8) for r in (wa_ref, wb_ref) for p in range(CS)], axis=0)
    w_out = jnp.concatenate([wide(r, (0, 0, p), 1024, 128, 8) for r in (wa_ref, wb_ref) for p in range(CS)], axis=0)
    bias = jnp.concatenate([r[0, 0, p, 2048:2049] for r in (wa_ref, wb_ref) for p in range(CS)], axis=1)
    x = mm(x_ref[...], w_in, NT) + bias.astype(jnp.float32)
    squared = x * x
    tanh = jnp.tanh(C0 * x * (1.0 + 0.044715 * squared))
    half = 0.5 * (1.0 + tanh)
    act = (x * half).astype(jnp.bfloat16)
    slope = half + 0.5 * x * (1.0 - tanh * tanh) * (C0 * (1.0 + 3 * 0.044715 * squared))
    hid = (mm(g_ref[...], w_out, NT) * slope).astype(jnp.bfloat16)
    out_acc[...] += mm(act, w_out)
    dn_acc[...] += mm(hid, w_in)
    bsum_ref[0] = jnp.sum(hid.astype(jnp.float32), axis=0, keepdims=True)
    out_part = mm(gt_ref[...], act).astype(jnp.bfloat16)
    in_part = mm(xt_ref[...], hid).astype(jnp.bfloat16)
    put_tiles(
        [jnp.concatenate([out_part[:, a * 256:(a + 1) * 256], in_part[:, a * 256:(a + 1) * 256]], axis=1)
         for a in range(XS)], keep_ref, send_ref)

    @pl.when(step == pl.num_programs(0) - 1)
    def _():
        out_ref[...] = out_acc[...]
        dn_ref[...] = dn_acc[...]


def mlp_half(h, place, normed, normed_turned, branch, branch_turned, g2, sums):
    tokens = normed.shape[0]
    one = lambda *dims: pl.BlockSpec(dims, lambda k, p: (0,) * len(dims), pipeline_mode=pl.Buffered(1))
    weight = lambda xr: pl.BlockSpec(
        (1, 1, CS, G2_ROWS, 128),
        lambda k, p: (z_of(p, k) * XS + lax.rem(p[1] % XS + xr, XS), h, 0, 0, 0))
    views = g2.reshape(ZS * XS, YS, CS, G2_ROWS, 128)
    full = jax.ShapeDtypeStruct((tokens, D), jnp.float32)
    return pl.pallas_call(
        partial(mlp_kernel, not sums),
        grid_spec=pltpu.PrefetchScalarGridSpec(
            num_scalar_prefetch=1, grid=(ZS,),
            in_specs=[one(tokens, D), one(D, tokens), one(tokens, D), one(D, tokens), weight(0), weight(1)]
            + [one(tokens, D)] * len(sums),
            out_specs=[one(tokens, D), one(tokens, D)] + tile_specs(512, lambda k, p: (0, 0, k, 0, 0))
            + [pl.BlockSpec((1, 1, 512), lambda k, p: (k, 0, 0))],
            scratch_shapes=[pltpu.VMEM((tokens, D), jnp.float32), pltpu.VMEM((tokens, D), jnp.float32)]),
        out_shape=[full, full] + tile_shapes(512) + [jax.ShapeDtypeStruct((ZS, 1, 512), jnp.float32)],
        compiler_params=pltpu.CompilerParams(vmem_limit_bytes=62 << 20),
        cost_estimate=pl.CostEstimate(flops=26 << 30, bytes_accessed=30 << 20, transcendentals=2 << 20),
        name="mlp",
    )(place, normed, normed_turned.reshape(D, tokens), branch, branch_turned.reshape(D, tokens), views, views, *sums)


def output_kernel(place_ref, ctx_ref, w_ref, gt_ref, x_ref, mlp_ref, b_ref, out_ref, keep_ref, send_ref, acc_ref):
    step = pl.program_id(0)
    ctx = ctx_ref[...]

    @pl.when(step == 0)
    def _():
        acc_ref[...] = x_ref[...].astype(jnp.float32) + b_ref[...].astype(jnp.float32) + mlp_ref[...]

    acc_ref[...] += mm(ctx, w_ref[...])
    put_tiles(by_x(place_ref[1] % XS, mm(gt_ref[...], ctx).astype(jnp.bfloat16)), keep_ref, send_ref)

    @pl.when(step == pl.num_programs(0) - 1)
    def _():
        out_ref[...] = acc_ref[...].astype(jnp.bfloat16)


def layer_output(place, context, w_output, branch_turned, inputs, mlp_out, b_out):
    tokens = context.shape[0]
    whole = lambda *dims: pl.BlockSpec(dims, lambda k, p: (0,) * len(dims), pipeline_mode=pl.Buffered(1))
    return pl.pallas_call(
        output_kernel,
        grid_spec=pltpu.PrefetchScalarGridSpec(
            num_scalar_prefetch=1, grid=(ZS,),
            in_specs=[
                pl.BlockSpec((tokens, 256), lambda k, p: (0, z_of(p, k))),
                pl.BlockSpec((256, D), lambda k, p: (z_of(p, k), 0)),
                whole(D, tokens), whole(tokens, D), whole(tokens, D), whole(1, D),
            ],
            out_specs=[whole(tokens, D)] + tile_specs(128, lambda k, p: (0, 0, k, 0, 0)),
            scratch_shapes=[pltpu.VMEM((tokens, D), jnp.float32)]),
        out_shape=[jax.ShapeDtypeStruct((tokens, D), jnp.bfloat16)] + tile_shapes(128),
        compiler_params=pltpu.CompilerParams(vmem_limit_bytes=48 << 20),
        cost_estimate=pl.CostEstimate(flops=4 << 30, bytes_accessed=18 << 20, transcendentals=0),
        name="layer_output",
    )(place, context, w_output, branch_turned.reshape(D, tokens), inputs, mlp_out, b_out[None])


def norm_back_kernel(x_ref, g_ref, a_ref, m_ref, gain_ref, weight_ref, out_ref, sums_ref):
    x = x_ref[...].astype(jnp.float32)
    centred = x - jnp.mean(x, axis=-1, keepdims=True)
    inverse = lax.rsqrt(jnp.mean(centred * centred, axis=-1, keepdims=True) + EPSILON)
    standard = centred * inverse
    grad = a_ref[...].astype(jnp.float32) + m_ref[...]
    scaled = grad * gain_ref[...]
    part = inverse * (
        scaled
        - jnp.mean(scaled, axis=-1, keepdims=True)
        - standard * jnp.mean(scaled * standard, axis=-1, keepdims=True)
    )
    out_ref[...] = (g_ref[...].astype(jnp.float32) * weight_ref[...] + part).astype(jnp.bfloat16)
    sums = jnp.concatenate(
        [jnp.sum(grad * standard, axis=0, keepdims=True), jnp.sum(grad, axis=0, keepdims=True)], axis=0)

    @pl.when(pl.program_id(0) == 0)
    def _():
        sums_ref[...] = sums

    @pl.when(pl.program_id(0) > 0)
    def _():
        sums_ref[...] += sums


def norm_back(inputs, out_grad, attn_grad, mlp_grad, ln_gain, weight):
    tokens = inputs.shape[0]
    block = pl.BlockSpec((128, D), lambda i: (i, 0))
    return pl.pallas_call(
        norm_back_kernel,
        grid=(tokens // 128,),
        in_specs=[block] * 4 + [pl.BlockSpec((1, D), lambda i: (0, 0)), pl.BlockSpec((1, 1), lambda i: (0, 0))],
        out_specs=[block, pl.BlockSpec((2, D), lambda i: (0, 0))],
        out_shape=[jax.ShapeDtypeStruct((tokens, D), jnp.bfloat16), jax.ShapeDtypeStruct((2, D), jnp.float32)],
        cost_estimate=pl.CostEstimate(flops=20 << 20, bytes_accessed=12 << 20, transcendentals=0),
        name="norm_back",
    )(inputs, out_grad, attn_grad, mlp_grad, ln_gain[None], weight)


def pass_over(tensor, axis, k=1):
    if axis == "c":
        return lax.ppermute(tensor, "dp", [(i, i ^ 1) for i in range(YS * CS)])
    if axis == "y":
        return lax.ppermute(tensor, "dp", [(i, i ^ 2) for i in range(YS * CS)])
    if axis == "x":
        return lax.ppermute(tensor, "mp", [(i, i ^ 1) for i in range(ZS * XS)])
    return lax.ppermute(
        tensor, "mp", [(i, (i // XS + k) % ZS * XS + i % XS) for i in range(ZS * XS)])


def plus(a, b):
    return (a.astype(jnp.float32) + b.astype(jnp.float32)).astype(jnp.bfloat16)


def reduce_tiles(keep, send):
    got = pass_over(send, "c")
    away, stay = plus(keep[1], got[1]), plus(keep[0], got[0])
    got = pass_over(away, "y")
    away, stay = plus(stay[1], got[1]), plus(stay[0], got[0])
    got = pass_over(away, "x")
    parts = plus(stay, got)
    total = parts[0].astype(jnp.float32)
    for k in range(1, ZS):
        total = total + pass_over(parts[k], "z", k).astype(jnp.float32)
    return total


def reduce_all(vector):
    for axis in ("c", "y", "x"):
        vector = vector + pass_over(vector, axis)
    return vector + pass_over(vector, "z", 1) + pass_over(vector, "z", 2) + pass_over(vector, "z", 3)


def on_device_rows(
    inputs,
    seg_lengths,
    group_counts,
    out_grad,
    ln_gain,
    ln_bias,
    w_query,
    w_key,
    w_value,
    w_output,
    w_in,
    b_in,
    w_out,
    b_out,
):
    row_count, own_tokens = inputs.shape[0], inputs.shape[1]
    tokens = row_count * own_tokens
    group, member = lax.axis_index("dp"), lax.axis_index("mp")
    place = jnp.stack([group, member]).astype(jnp.int32)

    def quarter(matrix, axis):
        size = matrix.shape[axis] // (YS * CS)
        return lax.dynamic_slice_in_dim(matrix, group * size, size, axis)

    def narrow(matrix):
        return matrix.reshape(matrix.shape[0], D // 128, 128).transpose(1, 0, 2).reshape(-1, 128)

    def exchange(tensor):
        blocks = tensor.reshape(row_count, own_tokens, D)
        return lax.all_to_all(blocks, "mp", 0, 0, tiled=True).reshape(tokens, D)

    counts = jnp.broadcast_to(group_counts.astype(jnp.float32)[:, None], (8, 128))
    g1 = jnp.concatenate(
        [quarter(w_query, 0), quarter(w_key, 0), quarter(w_value, 0), narrow(quarter(w_output, 0))], axis=0)
    bias_rows = jnp.pad(quarter(b_in, 0)[None], ((0, G2_ROWS - 2049), (0, 0)))
    g2 = jnp.concatenate([narrow(quarter(w_in, 0)), narrow(quarter(w_out, 0)), bias_rows], axis=0)
    normed, normed_turned, normed_row, g1_all, g2_all, counts_all = gather_all(
        inputs, ln_gain, ln_bias, counts, g1, g2)
    normed = normed.reshape(tokens, D)
    weight = (YS * CS * counts_all[group, 0, 0] / jnp.sum(counts_all[:, 0, 0])).reshape(1, 1)

    flat_grad = out_grad.reshape(tokens, D)
    branch, branch_turned, ctx_grad, w_output_all, out_sum = cotangent(place, flat_grad, weight, g1_all)
    ctx_grad_row = exchange(ctx_grad)
    own_row = lax.dynamic_index_in_dim(seg_lengths, member, 0, keepdims=True)
    _, positions = segment_layout(own_row)
    positions = positions[0]
    cosines, sines = lane_tables(positions)
    starts = jnp.arange(SEQ, dtype=jnp.int32) - positions
    qkv = project(normed_row, g1_all, cosines, sines)
    mlp_out, mlp_grad, keep0, send0, bsum0 = mlp_half(
        0, place, normed, normed_turned, branch, branch_turned, g2_all, ())
    tiles0 = reduce_tiles(keep0, send0)
    context_row, qkv_grad = attention(qkv, ctx_grad_row, starts, cosines, sines)
    context = exchange(context_row)
    normed_row_grad, keep_a, send_a = back(place, normed_row, g1_all, qkv_grad)
    attn_grad = exchange(normed_row_grad)
    tiles_a = reduce_tiles(keep_a, send_a)
    mlp_out, mlp_grad, keep1, send1, bsum1 = mlp_half(
        1, place, normed, normed_turned, branch, branch_turned, g2_all, (mlp_out, mlp_grad))
    tiles1 = reduce_tiles(keep1, send1)
    layer_out, keep_o, send_o = layer_output(
        place, context, w_output_all, branch_turned, inputs.reshape(tokens, D), mlp_out, b_out)
    tiles_o = reduce_tiles(keep_o, send_o)
    input_grad, sums = norm_back(inputs.reshape(tokens, D), flat_grad, attn_grad, mlp_grad, ln_gain, weight)

    bsums = jnp.stack([bsum0, bsum1]).reshape(YS, ZS * XS, CS, 128)
    targets = jnp.arange(ZS * XS)
    spots = (targets // XS - member // XS) % ZS * XS + (targets % XS - member % XS) % XS
    bsums = jnp.take(bsums, spots, axis=1).transpose(1, 0, 2, 3).reshape(ZS * XS * 4, 128)
    early = reduce_all(jnp.concatenate([bsums, out_sum.reshape(8, 128)], axis=0))
    late = reduce_all(sums)
    b_in_grad = lax.dynamic_slice_in_dim(early, member * 4, 4, 0).reshape(512)
    own_place = group * (ZS * XS) + member
    pick = lambda vector: lax.dynamic_slice_in_dim(vector, own_place * (D // PLACES), D // PLACES, 0)
    b_out_grad = pick(early[ZS * XS * 4:].reshape(D))
    shape = (row_count, own_tokens, D)
    return (
        layer_out.reshape(shape),
        input_grad.reshape(shape),
        pick(sums_row(late, 0)),
        pick(sums_row(late, 1)),
        tiles_a[:, :128],
        tiles_a[:, 128:256],
        tiles_a[:, 256:],
        tiles_o.T,
        jnp.concatenate([tiles0[:, 256:], tiles1[:, 256:]], axis=1).T,
        b_in_grad,
        jnp.concatenate([tiles0[:, :256], tiles1[:, :256]], axis=1).T,
        b_out_grad,
    )


def sums_row(sums, i):
    return sums[i]


def solution(mesh):
    placed = (
        P("dp", "mp", None),
        P("dp", None),
        P("dp"),
        P("dp", "mp", None),
        P(),
        P(),
        P(None, "mp"),
        P(None, "mp"),
        P(None, "mp"),
        P("mp", None),
        P("mp", None),
        P("mp"),
        P("mp", None),
        P(),
    )
    sizes = (mesh.shape["dp"], mesh.shape["mp"])

    def on_device(*args):
        if sizes == (YS * CS, ZS * XS) and args[0].shape[0] == ZS * XS:
            return on_device_rows(*args)
        return on_device_gathered(*args)

    return jax.shard_map(
        on_device,
        mesh=mesh,
        in_specs=placed,
        out_specs=(
            P("dp", "mp", None),
            P("dp", "mp", None),
            P(("dp", "mp")),
            P(("dp", "mp")),
            P("dp", "mp"),
            P("dp", "mp"),
            P("dp", "mp"),
            P("mp", "dp"),
            P("mp", "dp"),
            P("mp"),
            P("mp", "dp"),
            P(("dp", "mp")),
        ),
        check_vma=False,
    )
```

```python
from functools import partial
import math
import jax
import jax.numpy as jnp
from jax import lax
from jax.sharding import PartitionSpec as P
from jax.experimental import pallas as pl
from jax.experimental.pallas import tpu as pltpu


D = 1024
HD = 64
ROT = 32
SEQ = 1024


EPSILON = 1e-05


def segment_layout(seg_lengths):
    seg_ends = jnp.cumsum(seg_lengths, axis=-1)
    seg_starts = seg_ends - seg_lengths
    places = jnp.arange(SEQ, dtype=jnp.int32)
    passed = places[None, :, None] >= seg_ends[:, None, :]
    seg_ids = jnp.sum(passed.astype(jnp.int32), axis=-1)
    inside = (places[None, :, None] >= seg_starts[:, None, :]) & jnp.logical_not(passed)
    begins = jnp.sum(jnp.where(inside, seg_starts[:, None, :], 0), axis=-1)
    return (seg_ids, places[None, :] - begins)


def rotary_tables(positions):
    exponents = jnp.arange(0, ROT, 2, dtype=jnp.float32) / ROT
    freqs = jnp.power(10000.0, -exponents)
    angles = positions.astype(jnp.float32)[..., None] * freqs
    return (jnp.cos(angles)[..., None, :], jnp.sin(angles)[..., None, :])


def turn_pairs(tensor, cosines, sines):
    rotary = tensor[..., :ROT]
    passive = tensor[..., ROT:]
    paired = rotary.reshape(rotary.shape[:-1] + (ROT // 2, 2))
    evens = paired[..., 0]
    odd_part = paired[..., 1]
    turned = jnp.stack(
        [evens * cosines - odd_part * sines, evens * sines + odd_part * cosines], axis=-1
    )
    return jnp.concatenate([turned.reshape(rotary.shape), passive], axis=-1)


def norm_rows(inputs, ln_gain, ln_bias):
    values_in = inputs.astype(jnp.float32)
    centred = values_in - jnp.mean(values_in, axis=-1, keepdims=True)
    inverse = lax.rsqrt(jnp.mean(centred * centred, axis=-1, keepdims=True) + EPSILON)
    standard = centred * inverse
    return (standard, inverse, (standard * ln_gain + ln_bias).astype(jnp.bfloat16))


def masked_scores(queries, keys_rot, seg_ids):
    places = jnp.arange(SEQ, dtype=jnp.int32)
    allowed = (seg_ids[:, None] == seg_ids[None, :]) & (places[:, None] >= places[None, :])
    scores = jnp.einsum("qhd,khd->hqk", queries, keys_rot, preferred_element_type=jnp.float32) * (
        1.0 / math.sqrt(HD)
    )
    return jnp.where(allowed[None], scores, -1e30)


def attend_forward(operands):
    queries, keys_rot, values, seg_ids = operands
    scores = masked_scores(queries, keys_rot, seg_ids)
    row_peak = jnp.max(scores, axis=-1, keepdims=True)
    lifted = jnp.exp(scores - row_peak)
    row_mass = jnp.sum(lifted, axis=-1, keepdims=True)
    probs = (lifted / row_mass).astype(jnp.bfloat16)
    context = jnp.einsum("hqk,khd->qhd", probs, values, preferred_element_type=jnp.float32)
    return (context.astype(jnp.bfloat16), (row_peak + jnp.log(row_mass))[..., 0])


def attend_backward(operands):
    queries, keys_rot, values, seg_ids, log_mass, ctx_grad = operands
    score_scale = 1.0 / math.sqrt(HD)
    scores = masked_scores(queries, keys_rot, seg_ids)
    probs = jnp.exp(scores - log_mass[..., None])
    rounded = probs.astype(jnp.bfloat16)
    value_grad = jnp.einsum("hqk,qhd->khd", rounded, ctx_grad, preferred_element_type=jnp.float32)
    prob_grad = jnp.einsum("qhd,khd->hqk", ctx_grad, values, preferred_element_type=jnp.float32)
    score_grad = (probs * (prob_grad - jnp.sum(probs * prob_grad, axis=-1, keepdims=True))).astype(
        jnp.bfloat16
    )
    query_grad = (
        jnp.einsum("hqk,khd->qhd", score_grad, keys_rot, preferred_element_type=jnp.float32)
        * score_scale
    )
    key_grad = (
        jnp.einsum("hqk,qhd->khd", score_grad, queries, preferred_element_type=jnp.float32)
        * score_scale
    )
    return (query_grad, key_grad, value_grad)


def project_heads(flat_rows, matrix, row_count):
    local_heads = matrix.shape[1] // HD
    return jnp.dot(flat_rows, matrix, preferred_element_type=jnp.float32).reshape(
        row_count, -1, local_heads, HD
    )


def attention_inputs(flat_rows, w_query, w_key, w_value, cosines, sines, row_count):
    queries = turn_pairs(project_heads(flat_rows, w_query, row_count), cosines, sines).astype(
        jnp.bfloat16
    )
    keys_rot = turn_pairs(project_heads(flat_rows, w_key, row_count), cosines, sines).astype(
        jnp.bfloat16
    )
    values = project_heads(flat_rows, w_value, row_count).astype(jnp.bfloat16)
    return (queries, keys_rot, values)


def mlp_inputs(flat_rows, w_in, b_in):
    hidden = jnp.dot(flat_rows, w_in.T, preferred_element_type=jnp.float32) + b_in.astype(
        jnp.float32
    )
    return (hidden, jax.nn.gelu(hidden, approximate=True).astype(jnp.bfloat16))


def gelu_grad(hidden, act_grad):
    pulled = jax.vjp(partial(jax.nn.gelu, approximate=True), hidden)[1](act_grad)[0]
    return pulled.astype(jnp.bfloat16)


def head_products(flat_rows, query_back, key_back, value_back, w_query, w_key, w_value):
    normed_part = (
        jnp.dot(query_back, w_query.T, preferred_element_type=jnp.float32)
        + jnp.dot(key_back, w_key.T, preferred_element_type=jnp.float32)
        + jnp.dot(value_back, w_value.T, preferred_element_type=jnp.float32)
    )
    w_query_part = jnp.dot(flat_rows.T, query_back, preferred_element_type=jnp.float32)
    w_key_part = jnp.dot(flat_rows.T, key_back, preferred_element_type=jnp.float32)
    w_value_part = jnp.dot(flat_rows.T, value_back, preferred_element_type=jnp.float32)
    return (normed_part, w_query_part, w_key_part, w_value_part)


def on_device_gathered(
    inputs,
    seg_lengths,
    group_counts,
    out_grad,
    ln_gain,
    ln_bias,
    w_query,
    w_key,
    w_value,
    w_output,
    w_in,
    b_in,
    w_out,
    b_out,
):
    row_count = inputs.shape[0]
    own_tokens = inputs.shape[1]
    local_width = w_query.shape[1]
    local_heads = local_width // HD
    seg_ids, positions = segment_layout(seg_lengths)
    cosines, sines = rotary_tables(positions)
    standard, inverse, normed = norm_rows(inputs, ln_gain, ln_bias)
    base_out = inputs.astype(jnp.float32) + b_out.astype(jnp.float32)
    gathered = lax.all_gather(normed, "mp", axis=1, tiled=True)
    flat_rows = gathered.reshape(row_count * SEQ, D)
    queries, keys_rot, values = attention_inputs(
        flat_rows, w_query, w_key, w_value, cosines, sines, row_count
    )
    context, log_mass = lax.map(attend_forward, (queries, keys_rot, values, seg_ids))
    ctx_flat = context.reshape(row_count * SEQ, local_width)
    hidden, activated = mlp_inputs(flat_rows, w_in, b_in)
    partial_out = jnp.dot(ctx_flat, w_output, preferred_element_type=jnp.float32) + jnp.dot(
        activated, w_out, preferred_element_type=jnp.float32
    )
    summed = lax.psum_scatter(
        partial_out.reshape(row_count, SEQ, D).astype(jnp.bfloat16),
        "mp",
        scatter_dimension=1,
        tiled=True,
    ).astype(jnp.float32)
    layer_out = (base_out + summed).astype(jnp.bfloat16)
    counts_now = group_counts.astype(jnp.float32)
    total_count = lax.psum(counts_now, "dp")
    weight_now = lax.axis_size("dp") * counts_now[0] / total_count[0]
    own_grad = out_grad.astype(jnp.float32) * weight_now
    own_rounded = own_grad.astype(jnp.bfloat16).reshape(row_count * own_tokens, D)
    cot_rows = lax.all_gather(out_grad, "mp", axis=1, tiled=True)
    branch_grad = (
        (cot_rows.astype(jnp.float32) * weight_now).astype(jnp.bfloat16).reshape(row_count * SEQ, D)
    )
    act_grad = jnp.dot(branch_grad, w_out.T, preferred_element_type=jnp.float32)
    hidden_grad = gelu_grad(hidden, act_grad)
    w_out_part = jnp.dot(activated.T, branch_grad, preferred_element_type=jnp.float32)
    w_in_part = jnp.dot(hidden_grad.T, flat_rows, preferred_element_type=jnp.float32)
    b_in_part = jnp.sum(hidden_grad.astype(jnp.float32), axis=0)
    ctx_grad = jnp.dot(branch_grad, w_output.T, preferred_element_type=jnp.float32).astype(
        jnp.bfloat16
    )
    w_output_part = jnp.dot(ctx_flat.T, branch_grad, preferred_element_type=jnp.float32)
    rot_query_grad, rot_key_grad, value_grad = lax.map(
        attend_backward,
        (
            queries,
            keys_rot,
            values,
            seg_ids,
            log_mass,
            ctx_grad.reshape(row_count, SEQ, local_heads, HD),
        ),
    )
    query_back = (
        turn_pairs(rot_query_grad, cosines, -sines)
        .astype(jnp.bfloat16)
        .reshape(row_count, SEQ, local_width)
    )
    key_back = (
        turn_pairs(rot_key_grad, cosines, -sines)
        .astype(jnp.bfloat16)
        .reshape(row_count, SEQ, local_width)
    )
    value_back = value_grad.astype(jnp.bfloat16).reshape(row_count, SEQ, local_width)
    normed_part, w_query_part, w_key_part, w_value_part = head_products(
        flat_rows,
        query_back.reshape(row_count * SEQ, local_width),
        key_back.reshape(row_count * SEQ, local_width),
        value_back.reshape(row_count * SEQ, local_width),
        w_query,
        w_key,
        w_value,
    )
    normed_part = normed_part + jnp.dot(hidden_grad, w_in, preferred_element_type=jnp.float32)
    normed_grad = lax.psum_scatter(
        normed_part.reshape(row_count, SEQ, D).astype(jnp.bfloat16),
        "mp",
        scatter_dimension=1,
        tiled=True,
    ).astype(jnp.float32)
    scaled = normed_grad * ln_gain
    input_part = inverse * (
        scaled
        - jnp.mean(scaled, axis=-1, keepdims=True)
        - standard * jnp.mean(scaled * standard, axis=-1, keepdims=True)
    )
    input_grad = (own_grad + input_part).astype(jnp.bfloat16)
    gain_part = jnp.sum(normed_grad * standard, axis=(0, 1))
    bias_part = jnp.sum(normed_grad, axis=(0, 1))
    out_bias_part = jnp.sum(own_rounded.astype(jnp.float32), axis=0)
    ln_gain_grad, ln_bias_grad, b_out_grad = (
        lax.psum_scatter(gain_part, ("dp", "mp"), scatter_dimension=0, tiled=True),
        lax.psum_scatter(bias_part, ("dp", "mp"), scatter_dimension=0, tiled=True),
        lax.psum_scatter(out_bias_part, ("dp", "mp"), scatter_dimension=0, tiled=True),
    )
    w_query_grad, w_key_grad, w_value_grad = (
        lax.psum_scatter(
            w_query_part.astype(jnp.bfloat16), "dp", scatter_dimension=0, tiled=True
        ).astype(jnp.float32),
        lax.psum_scatter(
            w_key_part.astype(jnp.bfloat16), "dp", scatter_dimension=0, tiled=True
        ).astype(jnp.float32),
        lax.psum_scatter(
            w_value_part.astype(jnp.bfloat16), "dp", scatter_dimension=0, tiled=True
        ).astype(jnp.float32),
    )
    w_output_grad, w_in_grad, w_out_grad = (
        lax.psum_scatter(
            w_output_part.astype(jnp.bfloat16), "dp", scatter_dimension=1, tiled=True
        ).astype(jnp.float32),
        lax.psum_scatter(
            w_in_part.astype(jnp.bfloat16), "dp", scatter_dimension=1, tiled=True
        ).astype(jnp.float32),
        lax.psum_scatter(
            w_out_part.astype(jnp.bfloat16), "dp", scatter_dimension=1, tiled=True
        ).astype(jnp.float32),
    )
    b_in_grad = lax.psum(b_in_part, "dp")
    return (
        layer_out,
        input_grad,
        ln_gain_grad,
        ln_bias_grad,
        w_query_grad,
        w_key_grad,
        w_value_grad,
        w_output_grad,
        w_in_grad,
        b_in_grad,
        w_out_grad,
        b_out_grad,
    )


QB = 256

NT = (((1,), (1,)), ((), ()))
NN = (((1,), (0,)), ((), ()))


def mm(a, b, dims=NN):
    return lax.dot_general(a, b, dims, preferred_element_type=jnp.float32)


def lane_turn(x, cosines, sines):
    width = x.shape[1]
    lanes = lax.broadcasted_iota(jnp.int32, x.shape, 1)
    swapped = jnp.where(lanes % 2 == 0, pltpu.roll(x, width - 1, 1), pltpu.roll(x, 1, 1))
    return x * cosines + swapped * sines


def attn_kernel(kb_ref, start_ref, q_ref, k_ref, v_ref, do_ref, cosq_ref, sinq_ref, cos_ref, sin_ref,
                ctx_ref, dq_ref, dk_ref, dv_ref, dk_acc, dv_acc, bias_ref):
    i, hp = pl.program_id(0), pl.program_id(1)
    kb = kb_ref[i]

    @pl.when(i == 0)
    def _():
        dk_acc[hp] = jnp.zeros(dk_acc.shape[1:], jnp.float32)
        dv_acc[hp] = jnp.zeros(dv_acc.shape[1:], jnp.float32)

    def body(blocks):
        w = blocks * QB
        k0 = pl.multiple_of(kb * QB, QB)

        @pl.when(hp == 0)
        def _():
            keys = lax.broadcasted_iota(jnp.int32, (w, QB), 0) + k0
            queries = lax.broadcasted_iota(jnp.int32, (w, QB), 1) + i * QB
            fine = (keys >= start_ref[...]) & (keys <= queries)
            bias_ref[:w] = jnp.where(fine, 0.0, -1e30)

        q, do = q_ref[...], do_ref[...]
        low = lax.broadcasted_iota(jnp.int32, q.shape, 1) < HD
        zero = jnp.zeros_like(q)
        k, v = k_ref[pl.ds(k0, w), :], v_ref[pl.ds(k0, w), :]
        kt, vt = k.T, v.T
        outs, dqs = [], []
        dk_new, dv_new = dk_acc[hp, pl.ds(k0, w), :], dv_acc[hp, pl.ds(k0, w), :]
        for head in range(2):
            qh = jnp.where(low, q, zero) if head == 0 else jnp.where(low, zero, q)
            doh = jnp.where(low, do, zero) if head == 0 else jnp.where(low, zero, do)
            s = mm(k, qh, NT) + bias_ref[:w]
            e = jnp.exp(s - jnp.max(s, axis=0, keepdims=True))
            p = e * (1.0 / jnp.sum(e, axis=0, keepdims=True))
            pb = p.astype(jnp.bfloat16)
            pd = p * mm(v, doh, NT)
            ds = (pd - p * jnp.sum(pd, axis=0, keepdims=True)).astype(jnp.bfloat16)
            dv_new = dv_new + mm(pb, doh)
            dk_new = dk_new + mm(ds, qh)
            outs.append(mm(vt[head * HD:(head + 1) * HD], pb))
            dqs.append(mm(kt[head * HD:(head + 1) * HD], ds))
        dk_acc[hp, pl.ds(k0, w), :] = dk_new
        dv_acc[hp, pl.ds(k0, w), :] = dv_new
        ctx_ref[...] = jnp.concatenate(outs, axis=0).T.astype(jnp.bfloat16)
        dq = jnp.concatenate(dqs, axis=0).T * 0.125
        dq_ref[...] = lane_turn(dq, cosq_ref[...], -sinq_ref[...]).astype(jnp.bfloat16)

    for blocks in range(1, 4):
        pl.when(i - kb + 1 == blocks)(partial(body, blocks))

    @pl.when(i == pl.num_programs(0) - 1)
    def _():
        dk_ref[...] = lane_turn(dk_acc[hp], cos_ref[...], -sin_ref[...]).astype(jnp.bfloat16)
        dv_ref[...] = dv_acc[hp].astype(jnp.bfloat16)


def attention(qkv, do, starts, cosines, sines):
    width = do.shape[1]
    pairs, steps = width // 128, SEQ // QB
    kb = starts[::QB] // QB
    last = steps - 1
    qspec = pl.BlockSpec((QB, 128), lambda i, h, kb: (i, h))
    kspec = pl.BlockSpec((SEQ, 128), lambda i, h, kb: (0, pairs + h))
    vspec = pl.BlockSpec((SEQ, 128), lambda i, h, kb: (0, 2 * pairs + h))
    outk = pl.BlockSpec((SEQ, 128), lambda i, h, kb: (0, jnp.where(i == last, h, 0)))
    shape = jax.ShapeDtypeStruct((SEQ, width), jnp.bfloat16)
    ctx, dq, dk, dv = pl.pallas_call(
        attn_kernel,
        grid_spec=pltpu.PrefetchScalarGridSpec(
            num_scalar_prefetch=1, grid=(steps, pairs),
            in_specs=[pl.BlockSpec((1, QB), lambda i, h, kb: (0, i)), qspec, kspec, vspec, qspec,
                      pl.BlockSpec((QB, 128), lambda i, h, kb: (i, 0)), pl.BlockSpec((QB, 128), lambda i, h, kb: (i, 0)),
                      pl.BlockSpec((SEQ, 128), lambda i, h, kb: (0, 0)), pl.BlockSpec((SEQ, 128), lambda i, h, kb: (0, 0))],
            out_specs=[qspec, qspec, outk, outk],
            scratch_shapes=[pltpu.VMEM((pairs, SEQ, 128), jnp.float32), pltpu.VMEM((pairs, SEQ, 128), jnp.float32),
                            pltpu.VMEM((3 * QB, QB), jnp.float32)]),
        out_shape=[shape] * 4,
        compiler_params=pltpu.CompilerParams(vmem_limit_bytes=48 << 20),
        cost_estimate=pl.CostEstimate(flops=30 << 30, bytes_accessed=16 << 20, transcendentals=8 << 20),
        name="attention",
    )(kb, starts[None], qkv, qkv, qkv, do, cosines, sines, cosines, sines)
    return ctx, jnp.concatenate([dq, dk, dv], axis=1)


def lane_tables(positions):
    lanes = jnp.arange(128, dtype=jnp.int32) % HD
    exponents = (lanes // 2 * 2).astype(jnp.float32) / ROT
    angles = positions.astype(jnp.float32)[:, None] * jnp.power(10000.0, -exponents)
    turned = (lanes < ROT)[None]
    signs = jnp.where(lanes % 2 == 0, -1.0, 1.0)[None]
    return jnp.where(turned, jnp.cos(angles), 1.0), jnp.where(turned, jnp.sin(angles) * signs, 0.0)


def weight_block(ref):
    half = ref.shape[0] // 2
    rows = half * ref.shape[2]
    return jnp.concatenate(
        [ref[:half, 0].reshape(rows, 128), ref[half:, 0].reshape(rows, 128)], axis=1
    )


def qkv_kernel(x_ref, w_ref, cos_ref, sin_ref, o_ref):
    j = pl.program_id(0)
    out = mm(x_ref[...], weight_block(w_ref))

    @pl.when(j < 2)
    def _():
        cosines = jnp.concatenate([cos_ref[...]] * 2, axis=1)
        sines = jnp.concatenate([sin_ref[...]] * 2, axis=1)
        scale = jnp.where(j == 0, 0.125, 1.0)
        o_ref[...] = (lane_turn(out, cosines, sines).astype(jnp.bfloat16) * scale.astype(jnp.bfloat16))

    @pl.when(j == 2)
    def _():
        o_ref[...] = out.astype(jnp.bfloat16)


MESH_ID = pl.DeviceIdType.MESH
ZS, XS, YS, CS = 4, 2, 2, 2
G1_ROWS = 1024
G2_ROWS = 2064
SPLITS = ((0, 512), (512, 512))


def place_of(z, x, y, c):
    return (z * XS + x) * (YS * CS) + y * CS + c


def gather_kernel(x_ref, gain_ref, bias_ref, count_ref, g1_ref,
                  normed_ref, turned_ref, row_ref, g1_out, counts_ref,
                  nv, tv, send_sem, recv_sem, own_sem, a2a_send, a2a_recv, row_sem, turn_sem, count_send, count_recv):
    dp, mp = lax.axis_index("dp"), lax.axis_index("mp")
    y, c, z, x = dp // CS, dp % CS, mp // XS, mp % XS
    members, own = ZS * XS, x_ref.shape[1]

    def device(z, x, y, c):
        return (y * CS + c, z * XS + x)

    barrier = pltpu.get_barrier_semaphore()
    others = [(dp, lax.rem(mp + k, members)) for k in range(1, members)]
    others += [(lax.rem(dp + k, YS * CS), mp) for k in range(1, YS * CS)]
    for other in others:
        pl.semaphore_signal(barrier, inc=1, device_id=other, device_id_type=MESH_ID)
    pl.semaphore_wait(barrier, len(others))

    copies = []

    def send(block, slot, piece, target, local=False):
        src, out = g1_ref, g1_out
        first, rows = SPLITS[block]
        spot = place_of(*piece)
        at = out.at[spot, pl.ds(first, rows)]
        copy = pltpu.make_async_remote_copy(
            src_ref=src.at[pl.ds(first, rows)] if local else at, dst_ref=at,
            send_sem=send_sem.at[block, slot], recv_sem=recv_sem.at[block, slot],
            device_id=device(*target), device_id_type=MESH_ID)
        copy.start()
        copies.append(copy)
        return copy

    recv = {}

    def hop(block, slot, piece, target, local=False):
        recv[block, slot] = send(block, slot, piece, target, local)

    flip = {"x": (z, 1 - x, y, c), "y": (z, x, 1 - y, c), "c": (z, x, y, 1 - c)}

    def orders(block):
        return ("x", "y") if block % 2 == 0 else ("y", "x")

    def begin(block):
        me = (z, x, y, c)
        for k in range(1, ZS):
            hop(block, k - 1, me, (lax.rem(z + k, ZS), x, y, c), True)
        one, two = orders(block)
        hop(block, 3, me, flip[one], True)
        hop(block, 7, me, flip[two], True)
        hop(block, 15, me, flip["c"], True)

    counts_ref[dp] = count_ref[...]
    count_copies = []
    for k in range(1, YS * CS):
        copy = pltpu.make_async_remote_copy(
            src_ref=count_ref, dst_ref=counts_ref.at[dp], send_sem=count_send.at[k], recv_sem=count_recv.at[k],
            device_id=(lax.rem(dp + k, YS * CS), mp), device_id_type=MESH_ID)
        copy.start()
        count_copies.append(copy)

    for block in range(2):
        begin(block)
    me_spot = place_of(z, x, y, c)
    own_copies = [pltpu.make_async_copy(g1_ref, g1_out.at[me_spot], own_sem.at[0])]

    def normalise(k, carry):
        row = lax.rem(mp + k, members)
        value = x_ref[row].astype(jnp.float32)
        centred = value - jnp.mean(value, axis=-1, keepdims=True)
        inverse = lax.rsqrt(jnp.mean(centred * centred, axis=-1, keepdims=True) + EPSILON)
        nv[k] = (centred * inverse * gain_ref[...] + bias_ref[...]).astype(jnp.bfloat16)
        pltpu.make_async_copy(nv.at[k], normed_ref.at[row], row_sem.at[k]).start()
        return carry

    lax.fori_loop(0, members, normalise, 0)
    mine = pl.ds(pl.multiple_of(mp * own, own), own)
    row_copies = []
    for k in range(1, members):
        row = lax.rem(mp + k, members)
        pltpu.make_async_copy(nv.at[k], normed_ref.at[row], row_sem.at[k]).wait()
        copy = pltpu.make_async_remote_copy(
            src_ref=normed_ref.at[row], dst_ref=row_ref.at[mine], send_sem=a2a_send.at[k], recv_sem=a2a_recv.at[k],
            device_id=(dp, row), device_id_type=MESH_ID)
        copy.start()
        row_copies.append(copy)
    pltpu.make_async_copy(nv.at[0], normed_ref.at[mp], row_sem.at[0]).wait()
    own_row = pltpu.make_async_copy(nv.at[0], row_ref.at[mine], row_sem.at[0])
    own_row.start()
    for copy in own_copies:
        copy.start()

    def turn(k, carry):
        row = lax.rem(mp + k, members)
        tv[:, pl.ds(pl.multiple_of(row * own, own), own)] = nv[k].T
        return carry

    lax.fori_loop(0, members, turn, 0)
    width = tv.shape[0] // (YS * CS)
    turn_copies = []
    for rel in range(YS * CS):
        yr, cr = rel % YS, rel // YS
        from_block = lax.rem(y + yr, YS) * CS + lax.rem(c + cr, CS)
        copy = pltpu.make_async_copy(
            tv.at[pl.ds(pl.multiple_of(from_block * width, width), width)], turned_ref.at[rel], turn_sem.at[rel])
        copy.start()
        turn_copies.append(copy)

    for blocks in ((0, 1),):
        for kz in range(1, ZS):
            for block in blocks:
                one, two = orders(block)
                recv[block, kz - 1].wait_recv()
                piece = (lax.rem(z + ZS - kz, ZS), x, y, c)
                hop(block, 3 + kz, piece, flip[one])
                hop(block, 7 + kz, piece, flip[two])
                hop(block, 15 + kz, piece, flip["c"])
        for kz in range(ZS):
            for block in blocks:
                one, two = orders(block)
                recv[block, 3 + kz].wait_recv()
                zz = lax.rem(z + ZS - kz, ZS)
                piece = (zz, 1 - x, y, c) if one == "x" else (zz, x, 1 - y, c)
                hop(block, 11 + kz, piece, flip[two])
                hop(block, 19 + kz, piece, flip["c"])
        for half in range(2):
            for kz in range(ZS):
                for block in blocks:
                    one, two = orders(block)
                    recv[block, 7 + half * ZS + kz].wait_recv()
                    zz = lax.rem(z + ZS - kz, ZS)
                    if half == 0:
                        piece = (zz, x, 1 - y, c) if two == "y" else (zz, 1 - x, y, c)
                    else:
                        piece = (zz, 1 - x, 1 - y, c)
                    hop(block, 23 + half * ZS + kz, piece, flip["c"])
    for block in range(2):
        for slot in range(15, 31):
            recv[block, slot].wait_recv()
    for copy in copies:
        copy.wait_send()
    for copy in own_copies + turn_copies:
        copy.wait()
    own_row.wait()
    for copy in row_copies + count_copies:
        copy.wait()


def gather_all(inputs, ln_gain, ln_bias, counts, g1):
    rows, own, width = inputs.shape
    places = ZS * XS * YS * CS
    any_space = pl.BlockSpec(memory_space=pl.ANY)
    vmem = pl.BlockSpec(memory_space=pltpu.VMEM)
    shape = jax.ShapeDtypeStruct
    half = jnp.bfloat16
    dma = pltpu.SemaphoreType.DMA
    return pl.pallas_call(
        gather_kernel,
        in_specs=[vmem, vmem, vmem, vmem, any_space],
        out_specs=[any_space] * 4 + [vmem],
        out_shape=[
            shape((rows, own, width), half),
            shape((YS * CS, width // (YS * CS), rows * own), half),
            shape((rows * own, width), half),
            shape((places,) + g1.shape, half),
            shape((YS * CS, 8, 128), jnp.float32),
        ],
        scratch_shapes=[
            pltpu.VMEM((rows, own, width), half), pltpu.VMEM((width, rows * own), half),
            dma((2, 31)), dma((2, 31)), dma((1,)), dma((rows,)), dma((rows,)), dma((rows,)), dma((YS * CS,)),
            dma((YS * CS,)), dma((YS * CS,)),
        ],
        compiler_params=pltpu.CompilerParams(collective_id=0, has_side_effects=True, vmem_limit_bytes=40 << 20),
        name="gather_weights",
    )(inputs, ln_gain[None], ln_bias[None], counts, g1)


PLACES = ZS * XS * YS * CS
PIECE = 256


def relative(dp, rel):
    return lax.rem(dp // CS + rel % YS, YS) * CS + lax.rem(dp % CS + rel // YS, CS)


def wide(ref, at, first, rows, count):
    return jnp.concatenate(
        [ref[at + (slice(first + b * rows, first + (b + 1) * rows),)] for b in range(count)], axis=-1
    )


def cotangent_kernel(place_ref, grad_ref, row_ref, weight_ref, piece_ref, branch_ref, turned_ref, row_turned_ref, ctx_ref,
                     w_ref, sum_ref):
    branch = (grad_ref[...].astype(jnp.float32) * weight_ref[...]).astype(jnp.bfloat16)
    branch_ref[...] = branch
    sum_ref[...] = jnp.sum(branch.astype(jnp.float32), axis=0, keepdims=True)
    for b in range(D // 128):
        w_ref[:, b * 128:(b + 1) * 128] = piece_ref[:, 0, b * 32:(b + 1) * 32, :].reshape(D, 128)
    branch_row = (row_ref[...].astype(jnp.float32) * weight_ref[...]).astype(jnp.bfloat16)
    ctx_ref[...] = mm(branch_row, w_ref[...], NT).astype(jnp.bfloat16)
    for rel in range(YS * CS):
        block = pl.ds(pl.multiple_of(relative(place_ref[0], rel) * PIECE, PIECE), PIECE)
        turned_ref[rel] = branch_ref[:, block].T
        row_turned_ref[rel] = (row_ref[:, block].astype(jnp.float32) * weight_ref[...]).astype(jnp.bfloat16).T


def cotangent(place, out_grad, grad_row, weight, g1):
    tokens = out_grad.shape[0]
    half = jnp.bfloat16
    shape = jax.ShapeDtypeStruct
    whole = lambda *dims: pl.BlockSpec(dims, lambda i, p: (0,) * len(dims), pipeline_mode=pl.Buffered(1))
    return pl.pallas_call(
        cotangent_kernel,
        grid_spec=pltpu.PrefetchScalarGridSpec(
            num_scalar_prefetch=1, grid=(1,),
            in_specs=[whole(tokens, D), whole(tokens, D), whole(1, 1),
                      pl.BlockSpec((PLACES, 1, 256, 128), lambda i, p: (0, 3, 0, 0))],
            out_specs=[whole(tokens, D), whole(4, PIECE, tokens), whole(4, PIECE, tokens), whole(tokens, D), whole(D, D),
                       whole(1, D)]),
        out_shape=[shape((tokens, D), half), shape((4, PIECE, tokens), half), shape((4, PIECE, tokens), half),
                   shape((tokens, D), half), shape((D, D), half), shape((1, D), jnp.float32)],
        compiler_params=pltpu.CompilerParams(vmem_limit_bytes=48 << 20),
        cost_estimate=pl.CostEstimate(flops=2 << 30, bytes_accessed=18 << 20, transcendentals=0),
        name="cotangent",
    )(place, out_grad, grad_row, weight, g1.reshape(PLACES, 4, 256, 128))


def project(rows, g1, cosines, sines):
    return pl.pallas_call(
        qkv_kernel,
        grid=(3, ZS),
        in_specs=[
            pl.BlockSpec((SEQ, D), lambda j, c: (0, 0)),
            pl.BlockSpec((8, 1, 256, 128), lambda j, c: (c, j, 0, 0)),
            pl.BlockSpec((SEQ, 128), lambda j, c: (0, 0)),
            pl.BlockSpec((SEQ, 128), lambda j, c: (0, 0)),
        ],
        out_specs=pl.BlockSpec((SEQ, 256), lambda j, c: (0, j * ZS + c)),
        out_shape=jax.ShapeDtypeStruct((SEQ, 3 * D), jnp.bfloat16),
        compiler_params=pltpu.CompilerParams(vmem_limit_bytes=40 << 20),
        cost_estimate=pl.CostEstimate(flops=6 << 30, bytes_accessed=14 << 20, transcendentals=0),
        name="qkv",
    )(rows, g1.reshape(PLACES, 4, 256, 128), cosines, sines)


def put_tiles(values, keep_ref, send_ref):
    for xr in range(XS):
        for yr in range(YS):
            keep_ref[yr, xr, 0] = values[xr][yr * PIECE:(yr + 1) * PIECE]
            send_ref[yr, xr, 0] = values[xr][(YS + yr) * PIECE:(YS + yr + 1) * PIECE]


def tile_specs(n, index):
    spec = pl.BlockSpec((YS, XS, 1, PIECE, n), index)
    return [spec, spec]


def tile_shapes(n):
    shape = jax.ShapeDtypeStruct((YS, XS, ZS, PIECE, n), jnp.bfloat16)
    return [shape, shape]


def by_x(x, value):
    low, high = value[:, :128], value[:, 128:]
    first = jnp.where(x == 0, low, high)
    return [first, jnp.where(x == 0, high, low)]


def back_kernel(place_ref, x_ref, w_ref, d_ref, n_ref, keep_ref, send_ref, xt_ref, acc_ref):
    step = pl.program_id(0) * pl.num_programs(1) + pl.program_id(1)

    @pl.when(step == 0)
    def _():
        for rel in range(YS * CS):
            block = relative(place_ref[0], rel)
            xt_ref[rel * PIECE:(rel + 1) * PIECE] = x_ref[:, pl.ds(pl.multiple_of(block * PIECE, PIECE), PIECE)].T
        acc_ref[...] = jnp.zeros_like(acc_ref)

    d = d_ref[...]
    acc_ref[...] += mm(d, weight_block(w_ref), NT)
    put_tiles(by_x(place_ref[1] % XS, mm(xt_ref[...], d).astype(jnp.bfloat16)), keep_ref, send_ref)

    @pl.when(step == pl.num_programs(0) * pl.num_programs(1) - 1)
    def _():
        n_ref[...] = acc_ref[...].astype(jnp.bfloat16)


def z_of(place, k):
    return lax.rem(place[1] // XS + k, ZS)


def back(place, rows, g1, grads):
    return pl.pallas_call(
        back_kernel,
        grid_spec=pltpu.PrefetchScalarGridSpec(
            num_scalar_prefetch=1, grid=(ZS, 3),
            in_specs=[
                pl.BlockSpec((SEQ, D), lambda k, j, p: (0, 0)),
                pl.BlockSpec((8, 1, 256, 128), lambda k, j, p: (z_of(p, k), j, 0, 0)),
                pl.BlockSpec((SEQ, 256), lambda k, j, p: (0, j * ZS + z_of(p, k))),
            ],
            out_specs=[pl.BlockSpec((SEQ, D), lambda k, j, p: (0, 0))]
            + tile_specs(128, lambda k, j, p: (0, 0, k, 0, j)),
            scratch_shapes=[pltpu.VMEM((D, SEQ), jnp.bfloat16), pltpu.VMEM((SEQ, D), jnp.float32)]),
        out_shape=[jax.ShapeDtypeStruct((SEQ, D), jnp.bfloat16)] + tile_shapes(384),
        compiler_params=pltpu.CompilerParams(vmem_limit_bytes=48 << 20),
        cost_estimate=pl.CostEstimate(flops=12 << 30, bytes_accessed=22 << 20, transcendentals=0),
        name="attention_back",
    )(place, rows, g1.reshape(PLACES, 4, 256, 128), grads)


C0 = math.sqrt(2.0 / math.pi)


def mlp_kernel(first, place_ref, x_ref, xt_ref, g_ref, gt_ref, wa_ref, wb_ref, *refs):
    if first:
        out_ref, dn_ref, keep_ref, send_ref, bsum_ref, out_acc, dn_acc = refs
    else:
        out_in, dn_in, out_ref, dn_ref, keep_ref, send_ref, bsum_ref, out_acc, dn_acc = refs
    step = pl.program_id(0)

    @pl.when(step == 0)
    def _():
        out_acc[...] = jnp.zeros_like(out_acc) if first else out_in[...]
        dn_acc[...] = jnp.zeros_like(dn_acc) if first else dn_in[...]

    w_in = jnp.concatenate([wide(r, (0, p, 0), 0, 128, 8) for r in (wa_ref, wb_ref) for p in range(CS)], axis=0)
    w_out = jnp.concatenate([wide(r, (0, p, 0), 1024, 128, 8) for r in (wa_ref, wb_ref) for p in range(CS)], axis=0)
    bias = jnp.concatenate([r[0, p, 0, 2048:2049] for r in (wa_ref, wb_ref) for p in range(CS)], axis=1)
    x = mm(x_ref[...], w_in, NT) + bias.astype(jnp.float32)
    squared = x * x
    tanh = jnp.tanh(C0 * x * (1.0 + 0.044715 * squared))
    half = 0.5 * (1.0 + tanh)
    act = (x * half).astype(jnp.bfloat16)
    slope = half + 0.5 * x * (1.0 - tanh * tanh) * (C0 * (1.0 + 3 * 0.044715 * squared))
    hid = (mm(g_ref[...], w_out, NT) * slope).astype(jnp.bfloat16)
    out_acc[...] += mm(act, w_out)
    dn_acc[...] += mm(hid, w_in)
    bsum_ref[0] = jnp.sum(hid.astype(jnp.float32), axis=0, keepdims=True)
    out_part = mm(gt_ref[...], act).astype(jnp.bfloat16)
    in_part = mm(xt_ref[...], hid).astype(jnp.bfloat16)
    put_tiles(
        [jnp.concatenate([out_part[:, a * 256:(a + 1) * 256], in_part[:, a * 256:(a + 1) * 256]], axis=1)
         for a in range(XS)], keep_ref, send_ref)

    @pl.when(step == pl.num_programs(0) - 1)
    def _():
        out_ref[...] = out_acc[...]
        dn_ref[...] = dn_acc[...]


def mlp_half(h, place, normed, normed_turned, branch, branch_turned, g2, sums):
    tokens = normed.shape[0]
    one = lambda *dims: pl.BlockSpec(dims, lambda k, p: (0,) * len(dims), pipeline_mode=pl.Buffered(1))
    weight = lambda xr: pl.BlockSpec(
        (1, CS, 1, G2_ROWS, 128),
        lambda k, p: (h, 0, z_of(p, k) * XS + lax.rem(p[1] % XS + xr, XS), 0, 0))
    views = g2.reshape(YS, CS, ZS * XS, G2_ROWS, 128)
    full = jax.ShapeDtypeStruct((tokens, D), jnp.float32)
    return pl.pallas_call(
        partial(mlp_kernel, not sums),
        grid_spec=pltpu.PrefetchScalarGridSpec(
            num_scalar_prefetch=1, grid=(ZS,),
            in_specs=[one(tokens, D), one(D, tokens), one(tokens, D), one(D, tokens), weight(0), weight(1)]
            + [one(tokens, D)] * len(sums),
            out_specs=[one(tokens, D), one(tokens, D)] + tile_specs(512, lambda k, p: (0, 0, k, 0, 0))
            + [pl.BlockSpec((1, 1, 512), lambda k, p: (k, 0, 0))],
            scratch_shapes=[pltpu.VMEM((tokens, D), jnp.float32), pltpu.VMEM((tokens, D), jnp.float32)]),
        out_shape=[full, full] + tile_shapes(512) + [jax.ShapeDtypeStruct((ZS, 1, 512), jnp.float32)],
        compiler_params=pltpu.CompilerParams(vmem_limit_bytes=62 << 20),
        cost_estimate=pl.CostEstimate(flops=26 << 30, bytes_accessed=30 << 20, transcendentals=2 << 20),
        name="mlp",
    )(place, normed, normed_turned.reshape(D, tokens), branch, branch_turned.reshape(D, tokens), views, views, *sums)


def output_kernel(place_ref, ctx_ref, w_ref, gt_ref, out_ref, keep_ref, send_ref, acc_ref):
    step = pl.program_id(0)
    ctx = ctx_ref[...]

    @pl.when(step == 0)
    def _():
        acc_ref[...] = jnp.zeros_like(acc_ref)

    acc_ref[...] += mm(ctx, w_ref[...])
    put_tiles(by_x(place_ref[1] % XS, mm(gt_ref[...], ctx).astype(jnp.bfloat16)), keep_ref, send_ref)

    @pl.when(step == pl.num_programs(0) - 1)
    def _():
        out_ref[...] = acc_ref[...].astype(jnp.bfloat16)


def row_output(place, context, w_output, branch_turned):
    tokens = context.shape[0]
    whole = lambda *dims: pl.BlockSpec(dims, lambda k, p: (0,) * len(dims), pipeline_mode=pl.Buffered(1))
    return pl.pallas_call(
        output_kernel,
        grid_spec=pltpu.PrefetchScalarGridSpec(
            num_scalar_prefetch=1, grid=(ZS,),
            in_specs=[
                pl.BlockSpec((tokens, 256), lambda k, p: (0, z_of(p, k))),
                pl.BlockSpec((256, D), lambda k, p: (z_of(p, k), 0)),
                whole(D, tokens),
            ],
            out_specs=[whole(tokens, D)] + tile_specs(128, lambda k, p: (0, 0, k, 0, 0)),
            scratch_shapes=[pltpu.VMEM((tokens, D), jnp.float32)]),
        out_shape=[jax.ShapeDtypeStruct((tokens, D), jnp.bfloat16)] + tile_shapes(128),
        compiler_params=pltpu.CompilerParams(vmem_limit_bytes=48 << 20),
        cost_estimate=pl.CostEstimate(flops=4 << 30, bytes_accessed=12 << 20, transcendentals=0),
        name="row_output",
    )(place, context, w_output, branch_turned.reshape(D, tokens))


def norm_back_kernel(x_ref, g_ref, a_ref, m_ref, ao_ref, mo_ref, gain_ref, bo_ref, weight_ref, out_ref, layer_ref, sums_ref):
    x = x_ref[...].astype(jnp.float32)
    layer = x + bo_ref[...].astype(jnp.float32) + ao_ref[...].astype(jnp.float32) + mo_ref[...]
    layer_ref[...] = layer.astype(jnp.bfloat16)
    centred = x - jnp.mean(x, axis=-1, keepdims=True)
    inverse = lax.rsqrt(jnp.mean(centred * centred, axis=-1, keepdims=True) + EPSILON)
    standard = centred * inverse
    grad = a_ref[...].astype(jnp.float32) + m_ref[...]
    scaled = grad * gain_ref[...]
    part = inverse * (
        scaled
        - jnp.mean(scaled, axis=-1, keepdims=True)
        - standard * jnp.mean(scaled * standard, axis=-1, keepdims=True)
    )
    out_ref[...] = (g_ref[...].astype(jnp.float32) * weight_ref[...] + part).astype(jnp.bfloat16)
    sums = jnp.concatenate(
        [jnp.sum(grad * standard, axis=0, keepdims=True), jnp.sum(grad, axis=0, keepdims=True)], axis=0)

    @pl.when(pl.program_id(0) == 0)
    def _():
        sums_ref[...] = sums

    @pl.when(pl.program_id(0) > 0)
    def _():
        sums_ref[...] += sums


def norm_back(inputs, out_grad, attn_grad, mlp_grad, attn_out, mlp_out, ln_gain, b_out, weight):
    tokens = inputs.shape[0]
    block = pl.BlockSpec((128, D), lambda i: (i, 0))
    row = pl.BlockSpec((1, D), lambda i: (0, 0))
    shape = jax.ShapeDtypeStruct((tokens, D), jnp.bfloat16)
    return pl.pallas_call(
        norm_back_kernel,
        grid=(tokens // 128,),
        in_specs=[block] * 6 + [row, row, pl.BlockSpec((1, 1), lambda i: (0, 0))],
        out_specs=[block, block, pl.BlockSpec((2, D), lambda i: (0, 0))],
        out_shape=[shape, shape, jax.ShapeDtypeStruct((2, D), jnp.float32)],
        cost_estimate=pl.CostEstimate(flops=20 << 20, bytes_accessed=20 << 20, transcendentals=0),
        name="norm_back",
    )(inputs, out_grad, attn_grad, mlp_grad, attn_out, mlp_out, ln_gain[None], b_out[None], weight)


HALF_PIECE = PIECE // 2
Z_ORDER = (2, 1, 3, 0)
BAND = 16


def reduce_kernel(*refs):
    sets = len(SET_WIDTHS)
    keeps, sends, small_ref = refs[:sets], refs[sets:2 * sets], refs[2 * sets]
    out_ref, small_out = refs[2 * sets + 1:2 * sets + 3]
    (own, got, first, second, last, small_got, small_own, own_sem, core_send, core_recv, first_send, first_recv,
     second_send, second_recv, last_send, last_recv, small_send, small_recv, small_sem) = refs[2 * sets + 3:]
    dp, mp = lax.axis_index("dp"), lax.axis_index("mp")
    y, c, z, x = dp // CS, dp % CS, mp // XS, mp % XS

    def device(z, x, y, c):
        return (y * CS + c, z * XS + x)

    groups, members = YS * CS, ZS * XS
    everyone = [(lax.rem(dp + a, groups), lax.rem(mp + b, members))
                for a in range(groups) for b in range(members) if (a, b) != (0, 0)]
    starts = [sum(SET_WIDTHS[:i]) for i in range(sets)]

    def mine(s, k):
        return pltpu.make_async_copy(
            keeps[s].at[:, :, k], own.at[k, :, :, :, pl.ds(starts[s], SET_WIDTHS[s])], own_sem.at[s, k])

    for k in Z_ORDER:
        for s in range(sets):
            mine(s, k).start()
    barrier = pltpu.get_barrier_semaphore()
    for other in everyone:
        pl.semaphore_signal(barrier, inc=1, device_id=other, device_id_type=MESH_ID)
    pl.semaphore_wait(barrier, len(everyone))

    def core(s, k):
        return pltpu.make_async_remote_copy(
            src_ref=sends[s].at[:, :, k], dst_ref=got.at[k, :, :, :, pl.ds(starts[s], SET_WIDTHS[s])],
            send_sem=core_send.at[s, k], recv_sem=core_recv.at[s, k],
            device_id=device(z, x, y, 1 - c), device_id_type=MESH_ID)

    for k in Z_ORDER:
        for s in range(sets):
            core(s, k).start()

    spot = dp * members + mp
    small_local = pltpu.make_async_copy(small_ref.at[spot], small_got.at[0], small_sem.at[0])
    small_local.start()
    small_copies = []
    for i, (a, b) in enumerate(everyone):
        copy = pltpu.make_async_remote_copy(
            src_ref=small_ref.at[a * members + b], dst_ref=small_got.at[i + 1], send_sem=small_send.at[i],
            recv_sem=small_recv.at[i], device_id=(a, b), device_id_type=MESH_ID)
        copy.start()
        small_copies.append(copy)

    def at(half, away, other):
        return (other, away) if half == 0 else (away, other)

    def rows(half):
        return half * HALF_PIECE

    def bands(body):
        lax.fori_loop(0, HALF_PIECE // BAND, lambda i, carry: (body(pl.multiple_of(i * BAND, BAND)), carry)[1], 0)

    def total(k, half, away, other, r, *extra):
        yy, xx = at(half, away, other)
        upper = pl.ds(rows(half) + r, BAND)
        value = own[k, yy, xx, upper].astype(jnp.float32) + got[k, yy, xx, upper].astype(jnp.float32)
        for ref in extra:
            value = value + ref[pl.ds(r, BAND)].astype(jnp.float32)
        return value

    def store(k, half, away, other, *extra):
        yy, xx = at(half, away, other)

        def body(r):
            own[k, yy, xx, pl.ds(rows(half) + r, BAND)] = total(k, half, away, other, r, *extra).astype(jnp.bfloat16)

        bands(body)
        return own.at[k, yy, xx, pl.ds(rows(half), HALF_PIECE)]

    axes = (device(z, 1 - x, y, c), device(z, x, 1 - y, c))

    def one(k, half, other):
        yy, xx = at(half, 1, other)
        return pltpu.make_async_remote_copy(
            src_ref=own.at[k, yy, xx, pl.ds(rows(half), HALF_PIECE)], dst_ref=first.at[k, half, other],
            send_sem=first_send.at[k, half, other], recv_sem=first_recv.at[k, half, other],
            device_id=axes[half], device_id_type=MESH_ID)

    def two(k, half):
        yy, xx = at(half, 0, 1)
        return pltpu.make_async_remote_copy(
            src_ref=own.at[k, yy, xx, pl.ds(rows(half), HALF_PIECE)], dst_ref=second.at[k, half],
            send_sem=second_send.at[k, half], recv_sem=second_recv.at[k, half],
            device_id=axes[1 - half], device_id_type=MESH_ID)

    def three(k, half):
        return pltpu.make_async_remote_copy(
            src_ref=own.at[k, 0, 0, pl.ds(rows(half), HALF_PIECE)], dst_ref=last.at[k, half],
            send_sem=last_send.at[k, half], recv_sem=last_recv.at[k, half],
            device_id=device(lax.rem(z + k, ZS), x, y, c), device_id_type=MESH_ID)

    def stage_one(k):
        for s in range(sets):
            mine(s, k).wait()
            core(s, k).wait_recv()
        for other in (1, 0):
            for half in range(2):
                store(k, half, 1, other)
                one(k, half, other).start()

    def stage_two(k):
        for half in range(2):
            one(k, half, 1).wait_recv()
            store(k, half, 0, 1, first.at[k, half, 1])
            two(k, half).start()

    def stage_three(k):
        for half in range(2):
            one(k, half, 0).wait_recv()
            two(k, half).wait_recv()
            if k:
                store(k, half, 0, 0, first.at[k, half, 0], second.at[k, half])
                three(k, half).start()

    order = Z_ORDER
    stage_one(order[0])
    stage_one(order[1])
    stage_two(order[0])
    stage_one(order[2])
    stage_three(order[0])
    stage_two(order[1])
    stage_one(order[3])
    stage_three(order[1])
    stage_two(order[2])
    stage_three(order[2])
    stage_two(order[3])
    small_local.wait()
    for copy in small_copies:
        copy.wait_recv()
    summed = small_got[0]
    for i in range(1, PLACES):
        summed = summed + small_got[i]
    small_out[...] = summed
    stage_three(0)
    for half in range(2):
        for k in range(1, ZS):
            three(k, half).wait_recv()

        def body(r):
            value = total(0, half, 0, 0, r, first.at[0, half, 0], second.at[0, half])
            for k in range(1, ZS):
                value = value + last[k, half, pl.ds(r, BAND)].astype(jnp.float32)
            out_ref[pl.ds(rows(half) + r, BAND)] = value

        bands(body)
    for k in range(ZS):
        for s in range(sets):
            core(s, k).wait_send()
        for half in range(2):
            for other in range(2):
                one(k, half, other).wait_send()
            two(k, half).wait_send()
            if k:
                three(k, half).wait_send()
    for copy in small_copies:
        copy.wait_send()


SET_WIDTHS = (384, 128, 512, 512)


def reduce_tiles(keeps, sends, small):
    width, sets = sum(SET_WIDTHS), len(SET_WIDTHS)
    any_space, vmem = pl.BlockSpec(memory_space=pl.ANY), pl.BlockSpec(memory_space=pltpu.VMEM)
    half = jnp.bfloat16
    dma = pltpu.SemaphoreType.DMA
    return pl.pallas_call(
        reduce_kernel,
        in_specs=[any_space] * (2 * sets + 1),
        out_specs=[vmem, vmem],
        out_shape=[jax.ShapeDtypeStruct((PIECE, width), jnp.float32), jax.ShapeDtypeStruct((8, 128), jnp.float32)],
        scratch_shapes=[
            pltpu.VMEM((ZS, YS, XS, PIECE, width), half), pltpu.VMEM((ZS, YS, XS, PIECE, width), half),
            pltpu.VMEM((ZS, 2, 2, HALF_PIECE, width), half), pltpu.VMEM((ZS, 2, HALF_PIECE, width), half),
            pltpu.VMEM((ZS, 2, HALF_PIECE, width), half), pltpu.VMEM((PLACES, 8, 128), jnp.float32),
            pltpu.VMEM((8, 128), jnp.float32),
            dma((sets, ZS)), dma((sets, ZS)), dma((sets, ZS)), dma((ZS, 2, 2)), dma((ZS, 2, 2)),
            dma((ZS, 2)), dma((ZS, 2)), dma((ZS, 2)), dma((ZS, 2)), dma((PLACES,)), dma((PLACES,)), dma((1,)),
        ],
        compiler_params=pltpu.CompilerParams(collective_id=1, has_side_effects=True, vmem_limit_bytes=56 << 20),
        name="reduce_tiles",
    )(*keeps, *sends, small)


def on_device_rows(
    inputs,
    seg_lengths,
    group_counts,
    out_grad,
    ln_gain,
    ln_bias,
    w_query,
    w_key,
    w_value,
    w_output,
    w_in,
    b_in,
    w_out,
    b_out,
):
    row_count, own_tokens = inputs.shape[0], inputs.shape[1]
    tokens = row_count * own_tokens
    group, member = lax.axis_index("dp"), lax.axis_index("mp")
    place = jnp.stack([group, member]).astype(jnp.int32)

    def quarter(matrix, axis):
        size = matrix.shape[axis] // (YS * CS)
        return lax.dynamic_slice_in_dim(matrix, group * size, size, axis)

    def narrow(matrix):
        return matrix.reshape(matrix.shape[0], D // 128, 128).transpose(1, 0, 2).reshape(-1, 128)

    def exchange(tensor):
        blocks = tensor.reshape(row_count, own_tokens, D)
        return lax.all_to_all(blocks, "mp", 0, 0, tiled=True).reshape(tokens, D)

    counts = jnp.broadcast_to(group_counts.astype(jnp.float32)[:, None], (8, 128))
    g1 = jnp.concatenate(
        [quarter(w_query, 0), quarter(w_key, 0), quarter(w_value, 0), narrow(quarter(w_output, 0))], axis=0)
    bias_rows = jnp.pad(quarter(b_in, 0)[None], ((0, G2_ROWS - 2049), (0, 0)))
    g2 = jnp.concatenate([narrow(quarter(w_in, 0)), narrow(quarter(w_out, 0)), bias_rows], axis=0)
    grad_row = exchange(out_grad)
    normed, normed_turned, normed_row, g1_all, counts_all = gather_all(inputs, ln_gain, ln_bias, counts, g1)
    g2, normed_row = lax.optimization_barrier((g2, normed_row))
    g2_all = lax.all_gather(g2, ("dp", "mp"))
    normed = normed.reshape(tokens, D)
    weight = (YS * CS * counts_all[group, 0, 0] / jnp.sum(counts_all[:, 0, 0])).reshape(1, 1)

    flat_grad = out_grad.reshape(tokens, D)
    branch, branch_turned, row_turned, ctx_grad_row, w_output_all, out_sum = cotangent(
        place, flat_grad, grad_row, weight, g1_all)
    own_row = lax.dynamic_index_in_dim(seg_lengths, member, 0, keepdims=True)
    _, positions = segment_layout(own_row)
    positions = positions[0]
    cosines, sines = lane_tables(positions)
    starts = jnp.arange(SEQ, dtype=jnp.int32) - positions
    qkv = project(normed_row, g1_all, cosines, sines)
    context_row, qkv_grad = attention(qkv, ctx_grad_row, starts, cosines, sines)
    out_row, keep_o, send_o = row_output(place, context_row, w_output_all, row_turned)
    attn_out = exchange(out_row)
    normed_row_grad, keep_a, send_a = back(place, normed_row, g1_all, qkv_grad)
    attn_grad = exchange(normed_row_grad)
    normed, keep_a = lax.optimization_barrier((normed, keep_a))
    mlp_out, mlp_grad, keep0, send0, bsum0 = mlp_half(
        0, place, normed, normed_turned, branch, branch_turned, g2_all, ())
    mlp_out, mlp_grad, keep1, send1, bsum1 = mlp_half(
        1, place, normed, normed_turned, branch, branch_turned, g2_all, (mlp_out, mlp_grad))
    input_grad, layer_out, sums = norm_back(
        inputs.reshape(tokens, D), flat_grad, attn_grad, mlp_grad, attn_out, mlp_out, ln_gain, b_out, weight)

    bsums = jnp.stack([bsum0, bsum1]).reshape(YS, ZS * XS, CS, 128)
    targets = jnp.arange(ZS * XS)
    spots = (targets // XS - member // XS) % ZS * XS + (targets % XS - member % XS) % XS
    bsums = jnp.take(bsums, spots, axis=1).transpose(1, 0, 2, 3).reshape(ZS * XS, 4, 128)
    own = D // PLACES
    vectors = jnp.concatenate([sums, out_sum], axis=0).reshape(3, PLACES, own).transpose(1, 0, 2)
    vectors = jnp.pad(vectors, ((0, 0), (0, 1), (0, 128 - own)))
    small = jnp.concatenate([jnp.tile(bsums, (YS * CS, 1, 1)), vectors], axis=1)
    grads, small = reduce_tiles((keep_a, keep_o, keep0, keep1), (send_a, send_o, send0, send1), small)
    shape = (row_count, own_tokens, D)
    return (
        layer_out.reshape(shape),
        input_grad.reshape(shape),
        small[4, :own],
        small[5, :own],
        grads[:, :128],
        grads[:, 128:256],
        grads[:, 256:384],
        grads[:, 384:512].T,
        jnp.concatenate([grads[:, 768:1024], grads[:, 1280:]], axis=1).T,
        small[:4].reshape(512),
        jnp.concatenate([grads[:, 512:768], grads[:, 1024:1280]], axis=1).T,
        small[6, :own],
    )


def solution(mesh):
    placed = (
        P("dp", "mp", None),
        P("dp", None),
        P("dp"),
        P("dp", "mp", None),
        P(),
        P(),
        P(None, "mp"),
        P(None, "mp"),
        P(None, "mp"),
        P("mp", None),
        P("mp", None),
        P("mp"),
        P("mp", None),
        P(),
    )
    sizes = (mesh.shape["dp"], mesh.shape["mp"])

    def on_device(*args):
        if sizes == (YS * CS, ZS * XS) and args[0].shape[0] == ZS * XS:
            return on_device_rows(*args)
        return on_device_gathered(*args)

    return jax.shard_map(
        on_device,
        mesh=mesh,
        in_specs=placed,
        out_specs=(
            P("dp", "mp", None),
            P("dp", "mp", None),
            P(("dp", "mp")),
            P(("dp", "mp")),
            P("dp", "mp"),
            P("dp", "mp"),
            P("dp", "mp"),
            P("mp", "dp"),
            P("mp", "dp"),
            P("mp"),
            P("mp", "dp"),
            P(("dp", "mp")),
        ),
        check_vma=False,
    )
```

```python
from functools import partial
import math
import jax
import jax.numpy as jnp
from jax import lax
from jax.sharding import PartitionSpec as P
from jax.experimental import pallas as pl
from jax.experimental.pallas import tpu as pltpu


D = 1024
HD = 64
ROT = 32
SEQ = 1024


EPSILON = 1e-05


def segment_layout(seg_lengths):
    seg_ends = jnp.cumsum(seg_lengths, axis=-1)
    seg_starts = seg_ends - seg_lengths
    places = jnp.arange(SEQ, dtype=jnp.int32)
    passed = places[None, :, None] >= seg_ends[:, None, :]
    seg_ids = jnp.sum(passed.astype(jnp.int32), axis=-1)
    inside = (places[None, :, None] >= seg_starts[:, None, :]) & jnp.logical_not(passed)
    begins = jnp.sum(jnp.where(inside, seg_starts[:, None, :], 0), axis=-1)
    return (seg_ids, places[None, :] - begins)


def rotary_tables(positions):
    exponents = jnp.arange(0, ROT, 2, dtype=jnp.float32) / ROT
    freqs = jnp.power(10000.0, -exponents)
    angles = positions.astype(jnp.float32)[..., None] * freqs
    return (jnp.cos(angles)[..., None, :], jnp.sin(angles)[..., None, :])


def turn_pairs(tensor, cosines, sines):
    rotary = tensor[..., :ROT]
    passive = tensor[..., ROT:]
    paired = rotary.reshape(rotary.shape[:-1] + (ROT // 2, 2))
    evens = paired[..., 0]
    odd_part = paired[..., 1]
    turned = jnp.stack(
        [evens * cosines - odd_part * sines, evens * sines + odd_part * cosines], axis=-1
    )
    return jnp.concatenate([turned.reshape(rotary.shape), passive], axis=-1)


def norm_rows(inputs, ln_gain, ln_bias):
    values_in = inputs.astype(jnp.float32)
    centred = values_in - jnp.mean(values_in, axis=-1, keepdims=True)
    inverse = lax.rsqrt(jnp.mean(centred * centred, axis=-1, keepdims=True) + EPSILON)
    standard = centred * inverse
    return (standard, inverse, (standard * ln_gain + ln_bias).astype(jnp.bfloat16))


def masked_scores(queries, keys_rot, seg_ids):
    places = jnp.arange(SEQ, dtype=jnp.int32)
    allowed = (seg_ids[:, None] == seg_ids[None, :]) & (places[:, None] >= places[None, :])
    scores = jnp.einsum("qhd,khd->hqk", queries, keys_rot, preferred_element_type=jnp.float32) * (
        1.0 / math.sqrt(HD)
    )
    return jnp.where(allowed[None], scores, -1e30)


def attend_forward(operands):
    queries, keys_rot, values, seg_ids = operands
    scores = masked_scores(queries, keys_rot, seg_ids)
    row_peak = jnp.max(scores, axis=-1, keepdims=True)
    lifted = jnp.exp(scores - row_peak)
    row_mass = jnp.sum(lifted, axis=-1, keepdims=True)
    probs = (lifted / row_mass).astype(jnp.bfloat16)
    context = jnp.einsum("hqk,khd->qhd", probs, values, preferred_element_type=jnp.float32)
    return (context.astype(jnp.bfloat16), (row_peak + jnp.log(row_mass))[..., 0])


def attend_backward(operands):
    queries, keys_rot, values, seg_ids, log_mass, ctx_grad = operands
    score_scale = 1.0 / math.sqrt(HD)
    scores = masked_scores(queries, keys_rot, seg_ids)
    probs = jnp.exp(scores - log_mass[..., None])
    rounded = probs.astype(jnp.bfloat16)
    value_grad = jnp.einsum("hqk,qhd->khd", rounded, ctx_grad, preferred_element_type=jnp.float32)
    prob_grad = jnp.einsum("qhd,khd->hqk", ctx_grad, values, preferred_element_type=jnp.float32)
    score_grad = (probs * (prob_grad - jnp.sum(probs * prob_grad, axis=-1, keepdims=True))).astype(
        jnp.bfloat16
    )
    query_grad = (
        jnp.einsum("hqk,khd->qhd", score_grad, keys_rot, preferred_element_type=jnp.float32)
        * score_scale
    )
    key_grad = (
        jnp.einsum("hqk,qhd->khd", score_grad, queries, preferred_element_type=jnp.float32)
        * score_scale
    )
    return (query_grad, key_grad, value_grad)


def project_heads(flat_rows, matrix, row_count):
    local_heads = matrix.shape[1] // HD
    return jnp.dot(flat_rows, matrix, preferred_element_type=jnp.float32).reshape(
        row_count, -1, local_heads, HD
    )


def attention_inputs(flat_rows, w_query, w_key, w_value, cosines, sines, row_count):
    queries = turn_pairs(project_heads(flat_rows, w_query, row_count), cosines, sines).astype(
        jnp.bfloat16
    )
    keys_rot = turn_pairs(project_heads(flat_rows, w_key, row_count), cosines, sines).astype(
        jnp.bfloat16
    )
    values = project_heads(flat_rows, w_value, row_count).astype(jnp.bfloat16)
    return (queries, keys_rot, values)


def mlp_inputs(flat_rows, w_in, b_in):
    hidden = jnp.dot(flat_rows, w_in.T, preferred_element_type=jnp.float32) + b_in.astype(
        jnp.float32
    )
    return (hidden, jax.nn.gelu(hidden, approximate=True).astype(jnp.bfloat16))


def gelu_grad(hidden, act_grad):
    pulled = jax.vjp(partial(jax.nn.gelu, approximate=True), hidden)[1](act_grad)[0]
    return pulled.astype(jnp.bfloat16)


def head_products(flat_rows, query_back, key_back, value_back, w_query, w_key, w_value):
    normed_part = (
        jnp.dot(query_back, w_query.T, preferred_element_type=jnp.float32)
        + jnp.dot(key_back, w_key.T, preferred_element_type=jnp.float32)
        + jnp.dot(value_back, w_value.T, preferred_element_type=jnp.float32)
    )
    w_query_part = jnp.dot(flat_rows.T, query_back, preferred_element_type=jnp.float32)
    w_key_part = jnp.dot(flat_rows.T, key_back, preferred_element_type=jnp.float32)
    w_value_part = jnp.dot(flat_rows.T, value_back, preferred_element_type=jnp.float32)
    return (normed_part, w_query_part, w_key_part, w_value_part)


def on_device_gathered(
    inputs,
    seg_lengths,
    group_counts,
    out_grad,
    ln_gain,
    ln_bias,
    w_query,
    w_key,
    w_value,
    w_output,
    w_in,
    b_in,
    w_out,
    b_out,
):
    row_count = inputs.shape[0]
    own_tokens = inputs.shape[1]
    local_width = w_query.shape[1]
    local_heads = local_width // HD
    seg_ids, positions = segment_layout(seg_lengths)
    cosines, sines = rotary_tables(positions)
    standard, inverse, normed = norm_rows(inputs, ln_gain, ln_bias)
    base_out = inputs.astype(jnp.float32) + b_out.astype(jnp.float32)
    gathered = lax.all_gather(normed, "mp", axis=1, tiled=True)
    flat_rows = gathered.reshape(row_count * SEQ, D)
    queries, keys_rot, values = attention_inputs(
        flat_rows, w_query, w_key, w_value, cosines, sines, row_count
    )
    context, log_mass = lax.map(attend_forward, (queries, keys_rot, values, seg_ids))
    ctx_flat = context.reshape(row_count * SEQ, local_width)
    hidden, activated = mlp_inputs(flat_rows, w_in, b_in)
    partial_out = jnp.dot(ctx_flat, w_output, preferred_element_type=jnp.float32) + jnp.dot(
        activated, w_out, preferred_element_type=jnp.float32
    )
    summed = lax.psum_scatter(
        partial_out.reshape(row_count, SEQ, D).astype(jnp.bfloat16),
        "mp",
        scatter_dimension=1,
        tiled=True,
    ).astype(jnp.float32)
    layer_out = (base_out + summed).astype(jnp.bfloat16)
    counts_now = group_counts.astype(jnp.float32)
    total_count = lax.psum(counts_now, "dp")
    weight_now = lax.axis_size("dp") * counts_now[0] / total_count[0]
    own_grad = out_grad.astype(jnp.float32) * weight_now
    own_rounded = own_grad.astype(jnp.bfloat16).reshape(row_count * own_tokens, D)
    cot_rows = lax.all_gather(out_grad, "mp", axis=1, tiled=True)
    branch_grad = (
        (cot_rows.astype(jnp.float32) * weight_now).astype(jnp.bfloat16).reshape(row_count * SEQ, D)
    )
    act_grad = jnp.dot(branch_grad, w_out.T, preferred_element_type=jnp.float32)
    hidden_grad = gelu_grad(hidden, act_grad)
    w_out_part = jnp.dot(activated.T, branch_grad, preferred_element_type=jnp.float32)
    w_in_part = jnp.dot(hidden_grad.T, flat_rows, preferred_element_type=jnp.float32)
    b_in_part = jnp.sum(hidden_grad.astype(jnp.float32), axis=0)
    ctx_grad = jnp.dot(branch_grad, w_output.T, preferred_element_type=jnp.float32).astype(
        jnp.bfloat16
    )
    w_output_part = jnp.dot(ctx_flat.T, branch_grad, preferred_element_type=jnp.float32)
    rot_query_grad, rot_key_grad, value_grad = lax.map(
        attend_backward,
        (
            queries,
            keys_rot,
            values,
            seg_ids,
            log_mass,
            ctx_grad.reshape(row_count, SEQ, local_heads, HD),
        ),
    )
    query_back = (
        turn_pairs(rot_query_grad, cosines, -sines)
        .astype(jnp.bfloat16)
        .reshape(row_count, SEQ, local_width)
    )
    key_back = (
        turn_pairs(rot_key_grad, cosines, -sines)
        .astype(jnp.bfloat16)
        .reshape(row_count, SEQ, local_width)
    )
    value_back = value_grad.astype(jnp.bfloat16).reshape(row_count, SEQ, local_width)
    normed_part, w_query_part, w_key_part, w_value_part = head_products(
        flat_rows,
        query_back.reshape(row_count * SEQ, local_width),
        key_back.reshape(row_count * SEQ, local_width),
        value_back.reshape(row_count * SEQ, local_width),
        w_query,
        w_key,
        w_value,
    )
    normed_part = normed_part + jnp.dot(hidden_grad, w_in, preferred_element_type=jnp.float32)
    normed_grad = lax.psum_scatter(
        normed_part.reshape(row_count, SEQ, D).astype(jnp.bfloat16),
        "mp",
        scatter_dimension=1,
        tiled=True,
    ).astype(jnp.float32)
    scaled = normed_grad * ln_gain
    input_part = inverse * (
        scaled
        - jnp.mean(scaled, axis=-1, keepdims=True)
        - standard * jnp.mean(scaled * standard, axis=-1, keepdims=True)
    )
    input_grad = (own_grad + input_part).astype(jnp.bfloat16)
    gain_part = jnp.sum(normed_grad * standard, axis=(0, 1))
    bias_part = jnp.sum(normed_grad, axis=(0, 1))
    out_bias_part = jnp.sum(own_rounded.astype(jnp.float32), axis=0)
    ln_gain_grad, ln_bias_grad, b_out_grad = (
        lax.psum_scatter(gain_part, ("dp", "mp"), scatter_dimension=0, tiled=True),
        lax.psum_scatter(bias_part, ("dp", "mp"), scatter_dimension=0, tiled=True),
        lax.psum_scatter(out_bias_part, ("dp", "mp"), scatter_dimension=0, tiled=True),
    )
    w_query_grad, w_key_grad, w_value_grad = (
        lax.psum_scatter(
            w_query_part.astype(jnp.bfloat16), "dp", scatter_dimension=0, tiled=True
        ).astype(jnp.float32),
        lax.psum_scatter(
            w_key_part.astype(jnp.bfloat16), "dp", scatter_dimension=0, tiled=True
        ).astype(jnp.float32),
        lax.psum_scatter(
            w_value_part.astype(jnp.bfloat16), "dp", scatter_dimension=0, tiled=True
        ).astype(jnp.float32),
    )
    w_output_grad, w_in_grad, w_out_grad = (
        lax.psum_scatter(
            w_output_part.astype(jnp.bfloat16), "dp", scatter_dimension=1, tiled=True
        ).astype(jnp.float32),
        lax.psum_scatter(
            w_in_part.astype(jnp.bfloat16), "dp", scatter_dimension=1, tiled=True
        ).astype(jnp.float32),
        lax.psum_scatter(
            w_out_part.astype(jnp.bfloat16), "dp", scatter_dimension=1, tiled=True
        ).astype(jnp.float32),
    )
    b_in_grad = lax.psum(b_in_part, "dp")
    return (
        layer_out,
        input_grad,
        ln_gain_grad,
        ln_bias_grad,
        w_query_grad,
        w_key_grad,
        w_value_grad,
        w_output_grad,
        w_in_grad,
        b_in_grad,
        w_out_grad,
        b_out_grad,
    )


QB = 256

NT = (((1,), (1,)), ((), ()))
NN = (((1,), (0,)), ((), ()))


def mm(a, b, dims=NN):
    return lax.dot_general(a, b, dims, preferred_element_type=jnp.float32)


def lane_turn(x, cosines, sines):
    width = x.shape[1]
    lanes = lax.broadcasted_iota(jnp.int32, x.shape, 1)
    swapped = jnp.where(lanes % 2 == 0, pltpu.roll(x, width - 1, 1), pltpu.roll(x, 1, 1))
    return x * cosines + swapped * sines


def attn_kernel(kb_ref, start_ref, q_ref, k_ref, v_ref, do_ref, cosq_ref, sinq_ref, cos_ref, sin_ref,
                ctx_ref, dq_ref, dk_ref, dv_ref, dk_acc, dv_acc, bias_ref):
    i, hp = pl.program_id(0), pl.program_id(1)
    kb = kb_ref[i]

    @pl.when(i == 0)
    def _():
        dk_acc[hp] = jnp.zeros(dk_acc.shape[1:], jnp.float32)
        dv_acc[hp] = jnp.zeros(dv_acc.shape[1:], jnp.float32)

    def body(blocks):
        w = blocks * QB
        k0 = pl.multiple_of(kb * QB, QB)

        @pl.when(hp == 0)
        def _():
            keys = lax.broadcasted_iota(jnp.int32, (w, QB), 0) + k0
            queries = lax.broadcasted_iota(jnp.int32, (w, QB), 1) + i * QB
            fine = (keys >= start_ref[...]) & (keys <= queries)
            bias_ref[:w] = jnp.where(fine, 0.0, -1e30)

        q, do = q_ref[...], do_ref[...]
        low = lax.broadcasted_iota(jnp.int32, q.shape, 1) < HD
        zero = jnp.zeros_like(q)
        k, v = k_ref[pl.ds(k0, w), :], v_ref[pl.ds(k0, w), :]
        kt, vt = k.T, v.T
        outs, dqs = [], []
        dk_new, dv_new = dk_acc[hp, pl.ds(k0, w), :], dv_acc[hp, pl.ds(k0, w), :]
        for head in range(2):
            qh = jnp.where(low, q, zero) if head == 0 else jnp.where(low, zero, q)
            doh = jnp.where(low, do, zero) if head == 0 else jnp.where(low, zero, do)
            s = mm(k, qh, NT) + bias_ref[:w]
            e = jnp.exp(s - jnp.max(s, axis=0, keepdims=True))
            p = e * (1.0 / jnp.sum(e, axis=0, keepdims=True))
            pb = p.astype(jnp.bfloat16)
            pd = p * mm(v, doh, NT)
            ds = (pd - p * jnp.sum(pd, axis=0, keepdims=True)).astype(jnp.bfloat16)
            dv_new = dv_new + mm(pb, doh)
            dk_new = dk_new + mm(ds, qh)
            outs.append(mm(vt[head * HD:(head + 1) * HD], pb))
            dqs.append(mm(kt[head * HD:(head + 1) * HD], ds))
        dk_acc[hp, pl.ds(k0, w), :] = dk_new
        dv_acc[hp, pl.ds(k0, w), :] = dv_new
        ctx_ref[...] = jnp.concatenate(outs, axis=0).T.astype(jnp.bfloat16)
        dq = jnp.concatenate(dqs, axis=0).T * 0.125
        dq_ref[...] = lane_turn(dq, cosq_ref[...], -sinq_ref[...]).astype(jnp.bfloat16)

    for blocks in range(1, 4):
        pl.when(i - kb + 1 == blocks)(partial(body, blocks))

    @pl.when(i == pl.num_programs(0) - 1)
    def _():
        dk_ref[...] = lane_turn(dk_acc[hp], cos_ref[...], -sin_ref[...]).astype(jnp.bfloat16)
        dv_ref[...] = dv_acc[hp].astype(jnp.bfloat16)


def attention(qkv, do, starts, cosines, sines):
    width = do.shape[1]
    pairs, steps = width // 128, SEQ // QB
    kb = starts[::QB] // QB
    last = steps - 1
    qspec = pl.BlockSpec((QB, 128), lambda i, h, kb: (i, h))
    kspec = pl.BlockSpec((SEQ, 128), lambda i, h, kb: (0, pairs + h))
    vspec = pl.BlockSpec((SEQ, 128), lambda i, h, kb: (0, 2 * pairs + h))
    outk = pl.BlockSpec((SEQ, 128), lambda i, h, kb: (0, jnp.where(i == last, h, 0)))
    shape = jax.ShapeDtypeStruct((SEQ, width), jnp.bfloat16)
    ctx, dq, dk, dv = pl.pallas_call(
        attn_kernel,
        grid_spec=pltpu.PrefetchScalarGridSpec(
            num_scalar_prefetch=1, grid=(steps, pairs),
            in_specs=[pl.BlockSpec((1, QB), lambda i, h, kb: (0, i)), qspec, kspec, vspec, qspec,
                      pl.BlockSpec((QB, 128), lambda i, h, kb: (i, 0)), pl.BlockSpec((QB, 128), lambda i, h, kb: (i, 0)),
                      pl.BlockSpec((SEQ, 128), lambda i, h, kb: (0, 0)), pl.BlockSpec((SEQ, 128), lambda i, h, kb: (0, 0))],
            out_specs=[qspec, qspec, outk, outk],
            scratch_shapes=[pltpu.VMEM((pairs, SEQ, 128), jnp.float32), pltpu.VMEM((pairs, SEQ, 128), jnp.float32),
                            pltpu.VMEM((3 * QB, QB), jnp.float32)]),
        out_shape=[shape] * 4,
        compiler_params=pltpu.CompilerParams(vmem_limit_bytes=48 << 20),
        cost_estimate=pl.CostEstimate(flops=30 << 30, bytes_accessed=16 << 20, transcendentals=8 << 20),
        name="attention",
    )(kb, starts[None], qkv, qkv, qkv, do, cosines, sines, cosines, sines)
    return ctx, (dq, dk, dv)


def lane_tables(positions):
    lanes = jnp.arange(128, dtype=jnp.int32) % HD
    exponents = (lanes // 2 * 2).astype(jnp.float32) / ROT
    angles = positions.astype(jnp.float32)[:, None] * jnp.power(10000.0, -exponents)
    turned = (lanes < ROT)[None]
    signs = jnp.where(lanes % 2 == 0, -1.0, 1.0)[None]
    return jnp.where(turned, jnp.cos(angles), 1.0), jnp.where(turned, jnp.sin(angles) * signs, 0.0)


def weight_block(ref):
    half = ref.shape[0] // 2
    rows = half * ref.shape[2]
    return jnp.concatenate(
        [ref[:half, 0].reshape(rows, 128), ref[half:, 0].reshape(rows, 128)], axis=1
    )


def qkv_kernel(x_ref, w_ref, cos_ref, sin_ref, o_ref):
    j = pl.program_id(0)
    out = mm(x_ref[...], weight_block(w_ref))

    @pl.when(j < 2)
    def _():
        cosines = jnp.concatenate([cos_ref[...]] * 2, axis=1)
        sines = jnp.concatenate([sin_ref[...]] * 2, axis=1)
        scale = jnp.where(j == 0, 0.125, 1.0)
        o_ref[...] = (lane_turn(out, cosines, sines).astype(jnp.bfloat16) * scale.astype(jnp.bfloat16))

    @pl.when(j == 2)
    def _():
        o_ref[...] = out.astype(jnp.bfloat16)


MESH_ID = pl.DeviceIdType.MESH
ZS, XS, YS, CS = 4, 2, 2, 2
G1_ROWS = 1024
G2_ROWS = 2064
SPLITS = ((0, 512), (512, 512))


def place_of(z, x, y, c):
    return (z * XS + x) * (YS * CS) + y * CS + c


def gather_kernel(x_ref, gain_ref, bias_ref, count_ref, g1_ref, grad_ref,
                  normed_ref, turned_ref, row_ref, grad_row, g1_out, counts_ref,
                  nv, tv, send_sem, recv_sem, own_sem, a2a_send, a2a_recv, row_sem, turn_sem, count_send, count_recv,
                  grad_send, grad_recv, grad_sem):
    dp, mp = lax.axis_index("dp"), lax.axis_index("mp")
    y, c, z, x = dp // CS, dp % CS, mp // XS, mp % XS
    members, own = ZS * XS, x_ref.shape[1]

    def device(z, x, y, c):
        return (y * CS + c, z * XS + x)

    barrier = pltpu.get_barrier_semaphore()
    others = [(dp, lax.rem(mp + k, members)) for k in range(1, members)]
    others += [(lax.rem(dp + k, YS * CS), mp) for k in range(1, YS * CS)]
    for other in others:
        pl.semaphore_signal(barrier, inc=1, device_id=other, device_id_type=MESH_ID)
    pl.semaphore_wait(barrier, len(others))

    copies = []

    def send(block, slot, piece, target, local=False):
        src, out = g1_ref, g1_out
        first, rows = SPLITS[block]
        spot = place_of(*piece)
        at = out.at[spot, pl.ds(first, rows)]
        copy = pltpu.make_async_remote_copy(
            src_ref=src.at[pl.ds(first, rows)] if local else at, dst_ref=at,
            send_sem=send_sem.at[block, slot], recv_sem=recv_sem.at[block, slot],
            device_id=device(*target), device_id_type=MESH_ID)
        copy.start()
        copies.append(copy)
        return copy

    recv = {}

    def hop(block, slot, piece, target, local=False):
        recv[block, slot] = send(block, slot, piece, target, local)

    flip = {"x": (z, 1 - x, y, c), "y": (z, x, 1 - y, c), "c": (z, x, y, 1 - c)}

    def orders(block):
        return ("x", "y") if block % 2 == 0 else ("y", "x")

    def begin(block):
        me = (z, x, y, c)
        for k in range(1, ZS):
            hop(block, k - 1, me, (lax.rem(z + k, ZS), x, y, c), True)
        one, two = orders(block)
        hop(block, 3, me, flip[one], True)
        hop(block, 7, me, flip[two], True)
        hop(block, 15, me, flip["c"], True)

    counts_ref[dp] = count_ref[...]
    count_copies = []
    for k in range(1, YS * CS):
        copy = pltpu.make_async_remote_copy(
            src_ref=count_ref, dst_ref=counts_ref.at[dp], send_sem=count_send.at[k], recv_sem=count_recv.at[k],
            device_id=(lax.rem(dp + k, YS * CS), mp), device_id_type=MESH_ID)
        copy.start()
        count_copies.append(copy)

    for block in range(2):
        begin(block)
    mine = pl.ds(pl.multiple_of(mp * own, own), own)
    grad_copies = []
    for k in range(1, members):
        row = lax.rem(mp + k, members)
        copy = pltpu.make_async_remote_copy(
            src_ref=grad_ref.at[row], dst_ref=grad_row.at[mine], send_sem=grad_send.at[k], recv_sem=grad_recv.at[k],
            device_id=(dp, row), device_id_type=MESH_ID)
        copy.start()
        grad_copies.append(copy)
    own_grad = pltpu.make_async_copy(grad_ref.at[mp], grad_row.at[mine], grad_sem.at[0])
    own_grad.start()
    me_spot = place_of(z, x, y, c)
    own_copies = [pltpu.make_async_copy(g1_ref, g1_out.at[me_spot], own_sem.at[0])]

    def normalise(k, carry):
        row = lax.rem(mp + k, members)
        value = x_ref[row].astype(jnp.float32)
        centred = value - jnp.mean(value, axis=-1, keepdims=True)
        inverse = lax.rsqrt(jnp.mean(centred * centred, axis=-1, keepdims=True) + EPSILON)
        nv[k] = (centred * inverse * gain_ref[...] + bias_ref[...]).astype(jnp.bfloat16)
        pltpu.make_async_copy(nv.at[k], normed_ref.at[row], row_sem.at[k]).start()
        return carry

    lax.fori_loop(0, members, normalise, 0)
    row_copies = []
    for k in range(1, members):
        row = lax.rem(mp + k, members)
        pltpu.make_async_copy(nv.at[k], normed_ref.at[row], row_sem.at[k]).wait()
        copy = pltpu.make_async_remote_copy(
            src_ref=normed_ref.at[row], dst_ref=row_ref.at[mine], send_sem=a2a_send.at[k], recv_sem=a2a_recv.at[k],
            device_id=(dp, row), device_id_type=MESH_ID)
        copy.start()
        row_copies.append(copy)
    pltpu.make_async_copy(nv.at[0], normed_ref.at[mp], row_sem.at[0]).wait()
    own_row = pltpu.make_async_copy(nv.at[0], row_ref.at[mine], row_sem.at[0])
    own_row.start()
    for copy in own_copies:
        copy.start()

    def turn(k, carry):
        row = lax.rem(mp + k, members)
        tv[:, pl.ds(pl.multiple_of(row * own, own), own)] = nv[k].T
        return carry

    lax.fori_loop(0, members, turn, 0)
    width = tv.shape[0] // (YS * CS)
    turn_copies = []
    for rel in range(YS * CS):
        yr, cr = rel % YS, rel // YS
        from_block = lax.rem(y + yr, YS) * CS + lax.rem(c + cr, CS)
        copy = pltpu.make_async_copy(
            tv.at[pl.ds(pl.multiple_of(from_block * width, width), width)], turned_ref.at[rel], turn_sem.at[rel])
        copy.start()
        turn_copies.append(copy)

    for blocks in ((0, 1),):
        for kz in range(1, ZS):
            for block in blocks:
                one, two = orders(block)
                recv[block, kz - 1].wait_recv()
                piece = (lax.rem(z + ZS - kz, ZS), x, y, c)
                hop(block, 3 + kz, piece, flip[one])
                hop(block, 7 + kz, piece, flip[two])
                hop(block, 15 + kz, piece, flip["c"])
        for kz in range(ZS):
            for block in blocks:
                one, two = orders(block)
                recv[block, 3 + kz].wait_recv()
                zz = lax.rem(z + ZS - kz, ZS)
                piece = (zz, 1 - x, y, c) if one == "x" else (zz, x, 1 - y, c)
                hop(block, 11 + kz, piece, flip[two])
                hop(block, 19 + kz, piece, flip["c"])
        for half in range(2):
            for kz in range(ZS):
                for block in blocks:
                    one, two = orders(block)
                    recv[block, 7 + half * ZS + kz].wait_recv()
                    zz = lax.rem(z + ZS - kz, ZS)
                    if half == 0:
                        piece = (zz, x, 1 - y, c) if two == "y" else (zz, 1 - x, y, c)
                    else:
                        piece = (zz, 1 - x, 1 - y, c)
                    hop(block, 23 + half * ZS + kz, piece, flip["c"])
    for block in range(2):
        for slot in range(15, 31):
            recv[block, slot].wait_recv()
    for copy in copies:
        copy.wait_send()
    for copy in own_copies + turn_copies:
        copy.wait()
    own_row.wait()
    own_grad.wait()
    for copy in row_copies + grad_copies + count_copies:
        copy.wait()


def gather_all(inputs, ln_gain, ln_bias, counts, g1, out_grad):
    rows, own, width = inputs.shape
    places = ZS * XS * YS * CS
    any_space = pl.BlockSpec(memory_space=pl.ANY)
    vmem = pl.BlockSpec(memory_space=pltpu.VMEM)
    shape = jax.ShapeDtypeStruct
    half = jnp.bfloat16
    dma = pltpu.SemaphoreType.DMA
    return pl.pallas_call(
        gather_kernel,
        in_specs=[vmem, vmem, vmem, vmem, any_space, any_space],
        out_specs=[any_space] * 5 + [vmem],
        out_shape=[
            shape((rows, own, width), half),
            shape((YS * CS, width // (YS * CS), rows * own), half),
            shape((rows * own, width), half),
            shape((rows * own, width), half),
            shape((places,) + g1.shape, half),
            shape((YS * CS, 8, 128), jnp.float32),
        ],
        scratch_shapes=[
            pltpu.VMEM((rows, own, width), half), pltpu.VMEM((width, rows * own), half),
            dma((2, 31)), dma((2, 31)), dma((1,)), dma((rows,)), dma((rows,)), dma((rows,)), dma((YS * CS,)),
            dma((YS * CS,)), dma((YS * CS,)), dma((rows,)), dma((rows,)), dma((1,)),
        ],
        compiler_params=pltpu.CompilerParams(collective_id=0, has_side_effects=True, vmem_limit_bytes=40 << 20),
        name="gather_weights",
    )(inputs, ln_gain[None], ln_bias[None], counts, g1, out_grad)


PLACES = ZS * XS * YS * CS
PIECE = 256


def relative(dp, rel):
    return lax.rem(dp // CS + rel % YS, YS) * CS + lax.rem(dp % CS + rel // YS, CS)


def wide(ref, at, first, rows, count):
    return jnp.concatenate(
        [ref[at + (slice(first + b * rows, first + (b + 1) * rows),)] for b in range(count)], axis=-1
    )


def cotangent_kernel(place_ref, grad_ref, row_ref, weight_ref, piece_ref, branch_ref, turned_ref, row_turned_ref, ctx_ref,
                     w_ref, sum_ref):
    branch = (grad_ref[...].astype(jnp.float32) * weight_ref[...]).astype(jnp.bfloat16)
    branch_ref[...] = branch
    sum_ref[...] = jnp.sum(branch.astype(jnp.float32), axis=0, keepdims=True)
    for b in range(D // 128):
        w_ref[:, b * 128:(b + 1) * 128] = piece_ref[:, 0, b * 32:(b + 1) * 32, :].reshape(D, 128)
    branch_row = (row_ref[...].astype(jnp.float32) * weight_ref[...]).astype(jnp.bfloat16)
    ctx_ref[...] = mm(branch_row, w_ref[...], NT).astype(jnp.bfloat16)
    for rel in range(YS * CS):
        block = pl.ds(pl.multiple_of(relative(place_ref[0], rel) * PIECE, PIECE), PIECE)
        turned_ref[rel] = branch_ref[:, block].T
        row_turned_ref[rel] = (row_ref[:, block].astype(jnp.float32) * weight_ref[...]).astype(jnp.bfloat16).T


def cotangent(place, out_grad, grad_row, weight, g1):
    tokens = out_grad.shape[0]
    half = jnp.bfloat16
    shape = jax.ShapeDtypeStruct
    whole = lambda *dims: pl.BlockSpec(dims, lambda i, p: (0,) * len(dims), pipeline_mode=pl.Buffered(1))
    return pl.pallas_call(
        cotangent_kernel,
        grid_spec=pltpu.PrefetchScalarGridSpec(
            num_scalar_prefetch=1, grid=(1,),
            in_specs=[whole(tokens, D), whole(tokens, D), whole(1, 1),
                      pl.BlockSpec((PLACES, 1, 256, 128), lambda i, p: (0, 3, 0, 0))],
            out_specs=[whole(tokens, D), whole(4, PIECE, tokens), whole(4, PIECE, tokens), whole(tokens, D), whole(D, D),
                       whole(1, D)]),
        out_shape=[shape((tokens, D), half), shape((4, PIECE, tokens), half), shape((4, PIECE, tokens), half),
                   shape((tokens, D), half), shape((D, D), half), shape((1, D), jnp.float32)],
        compiler_params=pltpu.CompilerParams(vmem_limit_bytes=48 << 20),
        cost_estimate=pl.CostEstimate(flops=2 << 30, bytes_accessed=18 << 20, transcendentals=0),
        name="cotangent",
    )(place, out_grad, grad_row, weight, g1.reshape(PLACES, 4, 256, 128))


def project(rows, g1, cosines, sines):
    return pl.pallas_call(
        qkv_kernel,
        grid=(3, ZS),
        in_specs=[
            pl.BlockSpec((SEQ, D), lambda j, c: (0, 0)),
            pl.BlockSpec((8, 1, 256, 128), lambda j, c: (c, j, 0, 0)),
            pl.BlockSpec((SEQ, 128), lambda j, c: (0, 0)),
            pl.BlockSpec((SEQ, 128), lambda j, c: (0, 0)),
        ],
        out_specs=pl.BlockSpec((SEQ, 256), lambda j, c: (0, j * ZS + c)),
        out_shape=jax.ShapeDtypeStruct((SEQ, 3 * D), jnp.bfloat16),
        compiler_params=pltpu.CompilerParams(vmem_limit_bytes=40 << 20),
        cost_estimate=pl.CostEstimate(flops=6 << 30, bytes_accessed=14 << 20, transcendentals=0),
        name="qkv",
    )(rows, g1.reshape(PLACES, 4, 256, 128), cosines, sines)


def put_tiles(values, keep_ref, send_ref):
    for xr in range(XS):
        for yr in range(YS):
            keep_ref[yr, xr, 0] = values[xr][yr * PIECE:(yr + 1) * PIECE]
            send_ref[yr, xr, 0] = values[xr][(YS + yr) * PIECE:(YS + yr + 1) * PIECE]


def tile_specs(n, index):
    spec = pl.BlockSpec((YS, XS, 1, PIECE, n), index)
    return [spec, spec]


def tile_shapes(n):
    shape = jax.ShapeDtypeStruct((YS, XS, ZS, PIECE, n), jnp.bfloat16)
    return [shape, shape]


def by_x(x, value):
    low, high = value[:, :128], value[:, 128:]
    first = jnp.where(x == 0, low, high)
    return [first, jnp.where(x == 0, high, low)]


def back_kernel(place_ref, x_ref, w_ref, dq_ref, dk_ref, dv_ref, n_ref, keep_ref, send_ref, xt_ref, acc_ref):
    step = pl.program_id(0)

    @pl.when(step == 0)
    def _():
        for rel in range(YS * CS):
            block = relative(place_ref[0], rel)
            xt_ref[rel * PIECE:(rel + 1) * PIECE] = x_ref[:, pl.ds(pl.multiple_of(block * PIECE, PIECE), PIECE)].T
        acc_ref[...] = jnp.zeros_like(acc_ref)

    x = place_ref[1] % XS
    total = acc_ref[...]
    for j, d_ref in enumerate((dq_ref, dk_ref, dv_ref)):
        d = d_ref[...]
        total = total + mm(d, weight_block(w_ref.at[:, j:j + 1]), NT)
        values = by_x(x, mm(xt_ref[...], d).astype(jnp.bfloat16))
        lanes = pl.ds(j * 128, 128)
        put_tiles(values, keep_ref.at[..., lanes], send_ref.at[..., lanes])
    acc_ref[...] = total

    @pl.when(step == pl.num_programs(0) - 1)
    def _():
        n_ref[...] = acc_ref[...].astype(jnp.bfloat16)


def z_of(place, k):
    return lax.rem(place[1] // XS + k, ZS)


def back(place, rows, g1, grads):
    return pl.pallas_call(
        back_kernel,
        grid_spec=pltpu.PrefetchScalarGridSpec(
            num_scalar_prefetch=1, grid=(ZS,),
            in_specs=[
                pl.BlockSpec((SEQ, D), lambda k, p: (0, 0), pipeline_mode=pl.Buffered(1)),
                pl.BlockSpec((8, 3, 256, 128), lambda k, p: (z_of(p, k), 0, 0, 0)),
            ]
            + [pl.BlockSpec((SEQ, 256), lambda k, p: (0, z_of(p, k)))] * 3,
            out_specs=[pl.BlockSpec((SEQ, D), lambda k, p: (0, 0), pipeline_mode=pl.Buffered(1))]
            + tile_specs(384, lambda k, p: (0, 0, k, 0, 0)),
            scratch_shapes=[pltpu.VMEM((D, SEQ), jnp.bfloat16), pltpu.VMEM((SEQ, D), jnp.float32)]),
        out_shape=[jax.ShapeDtypeStruct((SEQ, D), jnp.bfloat16)] + tile_shapes(384),
        compiler_params=pltpu.CompilerParams(vmem_limit_bytes=48 << 20),
        cost_estimate=pl.CostEstimate(flops=12 << 30, bytes_accessed=22 << 20, transcendentals=0),
        name="attention_back",
    )(place, rows, g1.reshape(PLACES, 4, 256, 128), *grads)


C0 = math.sqrt(2.0 / math.pi)


def mlp_kernel(first, place_ref, x_ref, xt_ref, g_ref, gt_ref, wa_ref, wb_ref, *refs):
    if first:
        out_ref, dn_ref, keep_ref, send_ref, bsum_ref, out_acc, dn_acc = refs
    else:
        out_in, dn_in, out_ref, dn_ref, keep_ref, send_ref, bsum_ref, out_acc, dn_acc = refs
    step = pl.program_id(0)

    @pl.when(step == 0)
    def _():
        out_acc[...] = jnp.zeros_like(out_acc) if first else out_in[...]
        dn_acc[...] = jnp.zeros_like(dn_acc) if first else dn_in[...]

    w_in = jnp.concatenate([wide(r, (0, p, 0), 0, 128, 8) for r in (wa_ref, wb_ref) for p in range(CS)], axis=0)
    w_out = jnp.concatenate([wide(r, (0, p, 0), 1024, 128, 8) for r in (wa_ref, wb_ref) for p in range(CS)], axis=0)
    bias = jnp.concatenate([r[0, p, 0, 2048:2049] for r in (wa_ref, wb_ref) for p in range(CS)], axis=1)
    x = mm(x_ref[...], w_in, NT) + bias.astype(jnp.float32)
    squared = x * x
    tanh = jnp.tanh(C0 * x * (1.0 + 0.044715 * squared))
    half = 0.5 * (1.0 + tanh)
    act = (x * half).astype(jnp.bfloat16)
    slope = half + 0.5 * x * (1.0 - tanh * tanh) * (C0 * (1.0 + 3 * 0.044715 * squared))
    hid = (mm(g_ref[...], w_out, NT) * slope).astype(jnp.bfloat16)
    out_acc[...] += mm(act, w_out)
    dn_acc[...] += mm(hid, w_in)
    bsum_ref[0] = jnp.sum(hid.astype(jnp.float32), axis=0, keepdims=True)
    out_part = mm(gt_ref[...], act).astype(jnp.bfloat16)
    in_part = mm(xt_ref[...], hid).astype(jnp.bfloat16)
    put_tiles(
        [jnp.concatenate([out_part[:, a * 256:(a + 1) * 256], in_part[:, a * 256:(a + 1) * 256]], axis=1)
         for a in range(XS)], keep_ref, send_ref)

    @pl.when(step == pl.num_programs(0) - 1)
    def _():
        out_ref[...] = out_acc[...]
        dn_ref[...] = dn_acc[...]


def mlp_half(h, place, normed, normed_turned, branch, branch_turned, g2, sums):
    tokens = normed.shape[0]
    one = lambda *dims: pl.BlockSpec(dims, lambda k, p: (0,) * len(dims), pipeline_mode=pl.Buffered(1))
    weight = lambda xr: pl.BlockSpec(
        (1, CS, 1, G2_ROWS, 128),
        lambda k, p: (h, 0, z_of(p, k) * XS + lax.rem(p[1] % XS + xr, XS), 0, 0))
    views = g2.reshape(YS, CS, ZS * XS, G2_ROWS, 128)
    full = jax.ShapeDtypeStruct((tokens, D), jnp.float32)
    return pl.pallas_call(
        partial(mlp_kernel, not sums),
        grid_spec=pltpu.PrefetchScalarGridSpec(
            num_scalar_prefetch=1, grid=(ZS,),
            in_specs=[one(tokens, D), one(D, tokens), one(tokens, D), one(D, tokens), weight(0), weight(1)]
            + [one(tokens, D)] * len(sums),
            out_specs=[one(tokens, D), one(tokens, D)] + tile_specs(512, lambda k, p: (0, 0, k, 0, 0))
            + [pl.BlockSpec((1, 1, 512), lambda k, p: (k, 0, 0))],
            scratch_shapes=[pltpu.VMEM((tokens, D), jnp.float32), pltpu.VMEM((tokens, D), jnp.float32)]),
        out_shape=[full, full] + tile_shapes(512) + [jax.ShapeDtypeStruct((ZS, 1, 512), jnp.float32)],
        compiler_params=pltpu.CompilerParams(vmem_limit_bytes=62 << 20),
        cost_estimate=pl.CostEstimate(flops=26 << 30, bytes_accessed=30 << 20, transcendentals=2 << 20),
        name="mlp",
    )(place, normed, normed_turned.reshape(D, tokens), branch, branch_turned.reshape(D, tokens), views, views, *sums)


def output_kernel(place_ref, ctx_ref, w_ref, gt_ref, out_ref, keep_ref, send_ref, acc_ref):
    step = pl.program_id(0)
    ctx = ctx_ref[...]

    @pl.when(step == 0)
    def _():
        acc_ref[...] = jnp.zeros_like(acc_ref)

    acc_ref[...] += mm(ctx, w_ref[...])
    put_tiles(by_x(place_ref[1] % XS, mm(gt_ref[...], ctx).astype(jnp.bfloat16)), keep_ref, send_ref)

    @pl.when(step == pl.num_programs(0) - 1)
    def _():
        out_ref[...] = acc_ref[...].astype(jnp.bfloat16)


def row_output(place, context, w_output, branch_turned):
    tokens = context.shape[0]
    whole = lambda *dims: pl.BlockSpec(dims, lambda k, p: (0,) * len(dims), pipeline_mode=pl.Buffered(1))
    return pl.pallas_call(
        output_kernel,
        grid_spec=pltpu.PrefetchScalarGridSpec(
            num_scalar_prefetch=1, grid=(ZS,),
            in_specs=[
                pl.BlockSpec((tokens, 256), lambda k, p: (0, z_of(p, k))),
                pl.BlockSpec((256, D), lambda k, p: (z_of(p, k), 0)),
                whole(D, tokens),
            ],
            out_specs=[whole(tokens, D)] + tile_specs(128, lambda k, p: (0, 0, k, 0, 0)),
            scratch_shapes=[pltpu.VMEM((tokens, D), jnp.float32)]),
        out_shape=[jax.ShapeDtypeStruct((tokens, D), jnp.bfloat16)] + tile_shapes(128),
        compiler_params=pltpu.CompilerParams(vmem_limit_bytes=48 << 20),
        cost_estimate=pl.CostEstimate(flops=4 << 30, bytes_accessed=12 << 20, transcendentals=0),
        name="row_output",
    )(place, context, w_output, branch_turned.reshape(D, tokens))


def norm_back_kernel(x_ref, g_ref, a_ref, m_ref, ao_ref, mo_ref, gain_ref, bo_ref, weight_ref, out_ref, layer_ref, sums_ref):
    x = x_ref[...].astype(jnp.float32)
    layer = x + bo_ref[...].astype(jnp.float32) + ao_ref[...].astype(jnp.float32) + mo_ref[...]
    layer_ref[...] = layer.astype(jnp.bfloat16)
    centred = x - jnp.mean(x, axis=-1, keepdims=True)
    inverse = lax.rsqrt(jnp.mean(centred * centred, axis=-1, keepdims=True) + EPSILON)
    standard = centred * inverse
    grad = a_ref[...].astype(jnp.float32) + m_ref[...]
    scaled = grad * gain_ref[...]
    part = inverse * (
        scaled
        - jnp.mean(scaled, axis=-1, keepdims=True)
        - standard * jnp.mean(scaled * standard, axis=-1, keepdims=True)
    )
    out_ref[...] = (g_ref[...].astype(jnp.float32) * weight_ref[...] + part).astype(jnp.bfloat16)
    sums = jnp.concatenate(
        [jnp.sum(grad * standard, axis=0, keepdims=True), jnp.sum(grad, axis=0, keepdims=True)], axis=0)

    @pl.when(pl.program_id(0) == 0)
    def _():
        sums_ref[...] = sums

    @pl.when(pl.program_id(0) > 0)
    def _():
        sums_ref[...] += sums


def norm_back(inputs, out_grad, attn_grad, mlp_grad, attn_out, mlp_out, ln_gain, b_out, weight):
    tokens = inputs.shape[0]
    block = pl.BlockSpec((128, D), lambda i: (i, 0))
    row = pl.BlockSpec((1, D), lambda i: (0, 0))
    shape = jax.ShapeDtypeStruct((tokens, D), jnp.bfloat16)
    return pl.pallas_call(
        norm_back_kernel,
        grid=(tokens // 128,),
        in_specs=[block] * 6 + [row, row, pl.BlockSpec((1, 1), lambda i: (0, 0))],
        out_specs=[block, block, pl.BlockSpec((2, D), lambda i: (0, 0))],
        out_shape=[shape, shape, jax.ShapeDtypeStruct((2, D), jnp.float32)],
        cost_estimate=pl.CostEstimate(flops=20 << 20, bytes_accessed=20 << 20, transcendentals=0),
        name="norm_back",
    )(inputs, out_grad, attn_grad, mlp_grad, attn_out, mlp_out, ln_gain[None], b_out[None], weight)


HALF_PIECE = PIECE // 2
Z_ORDER = (2, 1, 3, 0)
BAND = 16


def reduce_kernel(*refs):
    sets = len(SET_WIDTHS)
    keeps, sends, small_ref = refs[:sets], refs[sets:2 * sets], refs[2 * sets]
    out_ref, small_out = refs[2 * sets + 1:2 * sets + 3]
    (own, got, first, second, last, small_got, small_own, own_sem, core_send, core_recv, first_send, first_recv,
     second_send, second_recv, last_send, last_recv, small_send, small_recv, small_sem) = refs[2 * sets + 3:]
    dp, mp = lax.axis_index("dp"), lax.axis_index("mp")
    y, c, z, x = dp // CS, dp % CS, mp // XS, mp % XS

    def device(z, x, y, c):
        return (y * CS + c, z * XS + x)

    groups, members = YS * CS, ZS * XS
    everyone = [(lax.rem(dp + a, groups), lax.rem(mp + b, members))
                for a in range(groups) for b in range(members) if (a, b) != (0, 0)]
    starts = [sum(SET_WIDTHS[:i]) for i in range(sets)]

    def mine(s, k):
        return pltpu.make_async_copy(
            keeps[s].at[:, :, k], own.at[k, :, :, :, pl.ds(starts[s], SET_WIDTHS[s])], own_sem.at[s, k])

    for k in Z_ORDER:
        for s in range(sets):
            mine(s, k).start()
    barrier = pltpu.get_barrier_semaphore()
    for other in everyone:
        pl.semaphore_signal(barrier, inc=1, device_id=other, device_id_type=MESH_ID)
    pl.semaphore_wait(barrier, len(everyone))

    def core(s, k):
        return pltpu.make_async_remote_copy(
            src_ref=sends[s].at[:, :, k], dst_ref=got.at[k, :, :, :, pl.ds(starts[s], SET_WIDTHS[s])],
            send_sem=core_send.at[s, k], recv_sem=core_recv.at[s, k],
            device_id=device(z, x, y, 1 - c), device_id_type=MESH_ID)

    for k in Z_ORDER:
        for s in range(sets):
            core(s, k).start()

    spot = dp * members + mp
    small_local = pltpu.make_async_copy(small_ref.at[spot], small_got.at[0], small_sem.at[0])
    small_local.start()
    small_copies = []
    for i, (a, b) in enumerate(everyone):
        copy = pltpu.make_async_remote_copy(
            src_ref=small_ref.at[a * members + b], dst_ref=small_got.at[i + 1], send_sem=small_send.at[i],
            recv_sem=small_recv.at[i], device_id=(a, b), device_id_type=MESH_ID)
        copy.start()
        small_copies.append(copy)

    def at(half, away, other):
        return (other, away) if half == 0 else (away, other)

    def rows(half):
        return half * HALF_PIECE

    def bands(body):
        lax.fori_loop(0, HALF_PIECE // BAND, lambda i, carry: (body(pl.multiple_of(i * BAND, BAND)), carry)[1], 0)

    def total(k, half, away, other, r, *extra):
        yy, xx = at(half, away, other)
        upper = pl.ds(rows(half) + r, BAND)
        value = own[k, yy, xx, upper].astype(jnp.float32) + got[k, yy, xx, upper].astype(jnp.float32)
        for ref in extra:
            value = value + ref[pl.ds(r, BAND)].astype(jnp.float32)
        return value

    def store(k, half, away, other, *extra):
        yy, xx = at(half, away, other)

        def body(r):
            own[k, yy, xx, pl.ds(rows(half) + r, BAND)] = total(k, half, away, other, r, *extra).astype(jnp.bfloat16)

        bands(body)
        return own.at[k, yy, xx, pl.ds(rows(half), HALF_PIECE)]

    axes = (device(z, 1 - x, y, c), device(z, x, 1 - y, c))

    def one(k, half, other):
        yy, xx = at(half, 1, other)
        return pltpu.make_async_remote_copy(
            src_ref=own.at[k, yy, xx, pl.ds(rows(half), HALF_PIECE)], dst_ref=first.at[k, half, other],
            send_sem=first_send.at[k, half, other], recv_sem=first_recv.at[k, half, other],
            device_id=axes[half], device_id_type=MESH_ID)

    def two(k, half):
        yy, xx = at(half, 0, 1)
        return pltpu.make_async_remote_copy(
            src_ref=own.at[k, yy, xx, pl.ds(rows(half), HALF_PIECE)], dst_ref=second.at[k, half],
            send_sem=second_send.at[k, half], recv_sem=second_recv.at[k, half],
            device_id=axes[1 - half], device_id_type=MESH_ID)

    def three(k, half):
        return pltpu.make_async_remote_copy(
            src_ref=own.at[k, 0, 0, pl.ds(rows(half), HALF_PIECE)], dst_ref=last.at[k, half],
            send_sem=last_send.at[k, half], recv_sem=last_recv.at[k, half],
            device_id=device(lax.rem(z + k, ZS), x, y, c), device_id_type=MESH_ID)

    def stage_one(k):
        for s in range(sets):
            mine(s, k).wait()
            core(s, k).wait_recv()
        for other in (1, 0):
            for half in range(2):
                store(k, half, 1, other)
                one(k, half, other).start()

    def stage_two(k):
        for half in range(2):
            one(k, half, 1).wait_recv()
            store(k, half, 0, 1, first.at[k, half, 1])
            two(k, half).start()

    def stage_three(k):
        for half in range(2):
            one(k, half, 0).wait_recv()
            two(k, half).wait_recv()
            if k:
                store(k, half, 0, 0, first.at[k, half, 0], second.at[k, half])
                three(k, half).start()

    order = Z_ORDER
    stage_one(order[0])
    stage_one(order[1])
    stage_two(order[0])
    stage_one(order[2])
    stage_three(order[0])
    stage_two(order[1])
    stage_one(order[3])
    stage_three(order[1])
    stage_two(order[2])
    stage_three(order[2])
    stage_two(order[3])
    small_local.wait()
    for copy in small_copies:
        copy.wait_recv()
    summed = small_got[0]
    for i in range(1, PLACES):
        summed = summed + small_got[i]
    small_out[...] = summed
    stage_three(0)
    for half in range(2):
        for k in range(1, ZS):
            three(k, half).wait_recv()

        def body(r):
            value = total(0, half, 0, 0, r, first.at[0, half, 0], second.at[0, half])
            for k in range(1, ZS):
                value = value + last[k, half, pl.ds(r, BAND)].astype(jnp.float32)
            out_ref[pl.ds(rows(half) + r, BAND)] = value

        bands(body)
    for k in range(ZS):
        for s in range(sets):
            core(s, k).wait_send()
        for half in range(2):
            for other in range(2):
                one(k, half, other).wait_send()
            two(k, half).wait_send()
            if k:
                three(k, half).wait_send()
    for copy in small_copies:
        copy.wait_send()


SET_WIDTHS = (384, 128, 512, 512)


def reduce_tiles(keeps, sends, small):
    width, sets = sum(SET_WIDTHS), len(SET_WIDTHS)
    any_space, vmem = pl.BlockSpec(memory_space=pl.ANY), pl.BlockSpec(memory_space=pltpu.VMEM)
    half = jnp.bfloat16
    dma = pltpu.SemaphoreType.DMA
    return pl.pallas_call(
        reduce_kernel,
        in_specs=[any_space] * (2 * sets + 1),
        out_specs=[vmem, vmem],
        out_shape=[jax.ShapeDtypeStruct((PIECE, width), jnp.float32), jax.ShapeDtypeStruct((8, 128), jnp.float32)],
        scratch_shapes=[
            pltpu.VMEM((ZS, YS, XS, PIECE, width), half), pltpu.VMEM((ZS, YS, XS, PIECE, width), half),
            pltpu.VMEM((ZS, 2, 2, HALF_PIECE, width), half), pltpu.VMEM((ZS, 2, HALF_PIECE, width), half),
            pltpu.VMEM((ZS, 2, HALF_PIECE, width), half), pltpu.VMEM((PLACES, 8, 128), jnp.float32),
            pltpu.VMEM((8, 128), jnp.float32),
            dma((sets, ZS)), dma((sets, ZS)), dma((sets, ZS)), dma((ZS, 2, 2)), dma((ZS, 2, 2)),
            dma((ZS, 2)), dma((ZS, 2)), dma((ZS, 2)), dma((ZS, 2)), dma((PLACES,)), dma((PLACES,)), dma((1,)),
        ],
        compiler_params=pltpu.CompilerParams(collective_id=1, has_side_effects=True, vmem_limit_bytes=56 << 20),
        name="reduce_tiles",
    )(*keeps, *sends, small)


def on_device_rows(
    inputs,
    seg_lengths,
    group_counts,
    out_grad,
    ln_gain,
    ln_bias,
    w_query,
    w_key,
    w_value,
    w_output,
    w_in,
    b_in,
    w_out,
    b_out,
):
    row_count, own_tokens = inputs.shape[0], inputs.shape[1]
    tokens = row_count * own_tokens
    group, member = lax.axis_index("dp"), lax.axis_index("mp")
    place = jnp.stack([group, member]).astype(jnp.int32)

    def quarter(matrix, axis):
        size = matrix.shape[axis] // (YS * CS)
        return lax.dynamic_slice_in_dim(matrix, group * size, size, axis)

    def narrow(matrix):
        return matrix.reshape(matrix.shape[0], D // 128, 128).transpose(1, 0, 2).reshape(-1, 128)

    def exchange(tensor):
        blocks = tensor.reshape(row_count, own_tokens, D)
        return lax.all_to_all(blocks, "mp", 0, 0, tiled=True).reshape(tokens, D)

    counts = jnp.broadcast_to(group_counts.astype(jnp.float32)[:, None], (8, 128))
    g1 = jnp.concatenate(
        [quarter(w_query, 0), quarter(w_key, 0), quarter(w_value, 0), narrow(quarter(w_output, 0))], axis=0)
    bias_rows = jnp.pad(quarter(b_in, 0)[None], ((0, G2_ROWS - 2049), (0, 0)))
    g2 = jnp.concatenate([narrow(quarter(w_in, 0)), narrow(quarter(w_out, 0)), bias_rows], axis=0)
    normed, normed_turned, normed_row, grad_row, g1_all, counts_all = gather_all(
        inputs, ln_gain, ln_bias, counts, g1, out_grad)
    g2, normed_row = lax.optimization_barrier((g2, normed_row))
    g2_all = lax.all_gather(g2, ("dp", "mp"))
    normed = normed.reshape(tokens, D)
    weight = (YS * CS * counts_all[group, 0, 0] / jnp.sum(counts_all[:, 0, 0])).reshape(1, 1)

    flat_grad = out_grad.reshape(tokens, D)
    branch, branch_turned, row_turned, ctx_grad_row, w_output_all, out_sum = cotangent(
        place, flat_grad, grad_row, weight, g1_all)
    own_row = lax.dynamic_index_in_dim(seg_lengths, member, 0, keepdims=True)
    _, positions = segment_layout(own_row)
    positions = positions[0]
    cosines, sines = lane_tables(positions)
    starts = jnp.arange(SEQ, dtype=jnp.int32) - positions
    qkv = project(normed_row, g1_all, cosines, sines)
    context_row, qkv_grad = attention(qkv, ctx_grad_row, starts, cosines, sines)
    out_row, keep_o, send_o = row_output(place, context_row, w_output_all, row_turned)
    attn_out = exchange(out_row)
    normed_row_grad, keep_a, send_a = back(place, normed_row, g1_all, qkv_grad)
    normed, keep_a = lax.optimization_barrier((normed, keep_a))
    mlp_out, mlp_grad, keep0, send0, bsum0 = mlp_half(
        0, place, normed, normed_turned, branch, branch_turned, g2_all, ())
    normed_row_grad, keep0 = lax.optimization_barrier((normed_row_grad, keep0))
    attn_grad = exchange(normed_row_grad)
    mlp_out, mlp_grad, keep1, send1, bsum1 = mlp_half(
        1, place, normed, normed_turned, branch, branch_turned, g2_all, (mlp_out, mlp_grad))
    input_grad, layer_out, sums = norm_back(
        inputs.reshape(tokens, D), flat_grad, attn_grad, mlp_grad, attn_out, mlp_out, ln_gain, b_out, weight)

    bsums = jnp.stack([bsum0, bsum1]).reshape(YS, ZS * XS, CS, 128)
    targets = jnp.arange(ZS * XS)
    spots = (targets // XS - member // XS) % ZS * XS + (targets % XS - member % XS) % XS
    bsums = jnp.take(bsums, spots, axis=1).transpose(1, 0, 2, 3).reshape(ZS * XS, 4, 128)
    own = D // PLACES
    vectors = jnp.concatenate([sums, out_sum], axis=0).reshape(3, PLACES, own).transpose(1, 0, 2)
    vectors = jnp.pad(vectors, ((0, 0), (0, 1), (0, 128 - own)))
    small = jnp.concatenate([jnp.tile(bsums, (YS * CS, 1, 1)), vectors], axis=1)
    grads, small = reduce_tiles((keep_a, keep_o, keep0, keep1), (send_a, send_o, send0, send1), small)
    shape = (row_count, own_tokens, D)
    return (
        layer_out.reshape(shape),
        input_grad.reshape(shape),
        small[4, :own],
        small[5, :own],
        grads[:, :128],
        grads[:, 128:256],
        grads[:, 256:384],
        grads[:, 384:512].T,
        jnp.concatenate([grads[:, 768:1024], grads[:, 1280:]], axis=1).T,
        small[:4].reshape(512),
        jnp.concatenate([grads[:, 512:768], grads[:, 1024:1280]], axis=1).T,
        small[6, :own],
    )


def solution(mesh):
    placed = (
        P("dp", "mp", None),
        P("dp", None),
        P("dp"),
        P("dp", "mp", None),
        P(),
        P(),
        P(None, "mp"),
        P(None, "mp"),
        P(None, "mp"),
        P("mp", None),
        P("mp", None),
        P("mp"),
        P("mp", None),
        P(),
    )
    sizes = (mesh.shape["dp"], mesh.shape["mp"])

    def on_device(*args):
        if sizes == (YS * CS, ZS * XS) and args[0].shape[0] == ZS * XS:
            return on_device_rows(*args)
        return on_device_gathered(*args)

    return jax.shard_map(
        on_device,
        mesh=mesh,
        in_specs=placed,
        out_specs=(
            P("dp", "mp", None),
            P("dp", "mp", None),
            P(("dp", "mp")),
            P(("dp", "mp")),
            P("dp", "mp"),
            P("dp", "mp"),
            P("dp", "mp"),
            P("mp", "dp"),
            P("mp", "dp"),
            P("mp"),
            P("mp", "dp"),
            P(("dp", "mp")),
        ),
        check_vma=False,
    )
```

```python
from functools import partial
import math
import jax
import jax.numpy as jnp
from jax import lax
from jax.sharding import PartitionSpec as P
from jax.experimental import pallas as pl
from jax.experimental.pallas import tpu as pltpu


D = 1024
HD = 64
ROT = 32
SEQ = 1024


EPSILON = 1e-05


def segment_layout(seg_lengths):
    seg_ends = jnp.cumsum(seg_lengths, axis=-1)
    seg_starts = seg_ends - seg_lengths
    places = jnp.arange(SEQ, dtype=jnp.int32)
    passed = places[None, :, None] >= seg_ends[:, None, :]
    seg_ids = jnp.sum(passed.astype(jnp.int32), axis=-1)
    inside = (places[None, :, None] >= seg_starts[:, None, :]) & jnp.logical_not(passed)
    begins = jnp.sum(jnp.where(inside, seg_starts[:, None, :], 0), axis=-1)
    return (seg_ids, places[None, :] - begins)


def rotary_tables(positions):
    exponents = jnp.arange(0, ROT, 2, dtype=jnp.float32) / ROT
    freqs = jnp.power(10000.0, -exponents)
    angles = positions.astype(jnp.float32)[..., None] * freqs
    return (jnp.cos(angles)[..., None, :], jnp.sin(angles)[..., None, :])


def turn_pairs(tensor, cosines, sines):
    rotary = tensor[..., :ROT]
    passive = tensor[..., ROT:]
    paired = rotary.reshape(rotary.shape[:-1] + (ROT // 2, 2))
    evens = paired[..., 0]
    odd_part = paired[..., 1]
    turned = jnp.stack(
        [evens * cosines - odd_part * sines, evens * sines + odd_part * cosines], axis=-1
    )
    return jnp.concatenate([turned.reshape(rotary.shape), passive], axis=-1)


def norm_rows(inputs, ln_gain, ln_bias):
    values_in = inputs.astype(jnp.float32)
    centred = values_in - jnp.mean(values_in, axis=-1, keepdims=True)
    inverse = lax.rsqrt(jnp.mean(centred * centred, axis=-1, keepdims=True) + EPSILON)
    standard = centred * inverse
    return (standard, inverse, (standard * ln_gain + ln_bias).astype(jnp.bfloat16))


def masked_scores(queries, keys_rot, seg_ids):
    places = jnp.arange(SEQ, dtype=jnp.int32)
    allowed = (seg_ids[:, None] == seg_ids[None, :]) & (places[:, None] >= places[None, :])
    scores = jnp.einsum("qhd,khd->hqk", queries, keys_rot, preferred_element_type=jnp.float32) * (
        1.0 / math.sqrt(HD)
    )
    return jnp.where(allowed[None], scores, -1e30)


def attend_forward(operands):
    queries, keys_rot, values, seg_ids = operands
    scores = masked_scores(queries, keys_rot, seg_ids)
    row_peak = jnp.max(scores, axis=-1, keepdims=True)
    lifted = jnp.exp(scores - row_peak)
    row_mass = jnp.sum(lifted, axis=-1, keepdims=True)
    probs = (lifted / row_mass).astype(jnp.bfloat16)
    context = jnp.einsum("hqk,khd->qhd", probs, values, preferred_element_type=jnp.float32)
    return (context.astype(jnp.bfloat16), (row_peak + jnp.log(row_mass))[..., 0])


def attend_backward(operands):
    queries, keys_rot, values, seg_ids, log_mass, ctx_grad = operands
    score_scale = 1.0 / math.sqrt(HD)
    scores = masked_scores(queries, keys_rot, seg_ids)
    probs = jnp.exp(scores - log_mass[..., None])
    rounded = probs.astype(jnp.bfloat16)
    value_grad = jnp.einsum("hqk,qhd->khd", rounded, ctx_grad, preferred_element_type=jnp.float32)
    prob_grad = jnp.einsum("qhd,khd->hqk", ctx_grad, values, preferred_element_type=jnp.float32)
    score_grad = (probs * (prob_grad - jnp.sum(probs * prob_grad, axis=-1, keepdims=True))).astype(
        jnp.bfloat16
    )
    query_grad = (
        jnp.einsum("hqk,khd->qhd", score_grad, keys_rot, preferred_element_type=jnp.float32)
        * score_scale
    )
    key_grad = (
        jnp.einsum("hqk,qhd->khd", score_grad, queries, preferred_element_type=jnp.float32)
        * score_scale
    )
    return (query_grad, key_grad, value_grad)


def project_heads(flat_rows, matrix, row_count):
    local_heads = matrix.shape[1] // HD
    return jnp.dot(flat_rows, matrix, preferred_element_type=jnp.float32).reshape(
        row_count, -1, local_heads, HD
    )


def attention_inputs(flat_rows, w_query, w_key, w_value, cosines, sines, row_count):
    queries = turn_pairs(project_heads(flat_rows, w_query, row_count), cosines, sines).astype(
        jnp.bfloat16
    )
    keys_rot = turn_pairs(project_heads(flat_rows, w_key, row_count), cosines, sines).astype(
        jnp.bfloat16
    )
    values = project_heads(flat_rows, w_value, row_count).astype(jnp.bfloat16)
    return (queries, keys_rot, values)


def mlp_inputs(flat_rows, w_in, b_in):
    hidden = jnp.dot(flat_rows, w_in.T, preferred_element_type=jnp.float32) + b_in.astype(
        jnp.float32
    )
    return (hidden, jax.nn.gelu(hidden, approximate=True).astype(jnp.bfloat16))


def gelu_grad(hidden, act_grad):
    pulled = jax.vjp(partial(jax.nn.gelu, approximate=True), hidden)[1](act_grad)[0]
    return pulled.astype(jnp.bfloat16)


def head_products(flat_rows, query_back, key_back, value_back, w_query, w_key, w_value):
    normed_part = (
        jnp.dot(query_back, w_query.T, preferred_element_type=jnp.float32)
        + jnp.dot(key_back, w_key.T, preferred_element_type=jnp.float32)
        + jnp.dot(value_back, w_value.T, preferred_element_type=jnp.float32)
    )
    w_query_part = jnp.dot(flat_rows.T, query_back, preferred_element_type=jnp.float32)
    w_key_part = jnp.dot(flat_rows.T, key_back, preferred_element_type=jnp.float32)
    w_value_part = jnp.dot(flat_rows.T, value_back, preferred_element_type=jnp.float32)
    return (normed_part, w_query_part, w_key_part, w_value_part)


def on_device_gathered(
    inputs,
    seg_lengths,
    group_counts,
    out_grad,
    ln_gain,
    ln_bias,
    w_query,
    w_key,
    w_value,
    w_output,
    w_in,
    b_in,
    w_out,
    b_out,
):
    row_count = inputs.shape[0]
    own_tokens = inputs.shape[1]
    local_width = w_query.shape[1]
    local_heads = local_width // HD
    seg_ids, positions = segment_layout(seg_lengths)
    cosines, sines = rotary_tables(positions)
    standard, inverse, normed = norm_rows(inputs, ln_gain, ln_bias)
    base_out = inputs.astype(jnp.float32) + b_out.astype(jnp.float32)
    gathered = lax.all_gather(normed, "mp", axis=1, tiled=True)
    flat_rows = gathered.reshape(row_count * SEQ, D)
    queries, keys_rot, values = attention_inputs(
        flat_rows, w_query, w_key, w_value, cosines, sines, row_count
    )
    context, log_mass = lax.map(attend_forward, (queries, keys_rot, values, seg_ids))
    ctx_flat = context.reshape(row_count * SEQ, local_width)
    hidden, activated = mlp_inputs(flat_rows, w_in, b_in)
    partial_out = jnp.dot(ctx_flat, w_output, preferred_element_type=jnp.float32) + jnp.dot(
        activated, w_out, preferred_element_type=jnp.float32
    )
    summed = lax.psum_scatter(
        partial_out.reshape(row_count, SEQ, D).astype(jnp.bfloat16),
        "mp",
        scatter_dimension=1,
        tiled=True,
    ).astype(jnp.float32)
    layer_out = (base_out + summed).astype(jnp.bfloat16)
    counts_now = group_counts.astype(jnp.float32)
    total_count = lax.psum(counts_now, "dp")
    weight_now = lax.axis_size("dp") * counts_now[0] / total_count[0]
    own_grad = out_grad.astype(jnp.float32) * weight_now
    own_rounded = own_grad.astype(jnp.bfloat16).reshape(row_count * own_tokens, D)
    cot_rows = lax.all_gather(out_grad, "mp", axis=1, tiled=True)
    branch_grad = (
        (cot_rows.astype(jnp.float32) * weight_now).astype(jnp.bfloat16).reshape(row_count * SEQ, D)
    )
    act_grad = jnp.dot(branch_grad, w_out.T, preferred_element_type=jnp.float32)
    hidden_grad = gelu_grad(hidden, act_grad)
    w_out_part = jnp.dot(activated.T, branch_grad, preferred_element_type=jnp.float32)
    w_in_part = jnp.dot(hidden_grad.T, flat_rows, preferred_element_type=jnp.float32)
    b_in_part = jnp.sum(hidden_grad.astype(jnp.float32), axis=0)
    ctx_grad = jnp.dot(branch_grad, w_output.T, preferred_element_type=jnp.float32).astype(
        jnp.bfloat16
    )
    w_output_part = jnp.dot(ctx_flat.T, branch_grad, preferred_element_type=jnp.float32)
    rot_query_grad, rot_key_grad, value_grad = lax.map(
        attend_backward,
        (
            queries,
            keys_rot,
            values,
            seg_ids,
            log_mass,
            ctx_grad.reshape(row_count, SEQ, local_heads, HD),
        ),
    )
    query_back = (
        turn_pairs(rot_query_grad, cosines, -sines)
        .astype(jnp.bfloat16)
        .reshape(row_count, SEQ, local_width)
    )
    key_back = (
        turn_pairs(rot_key_grad, cosines, -sines)
        .astype(jnp.bfloat16)
        .reshape(row_count, SEQ, local_width)
    )
    value_back = value_grad.astype(jnp.bfloat16).reshape(row_count, SEQ, local_width)
    normed_part, w_query_part, w_key_part, w_value_part = head_products(
        flat_rows,
        query_back.reshape(row_count * SEQ, local_width),
        key_back.reshape(row_count * SEQ, local_width),
        value_back.reshape(row_count * SEQ, local_width),
        w_query,
        w_key,
        w_value,
    )
    normed_part = normed_part + jnp.dot(hidden_grad, w_in, preferred_element_type=jnp.float32)
    normed_grad = lax.psum_scatter(
        normed_part.reshape(row_count, SEQ, D).astype(jnp.bfloat16),
        "mp",
        scatter_dimension=1,
        tiled=True,
    ).astype(jnp.float32)
    scaled = normed_grad * ln_gain
    input_part = inverse * (
        scaled
        - jnp.mean(scaled, axis=-1, keepdims=True)
        - standard * jnp.mean(scaled * standard, axis=-1, keepdims=True)
    )
    input_grad = (own_grad + input_part).astype(jnp.bfloat16)
    gain_part = jnp.sum(normed_grad * standard, axis=(0, 1))
    bias_part = jnp.sum(normed_grad, axis=(0, 1))
    out_bias_part = jnp.sum(own_rounded.astype(jnp.float32), axis=0)
    ln_gain_grad, ln_bias_grad, b_out_grad = (
        lax.psum_scatter(gain_part, ("dp", "mp"), scatter_dimension=0, tiled=True),
        lax.psum_scatter(bias_part, ("dp", "mp"), scatter_dimension=0, tiled=True),
        lax.psum_scatter(out_bias_part, ("dp", "mp"), scatter_dimension=0, tiled=True),
    )
    w_query_grad, w_key_grad, w_value_grad = (
        lax.psum_scatter(
            w_query_part.astype(jnp.bfloat16), "dp", scatter_dimension=0, tiled=True
        ).astype(jnp.float32),
        lax.psum_scatter(
            w_key_part.astype(jnp.bfloat16), "dp", scatter_dimension=0, tiled=True
        ).astype(jnp.float32),
        lax.psum_scatter(
            w_value_part.astype(jnp.bfloat16), "dp", scatter_dimension=0, tiled=True
        ).astype(jnp.float32),
    )
    w_output_grad, w_in_grad, w_out_grad = (
        lax.psum_scatter(
            w_output_part.astype(jnp.bfloat16), "dp", scatter_dimension=1, tiled=True
        ).astype(jnp.float32),
        lax.psum_scatter(
            w_in_part.astype(jnp.bfloat16), "dp", scatter_dimension=1, tiled=True
        ).astype(jnp.float32),
        lax.psum_scatter(
            w_out_part.astype(jnp.bfloat16), "dp", scatter_dimension=1, tiled=True
        ).astype(jnp.float32),
    )
    b_in_grad = lax.psum(b_in_part, "dp")
    return (
        layer_out,
        input_grad,
        ln_gain_grad,
        ln_bias_grad,
        w_query_grad,
        w_key_grad,
        w_value_grad,
        w_output_grad,
        w_in_grad,
        b_in_grad,
        w_out_grad,
        b_out_grad,
    )


QB = 256

NT = (((1,), (1,)), ((), ()))
NN = (((1,), (0,)), ((), ()))


def mm(a, b, dims=NN):
    return lax.dot_general(a, b, dims, preferred_element_type=jnp.float32)


def lane_turn(x, cosines, sines):
    width = x.shape[1]
    lanes = lax.broadcasted_iota(jnp.int32, x.shape, 1)
    swapped = jnp.where(lanes % 2 == 0, pltpu.roll(x, width - 1, 1), pltpu.roll(x, 1, 1))
    return x * cosines + swapped * sines


def attn_kernel(kb_ref, start_ref, q_ref, k_ref, v_ref, do_ref, cosq_ref, sinq_ref, cos_ref, sin_ref,
                ctx_ref, dq_ref, dk_ref, dv_ref, dk_acc, dv_acc, bias_ref):
    i, hp = pl.program_id(0), pl.program_id(1)
    kb = kb_ref[i]

    @pl.when(i == 0)
    def _():
        dk_acc[hp] = jnp.zeros(dk_acc.shape[1:], jnp.float32)
        dv_acc[hp] = jnp.zeros(dv_acc.shape[1:], jnp.float32)

    def body(blocks):
        w = blocks * QB
        k0 = pl.multiple_of(kb * QB, QB)

        @pl.when(hp == 0)
        def _():
            keys = lax.broadcasted_iota(jnp.int32, (w, QB), 0) + k0
            queries = lax.broadcasted_iota(jnp.int32, (w, QB), 1) + i * QB
            fine = (keys >= start_ref[...]) & (keys <= queries)
            bias_ref[:w] = jnp.where(fine, 0.0, -1e30)

        q, do = q_ref[...], do_ref[...]
        low = lax.broadcasted_iota(jnp.int32, q.shape, 1) < HD
        zero = jnp.zeros_like(q)
        k, v = k_ref[pl.ds(k0, w), :], v_ref[pl.ds(k0, w), :]
        kt, vt = k.T, v.T
        outs, dqs = [], []
        dk_new, dv_new = dk_acc[hp, pl.ds(k0, w), :], dv_acc[hp, pl.ds(k0, w), :]
        for head in range(2):
            qh = jnp.where(low, q, zero) if head == 0 else jnp.where(low, zero, q)
            doh = jnp.where(low, do, zero) if head == 0 else jnp.where(low, zero, do)
            s = mm(k, qh, NT) + bias_ref[:w]
            e = jnp.exp(s - jnp.max(s, axis=0, keepdims=True))
            p = e * (1.0 / jnp.sum(e, axis=0, keepdims=True))
            pb = p.astype(jnp.bfloat16)
            pd = p * mm(v, doh, NT)
            ds = (pd - p * jnp.sum(pd, axis=0, keepdims=True)).astype(jnp.bfloat16)
            dv_new = dv_new + mm(pb, doh)
            dk_new = dk_new + mm(ds, qh)
            outs.append(mm(vt[head * HD:(head + 1) * HD], pb))
            dqs.append(mm(kt[head * HD:(head + 1) * HD], ds))
        dk_acc[hp, pl.ds(k0, w), :] = dk_new
        dv_acc[hp, pl.ds(k0, w), :] = dv_new
        ctx_ref[...] = jnp.concatenate(outs, axis=0).T.astype(jnp.bfloat16)
        dq = jnp.concatenate(dqs, axis=0).T * 0.125
        dq_ref[...] = lane_turn(dq, cosq_ref[...], -sinq_ref[...]).astype(jnp.bfloat16)

    for blocks in range(1, 4):
        pl.when(i - kb + 1 == blocks)(partial(body, blocks))

    @pl.when(i == pl.num_programs(0) - 1)
    def _():
        dk_ref[...] = lane_turn(dk_acc[hp], cos_ref[...], -sin_ref[...]).astype(jnp.bfloat16)
        dv_ref[...] = dv_acc[hp].astype(jnp.bfloat16)


def attention(qkv, do, starts, cosines, sines):
    width = do.shape[1]
    pairs, steps = width // 128, SEQ // QB
    kb = starts[::QB] // QB
    last = steps - 1
    qspec = pl.BlockSpec((QB, 128), lambda i, h, kb: (i, h))
    kspec = pl.BlockSpec((SEQ, 128), lambda i, h, kb: (0, pairs + h))
    vspec = pl.BlockSpec((SEQ, 128), lambda i, h, kb: (0, 2 * pairs + h))
    outk = pl.BlockSpec((SEQ, 128), lambda i, h, kb: (0, jnp.where(i == last, h, 0)))
    shape = jax.ShapeDtypeStruct((SEQ, width), jnp.bfloat16)
    ctx, dq, dk, dv = pl.pallas_call(
        attn_kernel,
        grid_spec=pltpu.PrefetchScalarGridSpec(
            num_scalar_prefetch=1, grid=(steps, pairs),
            in_specs=[pl.BlockSpec((1, QB), lambda i, h, kb: (0, i)), qspec, kspec, vspec, qspec,
                      pl.BlockSpec((QB, 128), lambda i, h, kb: (i, 0)), pl.BlockSpec((QB, 128), lambda i, h, kb: (i, 0)),
                      pl.BlockSpec((SEQ, 128), lambda i, h, kb: (0, 0)), pl.BlockSpec((SEQ, 128), lambda i, h, kb: (0, 0))],
            out_specs=[qspec, qspec, outk, outk],
            scratch_shapes=[pltpu.VMEM((pairs, SEQ, 128), jnp.float32), pltpu.VMEM((pairs, SEQ, 128), jnp.float32),
                            pltpu.VMEM((3 * QB, QB), jnp.float32)]),
        out_shape=[shape] * 4,
        compiler_params=pltpu.CompilerParams(vmem_limit_bytes=63 << 20),
        cost_estimate=pl.CostEstimate(flops=30 << 30, bytes_accessed=16 << 20, transcendentals=8 << 20),
        name="attention",
    )(kb, starts[None], qkv, qkv, qkv, do, cosines, sines, cosines, sines)
    return ctx, (dq, dk, dv)


def lane_tables(positions):
    lanes = jnp.arange(128, dtype=jnp.int32) % HD
    exponents = (lanes // 2 * 2).astype(jnp.float32) / ROT
    angles = positions.astype(jnp.float32)[:, None] * jnp.power(10000.0, -exponents)
    turned = (lanes < ROT)[None]
    signs = jnp.where(lanes % 2 == 0, -1.0, 1.0)[None]
    return jnp.where(turned, jnp.cos(angles), 1.0), jnp.where(turned, jnp.sin(angles) * signs, 0.0)


def weight_block(ref):
    half = ref.shape[0] // 2
    rows = half * ref.shape[2]
    return jnp.concatenate(
        [ref[:half, 0].reshape(rows, 128), ref[half:, 0].reshape(rows, 128)], axis=1
    )


def qkv_kernel(x_ref, w_ref, cos_ref, sin_ref, o_ref):
    j = pl.program_id(0)
    out = mm(x_ref[...], weight_block(w_ref))

    @pl.when(j < 2)
    def _():
        cosines = jnp.concatenate([cos_ref[...]] * 2, axis=1)
        sines = jnp.concatenate([sin_ref[...]] * 2, axis=1)
        scale = jnp.where(j == 0, 0.125, 1.0)
        o_ref[...] = (lane_turn(out, cosines, sines).astype(jnp.bfloat16) * scale.astype(jnp.bfloat16))

    @pl.when(j == 2)
    def _():
        o_ref[...] = out.astype(jnp.bfloat16)


MESH_ID = pl.DeviceIdType.MESH
ZS, XS, YS, CS = 4, 2, 2, 2
G1_ROWS = 1024
G2_ROWS = 2064
SPLITS = ((0, 512), (512, 512))


def place_of(z, x, y, c):
    return (z * XS + x) * (YS * CS) + y * CS + c


def gather_kernel(x_ref, gain_ref, bias_ref, count_ref, g1_ref, grad_ref,
                  normed_ref, turned_ref, row_ref, grad_row, g1_out, counts_ref,
                  nv, tv, send_sem, recv_sem, own_sem, a2a_send, a2a_recv, row_sem, turn_sem, count_send, count_recv,
                  grad_send, grad_recv, grad_sem):
    dp, mp = lax.axis_index("dp"), lax.axis_index("mp")
    y, c, z, x = dp // CS, dp % CS, mp // XS, mp % XS
    members, own = ZS * XS, x_ref.shape[1]

    def device(z, x, y, c):
        return (y * CS + c, z * XS + x)

    barrier = pltpu.get_barrier_semaphore()
    others = [(dp, lax.rem(mp + k, members)) for k in range(1, members)]
    others += [(lax.rem(dp + k, YS * CS), mp) for k in range(1, YS * CS)]
    for other in others:
        pl.semaphore_signal(barrier, inc=1, device_id=other, device_id_type=MESH_ID)
    pl.semaphore_wait(barrier, len(others))

    copies = []

    def send(block, slot, piece, target, local=False):
        src, out = g1_ref, g1_out
        first, rows = SPLITS[block]
        spot = place_of(*piece)
        at = out.at[spot, pl.ds(first, rows)]
        copy = pltpu.make_async_remote_copy(
            src_ref=src.at[pl.ds(first, rows)] if local else at, dst_ref=at,
            send_sem=send_sem.at[block, slot], recv_sem=recv_sem.at[block, slot],
            device_id=device(*target), device_id_type=MESH_ID)
        copy.start()
        copies.append(copy)
        return copy

    recv = {}

    def hop(block, slot, piece, target, local=False):
        recv[block, slot] = send(block, slot, piece, target, local)

    flip = {"x": (z, 1 - x, y, c), "y": (z, x, 1 - y, c), "c": (z, x, y, 1 - c)}

    def orders(block):
        return ("x", "y") if block % 2 == 0 else ("y", "x")

    def begin(block):
        me = (z, x, y, c)
        for k in range(1, ZS):
            hop(block, k - 1, me, (lax.rem(z + k, ZS), x, y, c), True)
        one, two = orders(block)
        hop(block, 3, me, flip[one], True)
        hop(block, 7, me, flip[two], True)
        hop(block, 15, me, flip["c"], True)

    counts_ref[dp] = count_ref[...]
    count_copies = []
    for k in range(1, YS * CS):
        copy = pltpu.make_async_remote_copy(
            src_ref=count_ref, dst_ref=counts_ref.at[dp], send_sem=count_send.at[k], recv_sem=count_recv.at[k],
            device_id=(lax.rem(dp + k, YS * CS), mp), device_id_type=MESH_ID)
        copy.start()
        count_copies.append(copy)

    for block in range(2):
        begin(block)
    mine = pl.ds(pl.multiple_of(mp * own, own), own)
    grad_copies = []
    for k in range(1, members):
        row = lax.rem(mp + k, members)
        copy = pltpu.make_async_remote_copy(
            src_ref=grad_ref.at[row], dst_ref=grad_row.at[mine], send_sem=grad_send.at[k], recv_sem=grad_recv.at[k],
            device_id=(dp, row), device_id_type=MESH_ID)
        copy.start()
        grad_copies.append(copy)
    own_grad = pltpu.make_async_copy(grad_ref.at[mp], grad_row.at[mine], grad_sem.at[0])
    own_grad.start()
    me_spot = place_of(z, x, y, c)
    own_copies = [pltpu.make_async_copy(g1_ref, g1_out.at[me_spot], own_sem.at[0])]

    def normalise(k, carry):
        row = lax.rem(mp + k, members)
        value = x_ref[row].astype(jnp.float32)
        centred = value - jnp.mean(value, axis=-1, keepdims=True)
        inverse = lax.rsqrt(jnp.mean(centred * centred, axis=-1, keepdims=True) + EPSILON)
        nv[k] = (centred * inverse * gain_ref[...] + bias_ref[...]).astype(jnp.bfloat16)
        pltpu.make_async_copy(nv.at[k], normed_ref.at[row], row_sem.at[k]).start()
        return carry

    lax.fori_loop(0, members, normalise, 0)
    row_copies = []
    for k in range(1, members):
        row = lax.rem(mp + k, members)
        pltpu.make_async_copy(nv.at[k], normed_ref.at[row], row_sem.at[k]).wait()
        copy = pltpu.make_async_remote_copy(
            src_ref=normed_ref.at[row], dst_ref=row_ref.at[mine], send_sem=a2a_send.at[k], recv_sem=a2a_recv.at[k],
            device_id=(dp, row), device_id_type=MESH_ID)
        copy.start()
        row_copies.append(copy)
    pltpu.make_async_copy(nv.at[0], normed_ref.at[mp], row_sem.at[0]).wait()
    own_row = pltpu.make_async_copy(nv.at[0], row_ref.at[mine], row_sem.at[0])
    own_row.start()
    for copy in own_copies:
        copy.start()

    def turn(k, carry):
        row = lax.rem(mp + k, members)
        tv[:, pl.ds(pl.multiple_of(row * own, own), own)] = nv[k].T
        return carry

    lax.fori_loop(0, members, turn, 0)
    width = tv.shape[0] // (YS * CS)
    turn_copies = []
    for rel in range(YS * CS):
        yr, cr = rel % YS, rel // YS
        from_block = lax.rem(y + yr, YS) * CS + lax.rem(c + cr, CS)
        copy = pltpu.make_async_copy(
            tv.at[pl.ds(pl.multiple_of(from_block * width, width), width)], turned_ref.at[rel], turn_sem.at[rel])
        copy.start()
        turn_copies.append(copy)

    for blocks in ((0, 1),):
        for kz in range(1, ZS):
            for block in blocks:
                one, two = orders(block)
                recv[block, kz - 1].wait_recv()
                piece = (lax.rem(z + ZS - kz, ZS), x, y, c)
                hop(block, 3 + kz, piece, flip[one])
                hop(block, 7 + kz, piece, flip[two])
                hop(block, 15 + kz, piece, flip["c"])
        for kz in range(ZS):
            for block in blocks:
                one, two = orders(block)
                recv[block, 3 + kz].wait_recv()
                zz = lax.rem(z + ZS - kz, ZS)
                piece = (zz, 1 - x, y, c) if one == "x" else (zz, x, 1 - y, c)
                hop(block, 11 + kz, piece, flip[two])
                hop(block, 19 + kz, piece, flip["c"])
        for half in range(2):
            for kz in range(ZS):
                for block in blocks:
                    one, two = orders(block)
                    recv[block, 7 + half * ZS + kz].wait_recv()
                    zz = lax.rem(z + ZS - kz, ZS)
                    if half == 0:
                        piece = (zz, x, 1 - y, c) if two == "y" else (zz, 1 - x, y, c)
                    else:
                        piece = (zz, 1 - x, 1 - y, c)
                    hop(block, 23 + half * ZS + kz, piece, flip["c"])
    for block in range(2):
        for slot in range(15, 31):
            recv[block, slot].wait_recv()
    for copy in copies:
        copy.wait_send()
    for copy in own_copies + turn_copies:
        copy.wait()
    own_row.wait()
    own_grad.wait()
    for copy in row_copies + grad_copies + count_copies:
        copy.wait()


def gather_all(inputs, ln_gain, ln_bias, counts, g1, out_grad):
    rows, own, width = inputs.shape
    places = ZS * XS * YS * CS
    any_space = pl.BlockSpec(memory_space=pl.ANY)
    vmem = pl.BlockSpec(memory_space=pltpu.VMEM)
    shape = jax.ShapeDtypeStruct
    half = jnp.bfloat16
    dma = pltpu.SemaphoreType.DMA
    return pl.pallas_call(
        gather_kernel,
        in_specs=[vmem, vmem, vmem, vmem, any_space, any_space],
        out_specs=[pl.BlockSpec(memory_space=pltpu.HBM)] * 5 + [vmem],
        out_shape=[
            shape((rows, own, width), half),
            shape((YS * CS, width // (YS * CS), rows * own), half),
            shape((rows * own, width), half),
            shape((rows * own, width), half),
            shape((places,) + g1.shape, half),
            shape((YS * CS, 8, 128), jnp.float32),
        ],
        scratch_shapes=[
            pltpu.VMEM((rows, own, width), half), pltpu.VMEM((width, rows * own), half),
            dma((2, 31)), dma((2, 31)), dma((1,)), dma((rows,)), dma((rows,)), dma((rows,)), dma((YS * CS,)),
            dma((YS * CS,)), dma((YS * CS,)), dma((rows,)), dma((rows,)), dma((1,)),
        ],
        compiler_params=pltpu.CompilerParams(collective_id=0, has_side_effects=True, vmem_limit_bytes=63 << 20),
        name="gather_weights",
    )(inputs, ln_gain[None], ln_bias[None], counts, g1, out_grad)


PLACES = ZS * XS * YS * CS
PIECE = 256


def relative(dp, rel):
    return lax.rem(dp // CS + rel % YS, YS) * CS + lax.rem(dp % CS + rel // YS, CS)


def wide(ref, at, first, rows, count):
    return jnp.concatenate(
        [ref[at + (slice(first + b * rows, first + (b + 1) * rows),)] for b in range(count)], axis=-1
    )


def cotangent_kernel(place_ref, grad_ref, row_ref, weight_ref, piece_ref, branch_ref, turned_ref, row_turned_ref, ctx_ref,
                     w_ref, sum_ref):
    branch = (grad_ref[...].astype(jnp.float32) * weight_ref[...]).astype(jnp.bfloat16)
    branch_ref[...] = branch
    sum_ref[...] = jnp.sum(branch.astype(jnp.float32), axis=0, keepdims=True)
    for b in range(D // 128):
        w_ref[:, b * 128:(b + 1) * 128] = piece_ref[:, 0, b * 32:(b + 1) * 32, :].reshape(D, 128)
    branch_row = (row_ref[...].astype(jnp.float32) * weight_ref[...]).astype(jnp.bfloat16)
    ctx_ref[...] = mm(branch_row, w_ref[...], NT).astype(jnp.bfloat16)
    for rel in range(YS * CS):
        block = pl.ds(pl.multiple_of(relative(place_ref[0], rel) * PIECE, PIECE), PIECE)
        turned_ref[rel] = branch_ref[:, block].T
        row_turned_ref[rel] = (row_ref[:, block].astype(jnp.float32) * weight_ref[...]).astype(jnp.bfloat16).T


def cotangent(place, out_grad, grad_row, weight, g1):
    tokens = out_grad.shape[0]
    half = jnp.bfloat16
    shape = jax.ShapeDtypeStruct
    whole = lambda *dims: pl.BlockSpec(dims, lambda i, p: (0,) * len(dims), pipeline_mode=pl.Buffered(1))
    return pl.pallas_call(
        cotangent_kernel,
        grid_spec=pltpu.PrefetchScalarGridSpec(
            num_scalar_prefetch=1, grid=(1,),
            in_specs=[whole(tokens, D), whole(tokens, D), whole(1, 1),
                      pl.BlockSpec((PLACES, 1, 256, 128), lambda i, p: (0, 3, 0, 0))],
            out_specs=[whole(tokens, D), whole(4, PIECE, tokens), whole(4, PIECE, tokens), whole(tokens, D), whole(D, D),
                       whole(1, D)]),
        out_shape=[shape((tokens, D), half), shape((4, PIECE, tokens), half), shape((4, PIECE, tokens), half),
                   shape((tokens, D), half), shape((D, D), half), shape((1, D), jnp.float32)],
        compiler_params=pltpu.CompilerParams(vmem_limit_bytes=63 << 20),
        cost_estimate=pl.CostEstimate(flops=2 << 30, bytes_accessed=18 << 20, transcendentals=0),
        name="cotangent",
    )(place, out_grad, grad_row, weight, g1.reshape(PLACES, 4, 256, 128))


def project(rows, g1, cosines, sines):
    return pl.pallas_call(
        qkv_kernel,
        grid=(3, ZS),
        in_specs=[
            pl.BlockSpec((SEQ, D), lambda j, c: (0, 0)),
            pl.BlockSpec((8, 1, 256, 128), lambda j, c: (c, j, 0, 0)),
            pl.BlockSpec((SEQ, 128), lambda j, c: (0, 0)),
            pl.BlockSpec((SEQ, 128), lambda j, c: (0, 0)),
        ],
        out_specs=pl.BlockSpec((SEQ, 256), lambda j, c: (0, j * ZS + c)),
        out_shape=jax.ShapeDtypeStruct((SEQ, 3 * D), jnp.bfloat16),
        compiler_params=pltpu.CompilerParams(vmem_limit_bytes=63 << 20),
        cost_estimate=pl.CostEstimate(flops=6 << 30, bytes_accessed=14 << 20, transcendentals=0),
        name="qkv",
    )(rows, g1.reshape(PLACES, 4, 256, 128), cosines, sines)


def put_tiles(values, keep_ref, send_ref):
    for xr in range(XS):
        for yr in range(YS):
            keep_ref[yr, xr, 0] = values[xr][yr * PIECE:(yr + 1) * PIECE]
            send_ref[yr, xr, 0] = values[xr][(YS + yr) * PIECE:(YS + yr + 1) * PIECE]


def tile_specs(n, index):
    spec = pl.BlockSpec((YS, XS, 1, PIECE, n), index)
    return [spec, spec]


def tile_shapes(n):
    shape = jax.ShapeDtypeStruct((YS, XS, ZS, PIECE, n), jnp.bfloat16)
    return [shape, shape]


def by_x(value):
    return [value[:, :128], value[:, 128:]]


def back_kernel(place_ref, x_ref, w_ref, dq_ref, dk_ref, dv_ref, n_ref, keep_ref, send_ref, xt_ref, acc_ref):
    step = pl.program_id(0)

    @pl.when(step == 0)
    def _():
        for rel in range(YS * CS):
            block = relative(place_ref[0], rel)
            xt_ref[rel * PIECE:(rel + 1) * PIECE] = x_ref[:, pl.ds(pl.multiple_of(block * PIECE, PIECE), PIECE)].T
        acc_ref[...] = jnp.zeros_like(acc_ref)

    total = acc_ref[...]
    for j, d_ref in enumerate((dq_ref, dk_ref, dv_ref)):
        d = d_ref[...]
        total = total + mm(d, weight_block(w_ref.at[:, j:j + 1]), NT)
        values = by_x(mm(xt_ref[...], d).astype(jnp.bfloat16))
        lanes = pl.ds(j * 128, 128)
        put_tiles(values, keep_ref.at[..., lanes], send_ref.at[..., lanes])
    acc_ref[...] = total

    @pl.when(step == pl.num_programs(0) - 1)
    def _():
        n_ref[...] = acc_ref[...].astype(jnp.bfloat16)


def back(place, rows, g1, grads):
    return pl.pallas_call(
        back_kernel,
        grid_spec=pltpu.PrefetchScalarGridSpec(
            num_scalar_prefetch=1, grid=(ZS,),
            in_specs=[
                pl.BlockSpec((SEQ, D), lambda k, p: (0, 0), pipeline_mode=pl.Buffered(1)),
                pl.BlockSpec((8, 3, 256, 128), lambda k, p: (k, 0, 0, 0)),
            ]
            + [pl.BlockSpec((SEQ, 256), lambda k, p: (0, k))] * 3,
            out_specs=[pl.BlockSpec((SEQ, D), lambda k, p: (0, 0), pipeline_mode=pl.Buffered(1))]
            + tile_specs(384, lambda k, p: (0, 0, k, 0, 0)),
            scratch_shapes=[pltpu.VMEM((D, SEQ), jnp.bfloat16), pltpu.VMEM((SEQ, D), jnp.float32)]),
        out_shape=[jax.ShapeDtypeStruct((SEQ, D), jnp.bfloat16)] + tile_shapes(384),
        compiler_params=pltpu.CompilerParams(vmem_limit_bytes=63 << 20),
        cost_estimate=pl.CostEstimate(flops=12 << 30, bytes_accessed=22 << 20, transcendentals=0),
        name="attention_back",
    )(place, rows, g1.reshape(PLACES, 4, 256, 128), *grads)


HALF_PIECE = PIECE // 2
Z_ORDER = (2, 1, 3, 0)
BAND = 16


class Reduction:
    def __init__(self, keeps, sends, bufs):
        self.keeps, self.sends = keeps, sends
        (self.own, self.got, self.first, self.second, self.last, self.own_sem, self.core_send, self.core_recv,
         self.first_send, self.first_recv, self.second_send, self.second_recv, self.last_send, self.last_recv) = bufs
        dp, mp = lax.axis_index("dp"), lax.axis_index("mp")
        y, c, z, x = dp // CS, dp % CS, mp // XS, mp % XS
        self.x, self.z = x, z
        device = lambda z, x, y, c: (y * CS + c, z * XS + x)
        self.partner = device(z, x, y, 1 - c)
        self.axes = (device(z, 1 - x, y, c), device(z, x, 1 - y, c))
        self.line = [device(lax.rem(z + k, ZS), x, y, c) for k in range(ZS)]
        self.peers = [self.partner, *self.axes, *self.line[1:]]

    def parts(self):
        at = 0
        for s, ref in enumerate(self.keeps):
            for i in range(XS):
                yield s, i, pl.ds(at, ref.shape[-1])
            at += ref.shape[-1]

    def mine(self, s, i, k, lanes):
        return pltpu.make_async_copy(
            self.keeps[s].at[:, lax.rem(self.x + i, XS), lax.rem(self.z + k, ZS)], self.own.at[k, i, :, :, lanes],
            self.own_sem.at[s, i, k])

    def core(self, s, i, k, lanes):
        return pltpu.make_async_remote_copy(
            src_ref=self.sends[s].at[:, lax.rem(self.x + i, XS), lax.rem(self.z + k, ZS)],
            dst_ref=self.got.at[k, i, :, :, lanes],
            send_sem=self.core_send.at[s, i, k], recv_sem=self.core_recv.at[s, i, k],
            device_id=self.partner, device_id_type=MESH_ID)

    def load(self):
        for k in Z_ORDER:
            for s, i, lanes in self.parts():
                self.mine(s, i, k, lanes).start()

    def begin(self):
        for k in Z_ORDER:
            for s, i, lanes in self.parts():
                self.core(s, i, k, lanes).start()

    def half_of(self, ref, k, half, away, other):
        yy, xx = (other, away) if half == 0 else (away, other)
        return ref.at[k, xx, yy, pl.ds(half * HALF_PIECE, HALF_PIECE)]

    def one(self, k, half, other):
        return pltpu.make_async_remote_copy(
            src_ref=self.half_of(self.own, k, half, 1, other), dst_ref=self.first.at[k, half, other],
            send_sem=self.first_send.at[k, half, other], recv_sem=self.first_recv.at[k, half, other],
            device_id=self.axes[half], device_id_type=MESH_ID)

    def two(self, k, half):
        return pltpu.make_async_remote_copy(
            src_ref=self.half_of(self.own, k, half, 0, 1), dst_ref=self.second.at[k, half],
            send_sem=self.second_send.at[k, half], recv_sem=self.second_recv.at[k, half],
            device_id=self.axes[1 - half], device_id_type=MESH_ID)

    def three(self, k, half):
        return pltpu.make_async_remote_copy(
            src_ref=self.half_of(self.own, k, half, 0, 0), dst_ref=self.last.at[k, half],
            send_sem=self.last_send.at[k, half], recv_sem=self.last_recv.at[k, half],
            device_id=self.line[k], device_id_type=MESH_ID)

    def add(self, refs, write):
        def body(i, carry):
            band = pl.ds(pl.multiple_of(i * BAND, BAND), BAND)
            value = refs[0][band].astype(jnp.float32)
            for ref in refs[1:]:
                value = value + ref[band].astype(jnp.float32)
            write(band, value)
            return carry

        lax.fori_loop(0, HALF_PIECE // BAND, body, 0)

    def store(self, k, half, away, other, *extra):
        own = self.half_of(self.own, k, half, away, other)

        def write(band, value):
            own[band] = value.astype(jnp.bfloat16)

        self.add((own, self.half_of(self.got, k, half, away, other), *extra), write)

    def stage_one(self, k):
        for s, i, lanes in self.parts():
            self.mine(s, i, k, lanes).wait()
            self.core(s, i, k, lanes).wait_recv()
        for other in (1, 0):
            for half in range(2):
                self.store(k, half, 1, other)
                self.one(k, half, other).start()

    def stage_two(self, k):
        for half in range(2):
            self.one(k, half, 1).wait_recv()
            self.store(k, half, 0, 1, self.first.at[k, half, 1])
            self.two(k, half).start()

    def stage_three(self, k):
        for half in range(2):
            self.one(k, half, 0).wait_recv()
            self.two(k, half).wait_recv()
            if k:
                self.store(k, half, 0, 0, self.first.at[k, half, 0], self.second.at[k, half])
                self.three(k, half).start()

    def finish(self, out_ref):
        self.stage_three(0)
        for half in range(2):
            for k in range(1, ZS):
                self.three(k, half).wait_recv()
            out = out_ref.at[pl.ds(half * HALF_PIECE, HALF_PIECE)]

            def write(band, value):
                out[band] = value

            self.add(
                [self.half_of(self.own, 0, half, 0, 0), self.half_of(self.got, 0, half, 0, 0), self.first.at[0, half, 0],
                 self.second.at[0, half]] + [self.last.at[k, half] for k in range(1, ZS)], write)
        for k in range(ZS):
            for s, i, lanes in self.parts():
                self.core(s, i, k, lanes).wait_send()
            for half in range(2):
                for other in range(2):
                    self.one(k, half, other).wait_send()
                self.two(k, half).wait_send()
                if k:
                    self.three(k, half).wait_send()


def greet(others):
    barrier = pltpu.get_barrier_semaphore()
    for other in others:
        pl.semaphore_signal(barrier, inc=1, device_id=other, device_id_type=MESH_ID)
    pl.semaphore_wait(barrier, len(others))


def reduction_scratch(sets, width):
    half, dma = jnp.bfloat16, pltpu.SemaphoreType.DMA
    tiles = pltpu.VMEM((ZS, XS, YS, PIECE, width), half)
    lines = pltpu.VMEM((ZS, 2, HALF_PIECE, width), half)
    return [tiles, tiles, pltpu.VMEM((ZS, 2, 2, HALF_PIECE, width), half), lines, lines,
            dma((sets, XS, ZS)), dma((sets, XS, ZS)), dma((sets, XS, ZS)), dma((ZS, 2, 2)), dma((ZS, 2, 2)),
            dma((ZS, 2)), dma((ZS, 2)), dma((ZS, 2)), dma((ZS, 2))]


REDUCTION_REFS = 14


def reduce_kernel(sets, *refs):
    keeps, sends, small_ref = refs[:sets], refs[sets:2 * sets], refs[2 * sets]
    out_ref, small_out = refs[2 * sets + 1:2 * sets + 3]
    small_got, small_send, small_recv, small_sem = refs[2 * sets + 3 + REDUCTION_REFS:]
    work = Reduction(keeps, sends, refs[2 * sets + 3:2 * sets + 3 + REDUCTION_REFS])
    dp, mp = lax.axis_index("dp"), lax.axis_index("mp")
    groups, members = YS * CS, ZS * XS
    everyone = [(lax.rem(dp + a, groups), lax.rem(mp + b, members))
                for a in range(groups) for b in range(members) if (a, b) != (0, 0)]
    work.load()
    greet(everyone)
    work.begin()
    small_local = pltpu.make_async_copy(small_ref.at[dp * members + mp], small_got.at[0], small_sem.at[0])
    small_local.start()
    small_copies = []
    for i, (a, b) in enumerate(everyone):
        copy = pltpu.make_async_remote_copy(
            src_ref=small_ref.at[a * members + b], dst_ref=small_got.at[i + 1], send_sem=small_send.at[i],
            recv_sem=small_recv.at[i], device_id=(a, b), device_id_type=MESH_ID)
        copy.start()
        small_copies.append(copy)
    order = Z_ORDER
    work.stage_one(order[0])
    work.stage_one(order[1])
    work.stage_two(order[0])
    work.stage_one(order[2])
    work.stage_three(order[0])
    work.stage_two(order[1])
    work.stage_one(order[3])
    work.stage_three(order[1])
    work.stage_two(order[2])
    work.stage_three(order[2])
    work.stage_two(order[3])
    small_local.wait()
    for copy in small_copies:
        copy.wait_recv()
    summed = small_got[0]
    for i in range(1, PLACES):
        summed = summed + small_got[i]
    small_out[...] = summed
    work.finish(out_ref)
    for copy in small_copies:
        copy.wait_send()


def reduce_tiles(keeps, sends, small):
    width, sets = sum(keep.shape[-1] for keep in keeps), len(keeps)
    any_space, vmem = pl.BlockSpec(memory_space=pl.ANY), pl.BlockSpec(memory_space=pltpu.VMEM)
    dma = pltpu.SemaphoreType.DMA
    return pl.pallas_call(
        partial(reduce_kernel, sets),
        in_specs=[any_space] * (2 * sets + 1),
        out_specs=[vmem, vmem],
        out_shape=[jax.ShapeDtypeStruct((PIECE, width), jnp.float32), jax.ShapeDtypeStruct((8, 128), jnp.float32)],
        scratch_shapes=reduction_scratch(sets, width) + [
            pltpu.VMEM((PLACES, 8, 128), jnp.float32), dma((PLACES,)), dma((PLACES,)), dma((1,))],
        compiler_params=pltpu.CompilerParams(collective_id=1, has_side_effects=True, vmem_limit_bytes=63 << 20),
        name="reduce_tiles",
    )(*keeps, *sends, small)


C0 = math.sqrt(2.0 / math.pi)


def mlp_kernel(sets, x_ref, xt_ref, g_ref, gt_ref, wa_ref, wb_ref, *refs):
    out_ref, dn_ref, keep_ref, send_ref, bsum_ref, sum_ref = refs[2 * sets:2 * sets + 6]
    work = Reduction(refs[:sets], refs[sets:2 * sets], refs[2 * sets + 6:])
    step = pl.program_id(0)
    order = Z_ORDER

    @pl.when(step == 0)
    def _():
        work.load()
        greet(work.peers)
        work.begin()
        out_ref[...] = jnp.zeros_like(out_ref)
        dn_ref[...] = jnp.zeros_like(dn_ref)

    def stages(at, *calls):
        @pl.when(step == at)
        def _():
            for stage, i in calls:
                stage(order[i])

    one, two, three = work.stage_one, work.stage_two, work.stage_three
    stages(1, (one, 1), (one, 2))
    stages(2, (two, 1))
    stages(3, (two, 3), (three, 1))
    w_in = jnp.concatenate([wide(r, (0, p, 0), 0, 128, 8) for r in (wa_ref, wb_ref) for p in range(CS)], axis=0)
    w_out = jnp.concatenate([wide(r, (0, p, 0), 1024, 128, 8) for r in (wa_ref, wb_ref) for p in range(CS)], axis=0)
    bias = jnp.concatenate([r[0, p, 0, 2048:2049] for r in (wa_ref, wb_ref) for p in range(CS)], axis=1)
    x = mm(x_ref[...], w_in, NT) + bias.astype(jnp.float32)
    squared = x * x
    tanh = jnp.tanh(C0 * x * (1.0 + 0.044715 * squared))
    half = 0.5 * (1.0 + tanh)
    act = (x * half).astype(jnp.bfloat16)
    slope = half + 0.5 * x * (1.0 - tanh * tanh) * (C0 * (1.0 + 3 * 0.044715 * squared))
    hid = (mm(g_ref[...], w_out, NT) * slope).astype(jnp.bfloat16)
    stages(0, (one, 0))
    stages(1, (two, 0), (one, 3))
    stages(2, (three, 0), (two, 2))
    stages(3, (three, 2))
    out_ref[...] += mm(act, w_out)
    dn_ref[...] += mm(hid, w_in)
    bsum_ref[0] = jnp.sum(hid.astype(jnp.float32), axis=0, keepdims=True)
    out_part = mm(gt_ref[...], act).astype(jnp.bfloat16)
    in_part = mm(xt_ref[...], hid).astype(jnp.bfloat16)
    put_tiles(
        [jnp.concatenate([out_part[:, a * 256:(a + 1) * 256], in_part[:, a * 256:(a + 1) * 256]], axis=1)
         for a in range(XS)], keep_ref, send_ref)

    @pl.when(step == pl.num_programs(0) - 1)
    def _():
        work.finish(sum_ref)


def mlp_half(h, normed, normed_turned, branch, branch_turned, g2, keeps, sends):
    tokens, sets, width = normed.shape[0], len(keeps), sum(keep.shape[-1] for keep in keeps)
    one = lambda *dims: pl.BlockSpec(dims, lambda k: (0,) * len(dims), pipeline_mode=pl.Buffered(1))
    weight = lambda x: pl.BlockSpec((1, CS, 1, G2_ROWS, 128), lambda k: (h, 0, k * XS + x, 0, 0))
    views = g2.reshape(YS, CS, ZS * XS, G2_ROWS, 128)
    full = jax.ShapeDtypeStruct((tokens, D), jnp.float32)
    return pl.pallas_call(
        partial(mlp_kernel, sets),
        grid=(ZS,),
        in_specs=[one(tokens, D), one(D, tokens), one(tokens, D), one(D, tokens), weight(0), weight(1)]
        + [pl.BlockSpec(memory_space=pl.ANY)] * (2 * sets),
        out_specs=[one(tokens, D), one(tokens, D)] + tile_specs(512, lambda k: (0, 0, k, 0, 0))
        + [pl.BlockSpec((1, 1, 512), lambda k: (k, 0, 0)), one(PIECE, width)],
        scratch_shapes=reduction_scratch(sets, width),
        out_shape=[full, full] + tile_shapes(512)
        + [jax.ShapeDtypeStruct((ZS, 1, 512), jnp.float32), jax.ShapeDtypeStruct((PIECE, width), jnp.float32)],
        compiler_params=pltpu.CompilerParams(collective_id=2 + h, has_side_effects=True, vmem_limit_bytes=63 << 20),
        cost_estimate=pl.CostEstimate(flops=26 << 30, bytes_accessed=30 << 20, transcendentals=2 << 20),
        name="mlp",
    )(normed, normed_turned.reshape(D, tokens), branch, branch_turned.reshape(D, tokens), views, views, *keeps, *sends)


def output_kernel(ctx_ref, w_ref, gt_ref, out_ref, keep_ref, send_ref, acc_ref):
    step = pl.program_id(0)
    ctx = ctx_ref[...]

    @pl.when(step == 0)
    def _():
        acc_ref[...] = jnp.zeros_like(acc_ref)

    acc_ref[...] += mm(ctx, w_ref[...])
    put_tiles(by_x(mm(gt_ref[...], ctx).astype(jnp.bfloat16)), keep_ref, send_ref)

    @pl.when(step == pl.num_programs(0) - 1)
    def _():
        out_ref[...] = acc_ref[...].astype(jnp.bfloat16)


def row_output(context, w_output, branch_turned):
    tokens = context.shape[0]
    whole = lambda *dims: pl.BlockSpec(dims, lambda k: (0,) * len(dims), pipeline_mode=pl.Buffered(1))
    return pl.pallas_call(
        output_kernel,
        grid=(ZS,),
        in_specs=[
            pl.BlockSpec((tokens, 256), lambda k: (0, k)),
            pl.BlockSpec((256, D), lambda k: (k, 0)),
            whole(D, tokens),
        ],
        out_specs=[whole(tokens, D)] + tile_specs(128, lambda k: (0, 0, k, 0, 0)),
        scratch_shapes=[pltpu.VMEM((tokens, D), jnp.float32)],
        out_shape=[jax.ShapeDtypeStruct((tokens, D), jnp.bfloat16)] + tile_shapes(128),
        compiler_params=pltpu.CompilerParams(vmem_limit_bytes=63 << 20),
        cost_estimate=pl.CostEstimate(flops=4 << 30, bytes_accessed=12 << 20, transcendentals=0),
        name="row_output",
    )(context, w_output, branch_turned.reshape(D, tokens))


def norm_back_kernel(x_ref, g_ref, a_ref, m0_ref, m1_ref, ao_ref, mo0_ref, mo1_ref, gain_ref, bo_ref, weight_ref, out_ref, layer_ref, sums_ref):
    x = x_ref[...].astype(jnp.float32)
    layer = x + bo_ref[...].astype(jnp.float32) + ao_ref[...].astype(jnp.float32) + (mo0_ref[...] + mo1_ref[...])
    layer_ref[...] = layer.astype(jnp.bfloat16)
    centred = x - jnp.mean(x, axis=-1, keepdims=True)
    inverse = lax.rsqrt(jnp.mean(centred * centred, axis=-1, keepdims=True) + EPSILON)
    standard = centred * inverse
    grad = a_ref[...].astype(jnp.float32) + (m0_ref[...] + m1_ref[...])
    scaled = grad * gain_ref[...]
    part = inverse * (
        scaled
        - jnp.mean(scaled, axis=-1, keepdims=True)
        - standard * jnp.mean(scaled * standard, axis=-1, keepdims=True)
    )
    out_ref[...] = (g_ref[...].astype(jnp.float32) * weight_ref[...] + part).astype(jnp.bfloat16)
    sums = jnp.concatenate(
        [jnp.sum(grad * standard, axis=0, keepdims=True), jnp.sum(grad, axis=0, keepdims=True)], axis=0)

    @pl.when(pl.program_id(0) == 0)
    def _():
        sums_ref[...] = sums

    @pl.when(pl.program_id(0) > 0)
    def _():
        sums_ref[...] += sums


def norm_back(inputs, out_grad, attn_grad, mlp_grads, attn_out, mlp_outs, ln_gain, b_out, weight):
    tokens = inputs.shape[0]
    block = pl.BlockSpec((128, D), lambda i: (i, 0))
    row = pl.BlockSpec((1, D), lambda i: (0, 0))
    shape = jax.ShapeDtypeStruct((tokens, D), jnp.bfloat16)
    return pl.pallas_call(
        norm_back_kernel,
        grid=(tokens // 128,),
        in_specs=[block] * 8 + [row, row, pl.BlockSpec((1, 1), lambda i: (0, 0))],
        out_specs=[block, block, pl.BlockSpec((2, D), lambda i: (0, 0))],
        out_shape=[shape, shape, jax.ShapeDtypeStruct((2, D), jnp.float32)],
        cost_estimate=pl.CostEstimate(flops=20 << 20, bytes_accessed=20 << 20, transcendentals=0),
        name="norm_back",
    )(inputs, out_grad, attn_grad, *mlp_grads, attn_out, *mlp_outs, ln_gain[None], b_out[None], weight)


def on_device_rows(
    inputs,
    seg_lengths,
    group_counts,
    out_grad,
    ln_gain,
    ln_bias,
    w_query,
    w_key,
    w_value,
    w_output,
    w_in,
    b_in,
    w_out,
    b_out,
):
    row_count, own_tokens = inputs.shape[0], inputs.shape[1]
    tokens = row_count * own_tokens
    group, member = lax.axis_index("dp"), lax.axis_index("mp")
    place = jnp.stack([group, member]).astype(jnp.int32)

    def quarter(matrix, axis):
        size = matrix.shape[axis] // (YS * CS)
        return lax.dynamic_slice_in_dim(matrix, group * size, size, axis)

    def narrow(matrix):
        return matrix.reshape(matrix.shape[0], D // 128, 128).transpose(1, 0, 2).reshape(-1, 128)

    def exchange(tensor):
        blocks = tensor.reshape(row_count, own_tokens, D)
        return lax.all_to_all(blocks, "mp", 0, 0, tiled=True).reshape(tokens, D)

    counts = jnp.broadcast_to(group_counts.astype(jnp.float32)[:, None], (8, 128))
    g1 = jnp.concatenate(
        [quarter(w_query, 0), quarter(w_key, 0), quarter(w_value, 0), narrow(quarter(w_output, 0))], axis=0)
    bias_rows = jnp.pad(quarter(b_in, 0)[None], ((0, G2_ROWS - 2049), (0, 0)))
    g2 = jnp.concatenate([narrow(quarter(w_in, 0)), narrow(quarter(w_out, 0)), bias_rows], axis=0)
    normed, normed_turned, normed_row, grad_row, g1_all, counts_all = gather_all(
        inputs, ln_gain, ln_bias, counts, g1, out_grad)
    g2, normed_row = lax.optimization_barrier((g2, normed_row))
    g2_all = lax.all_gather(g2, ("dp", "mp"))
    normed = normed.reshape(tokens, D)
    weight = (YS * CS * counts_all[group, 0, 0] / jnp.sum(counts_all[:, 0, 0])).reshape(1, 1)

    flat_grad = out_grad.reshape(tokens, D)
    branch, branch_turned, row_turned, ctx_grad_row, w_output_all, out_sum = cotangent(
        place, flat_grad, grad_row, weight, g1_all)
    own_row = lax.dynamic_index_in_dim(seg_lengths, member, 0, keepdims=True)
    _, positions = segment_layout(own_row)
    positions = positions[0]
    cosines, sines = lane_tables(positions)
    starts = jnp.arange(SEQ, dtype=jnp.int32) - positions
    qkv = project(normed_row, g1_all, cosines, sines)
    context_row, qkv_grad = attention(qkv, ctx_grad_row, starts, cosines, sines)
    out_row, keep_o, send_o = row_output(context_row, w_output_all, row_turned)
    attn_out = exchange(out_row)
    normed_row_grad, keep_a, send_a = back(place, normed_row, g1_all, qkv_grad)
    out0, grad0, keep0, send0, bsum0, grads_a = mlp_half(
        0, normed, normed_turned, branch, branch_turned, g2_all, (keep_a, keep_o), (send_a, send_o))
    normed_row_grad, keep0 = lax.optimization_barrier((normed_row_grad, keep0))
    attn_grad = exchange(normed_row_grad)
    out1, grad1, keep1, send1, bsum1, grads0 = mlp_half(
        1, normed, normed_turned, branch, branch_turned, g2_all, (keep0,), (send0,))
    input_grad, layer_out, sums = norm_back(
        inputs.reshape(tokens, D), flat_grad, attn_grad, (grad0, grad1), attn_out, (out0, out1), ln_gain, b_out, weight)

    bsums = jnp.stack([bsum0, bsum1]).reshape(YS, ZS * XS, CS, 128)
    bsums = bsums.transpose(1, 0, 2, 3).reshape(ZS * XS, 4, 128)
    own = D // PLACES
    vectors = jnp.concatenate([sums, out_sum], axis=0).reshape(3, PLACES, own).transpose(1, 0, 2)
    vectors = jnp.pad(vectors, ((0, 0), (0, 1), (0, 128 - own)))
    small = jnp.concatenate([jnp.tile(bsums, (YS * CS, 1, 1)), vectors], axis=1)
    grads1, small = reduce_tiles((keep1,), (send1,), small)
    shape = (row_count, own_tokens, D)
    return (
        layer_out.reshape(shape),
        input_grad.reshape(shape),
        small[4, :own],
        small[5, :own],
        grads_a[:, :128],
        grads_a[:, 128:256],
        grads_a[:, 256:384],
        grads_a[:, 384:].T,
        jnp.concatenate([grads0[:, 256:], grads1[:, 256:]], axis=1).T,
        small[:4].reshape(512),
        jnp.concatenate([grads0[:, :256], grads1[:, :256]], axis=1).T,
        small[6, :own],
    )


def solution(mesh):
    placed = (
        P("dp", "mp", None),
        P("dp", None),
        P("dp"),
        P("dp", "mp", None),
        P(),
        P(),
        P(None, "mp"),
        P(None, "mp"),
        P(None, "mp"),
        P("mp", None),
        P("mp", None),
        P("mp"),
        P("mp", None),
        P(),
    )
    sizes = (mesh.shape["dp"], mesh.shape["mp"])

    def on_device(*args):
        if sizes == (YS * CS, ZS * XS) and args[0].shape[0] == ZS * XS:
            return on_device_rows(*args)
        return on_device_gathered(*args)

    return jax.shard_map(
        on_device,
        mesh=mesh,
        in_specs=placed,
        out_specs=(
            P("dp", "mp", None),
            P("dp", "mp", None),
            P(("dp", "mp")),
            P(("dp", "mp")),
            P("dp", "mp"),
            P("dp", "mp"),
            P("dp", "mp"),
            P("mp", "dp"),
            P("mp", "dp"),
            P("mp"),
            P("mp", "dp"),
            P(("dp", "mp")),
        ),
        check_vma=False,
    )
```

```python
from functools import partial
import math
import jax
import jax.numpy as jnp
from jax import lax
from jax.sharding import PartitionSpec as P
from jax.experimental import pallas as pl
from jax.experimental.pallas import tpu as pltpu


D = 1024
HD = 64
ROT = 32
SEQ = 1024


EPSILON = 1e-05


def segment_layout(seg_lengths):
    seg_ends = jnp.cumsum(seg_lengths, axis=-1)
    seg_starts = seg_ends - seg_lengths
    places = jnp.arange(SEQ, dtype=jnp.int32)
    passed = places[None, :, None] >= seg_ends[:, None, :]
    seg_ids = jnp.sum(passed.astype(jnp.int32), axis=-1)
    inside = (places[None, :, None] >= seg_starts[:, None, :]) & jnp.logical_not(passed)
    begins = jnp.sum(jnp.where(inside, seg_starts[:, None, :], 0), axis=-1)
    return (seg_ids, places[None, :] - begins)


def rotary_tables(positions):
    exponents = jnp.arange(0, ROT, 2, dtype=jnp.float32) / ROT
    freqs = jnp.power(10000.0, -exponents)
    angles = positions.astype(jnp.float32)[..., None] * freqs
    return (jnp.cos(angles)[..., None, :], jnp.sin(angles)[..., None, :])


def turn_pairs(tensor, cosines, sines):
    rotary = tensor[..., :ROT]
    passive = tensor[..., ROT:]
    paired = rotary.reshape(rotary.shape[:-1] + (ROT // 2, 2))
    evens = paired[..., 0]
    odd_part = paired[..., 1]
    turned = jnp.stack(
        [evens * cosines - odd_part * sines, evens * sines + odd_part * cosines], axis=-1
    )
    return jnp.concatenate([turned.reshape(rotary.shape), passive], axis=-1)


def norm_rows(inputs, ln_gain, ln_bias):
    values_in = inputs.astype(jnp.float32)
    centred = values_in - jnp.mean(values_in, axis=-1, keepdims=True)
    inverse = lax.rsqrt(jnp.mean(centred * centred, axis=-1, keepdims=True) + EPSILON)
    standard = centred * inverse
    return (standard, inverse, (standard * ln_gain + ln_bias).astype(jnp.bfloat16))


def masked_scores(queries, keys_rot, seg_ids):
    places = jnp.arange(SEQ, dtype=jnp.int32)
    allowed = (seg_ids[:, None] == seg_ids[None, :]) & (places[:, None] >= places[None, :])
    scores = jnp.einsum("qhd,khd->hqk", queries, keys_rot, preferred_element_type=jnp.float32) * (
        1.0 / math.sqrt(HD)
    )
    return jnp.where(allowed[None], scores, -1e30)


def attend_forward(operands):
    queries, keys_rot, values, seg_ids = operands
    scores = masked_scores(queries, keys_rot, seg_ids)
    row_peak = jnp.max(scores, axis=-1, keepdims=True)
    lifted = jnp.exp(scores - row_peak)
    row_mass = jnp.sum(lifted, axis=-1, keepdims=True)
    probs = (lifted / row_mass).astype(jnp.bfloat16)
    context = jnp.einsum("hqk,khd->qhd", probs, values, preferred_element_type=jnp.float32)
    return (context.astype(jnp.bfloat16), (row_peak + jnp.log(row_mass))[..., 0])


def attend_backward(operands):
    queries, keys_rot, values, seg_ids, log_mass, ctx_grad = operands
    score_scale = 1.0 / math.sqrt(HD)
    scores = masked_scores(queries, keys_rot, seg_ids)
    probs = jnp.exp(scores - log_mass[..., None])
    rounded = probs.astype(jnp.bfloat16)
    value_grad = jnp.einsum("hqk,qhd->khd", rounded, ctx_grad, preferred_element_type=jnp.float32)
    prob_grad = jnp.einsum("qhd,khd->hqk", ctx_grad, values, preferred_element_type=jnp.float32)
    score_grad = (probs * (prob_grad - jnp.sum(probs * prob_grad, axis=-1, keepdims=True))).astype(
        jnp.bfloat16
    )
    query_grad = (
        jnp.einsum("hqk,khd->qhd", score_grad, keys_rot, preferred_element_type=jnp.float32)
        * score_scale
    )
    key_grad = (
        jnp.einsum("hqk,qhd->khd", score_grad, queries, preferred_element_type=jnp.float32)
        * score_scale
    )
    return (query_grad, key_grad, value_grad)


def project_heads(flat_rows, matrix, row_count):
    local_heads = matrix.shape[1] // HD
    return jnp.dot(flat_rows, matrix, preferred_element_type=jnp.float32).reshape(
        row_count, -1, local_heads, HD
    )


def attention_inputs(flat_rows, w_query, w_key, w_value, cosines, sines, row_count):
    queries = turn_pairs(project_heads(flat_rows, w_query, row_count), cosines, sines).astype(
        jnp.bfloat16
    )
    keys_rot = turn_pairs(project_heads(flat_rows, w_key, row_count), cosines, sines).astype(
        jnp.bfloat16
    )
    values = project_heads(flat_rows, w_value, row_count).astype(jnp.bfloat16)
    return (queries, keys_rot, values)


def mlp_inputs(flat_rows, w_in, b_in):
    hidden = jnp.dot(flat_rows, w_in.T, preferred_element_type=jnp.float32) + b_in.astype(
        jnp.float32
    )
    return (hidden, jax.nn.gelu(hidden, approximate=True).astype(jnp.bfloat16))


def gelu_grad(hidden, act_grad):
    pulled = jax.vjp(partial(jax.nn.gelu, approximate=True), hidden)[1](act_grad)[0]
    return pulled.astype(jnp.bfloat16)


def head_products(flat_rows, query_back, key_back, value_back, w_query, w_key, w_value):
    normed_part = (
        jnp.dot(query_back, w_query.T, preferred_element_type=jnp.float32)
        + jnp.dot(key_back, w_key.T, preferred_element_type=jnp.float32)
        + jnp.dot(value_back, w_value.T, preferred_element_type=jnp.float32)
    )
    w_query_part = jnp.dot(flat_rows.T, query_back, preferred_element_type=jnp.float32)
    w_key_part = jnp.dot(flat_rows.T, key_back, preferred_element_type=jnp.float32)
    w_value_part = jnp.dot(flat_rows.T, value_back, preferred_element_type=jnp.float32)
    return (normed_part, w_query_part, w_key_part, w_value_part)


def on_device_gathered(
    inputs,
    seg_lengths,
    group_counts,
    out_grad,
    ln_gain,
    ln_bias,
    w_query,
    w_key,
    w_value,
    w_output,
    w_in,
    b_in,
    w_out,
    b_out,
):
    row_count = inputs.shape[0]
    own_tokens = inputs.shape[1]
    local_width = w_query.shape[1]
    local_heads = local_width // HD
    seg_ids, positions = segment_layout(seg_lengths)
    cosines, sines = rotary_tables(positions)
    standard, inverse, normed = norm_rows(inputs, ln_gain, ln_bias)
    base_out = inputs.astype(jnp.float32) + b_out.astype(jnp.float32)
    gathered = lax.all_gather(normed, "mp", axis=1, tiled=True)
    flat_rows = gathered.reshape(row_count * SEQ, D)
    queries, keys_rot, values = attention_inputs(
        flat_rows, w_query, w_key, w_value, cosines, sines, row_count
    )
    context, log_mass = lax.map(attend_forward, (queries, keys_rot, values, seg_ids))
    ctx_flat = context.reshape(row_count * SEQ, local_width)
    hidden, activated = mlp_inputs(flat_rows, w_in, b_in)
    partial_out = jnp.dot(ctx_flat, w_output, preferred_element_type=jnp.float32) + jnp.dot(
        activated, w_out, preferred_element_type=jnp.float32
    )
    summed = lax.psum_scatter(
        partial_out.reshape(row_count, SEQ, D).astype(jnp.bfloat16),
        "mp",
        scatter_dimension=1,
        tiled=True,
    ).astype(jnp.float32)
    layer_out = (base_out + summed).astype(jnp.bfloat16)
    counts_now = group_counts.astype(jnp.float32)
    total_count = lax.psum(counts_now, "dp")
    weight_now = lax.axis_size("dp") * counts_now[0] / total_count[0]
    own_grad = out_grad.astype(jnp.float32) * weight_now
    own_rounded = own_grad.astype(jnp.bfloat16).reshape(row_count * own_tokens, D)
    cot_rows = lax.all_gather(out_grad, "mp", axis=1, tiled=True)
    branch_grad = (
        (cot_rows.astype(jnp.float32) * weight_now).astype(jnp.bfloat16).reshape(row_count * SEQ, D)
    )
    act_grad = jnp.dot(branch_grad, w_out.T, preferred_element_type=jnp.float32)
    hidden_grad = gelu_grad(hidden, act_grad)
    w_out_part = jnp.dot(activated.T, branch_grad, preferred_element_type=jnp.float32)
    w_in_part = jnp.dot(hidden_grad.T, flat_rows, preferred_element_type=jnp.float32)
    b_in_part = jnp.sum(hidden_grad.astype(jnp.float32), axis=0)
    ctx_grad = jnp.dot(branch_grad, w_output.T, preferred_element_type=jnp.float32).astype(
        jnp.bfloat16
    )
    w_output_part = jnp.dot(ctx_flat.T, branch_grad, preferred_element_type=jnp.float32)
    rot_query_grad, rot_key_grad, value_grad = lax.map(
        attend_backward,
        (
            queries,
            keys_rot,
            values,
            seg_ids,
            log_mass,
            ctx_grad.reshape(row_count, SEQ, local_heads, HD),
        ),
    )
    query_back = (
        turn_pairs(rot_query_grad, cosines, -sines)
        .astype(jnp.bfloat16)
        .reshape(row_count, SEQ, local_width)
    )
    key_back = (
        turn_pairs(rot_key_grad, cosines, -sines)
        .astype(jnp.bfloat16)
        .reshape(row_count, SEQ, local_width)
    )
    value_back = value_grad.astype(jnp.bfloat16).reshape(row_count, SEQ, local_width)
    normed_part, w_query_part, w_key_part, w_value_part = head_products(
        flat_rows,
        query_back.reshape(row_count * SEQ, local_width),
        key_back.reshape(row_count * SEQ, local_width),
        value_back.reshape(row_count * SEQ, local_width),
        w_query,
        w_key,
        w_value,
    )
    normed_part = normed_part + jnp.dot(hidden_grad, w_in, preferred_element_type=jnp.float32)
    normed_grad = lax.psum_scatter(
        normed_part.reshape(row_count, SEQ, D).astype(jnp.bfloat16),
        "mp",
        scatter_dimension=1,
        tiled=True,
    ).astype(jnp.float32)
    scaled = normed_grad * ln_gain
    input_part = inverse * (
        scaled
        - jnp.mean(scaled, axis=-1, keepdims=True)
        - standard * jnp.mean(scaled * standard, axis=-1, keepdims=True)
    )
    input_grad = (own_grad + input_part).astype(jnp.bfloat16)
    gain_part = jnp.sum(normed_grad * standard, axis=(0, 1))
    bias_part = jnp.sum(normed_grad, axis=(0, 1))
    out_bias_part = jnp.sum(own_rounded.astype(jnp.float32), axis=0)
    ln_gain_grad, ln_bias_grad, b_out_grad = (
        lax.psum_scatter(gain_part, ("dp", "mp"), scatter_dimension=0, tiled=True),
        lax.psum_scatter(bias_part, ("dp", "mp"), scatter_dimension=0, tiled=True),
        lax.psum_scatter(out_bias_part, ("dp", "mp"), scatter_dimension=0, tiled=True),
    )
    w_query_grad, w_key_grad, w_value_grad = (
        lax.psum_scatter(
            w_query_part.astype(jnp.bfloat16), "dp", scatter_dimension=0, tiled=True
        ).astype(jnp.float32),
        lax.psum_scatter(
            w_key_part.astype(jnp.bfloat16), "dp", scatter_dimension=0, tiled=True
        ).astype(jnp.float32),
        lax.psum_scatter(
            w_value_part.astype(jnp.bfloat16), "dp", scatter_dimension=0, tiled=True
        ).astype(jnp.float32),
    )
    w_output_grad, w_in_grad, w_out_grad = (
        lax.psum_scatter(
            w_output_part.astype(jnp.bfloat16), "dp", scatter_dimension=1, tiled=True
        ).astype(jnp.float32),
        lax.psum_scatter(
            w_in_part.astype(jnp.bfloat16), "dp", scatter_dimension=1, tiled=True
        ).astype(jnp.float32),
        lax.psum_scatter(
            w_out_part.astype(jnp.bfloat16), "dp", scatter_dimension=1, tiled=True
        ).astype(jnp.float32),
    )
    b_in_grad = lax.psum(b_in_part, "dp")
    return (
        layer_out,
        input_grad,
        ln_gain_grad,
        ln_bias_grad,
        w_query_grad,
        w_key_grad,
        w_value_grad,
        w_output_grad,
        w_in_grad,
        b_in_grad,
        w_out_grad,
        b_out_grad,
    )


QB = 256

NT = (((1,), (1,)), ((), ()))
NN = (((1,), (0,)), ((), ()))


def mm(a, b, dims=NN):
    return lax.dot_general(a, b, dims, preferred_element_type=jnp.float32)


def lane_turn(x, cosines, sines):
    width = x.shape[1]
    lanes = lax.broadcasted_iota(jnp.int32, x.shape, 1)
    swapped = jnp.where(lanes % 2 == 0, pltpu.roll(x, width - 1, 1), pltpu.roll(x, 1, 1))
    return x * cosines + swapped * sines


def attn_kernel(kb_ref, start_ref, q_ref, k_ref, v_ref, do_ref, cosq_ref, sinq_ref, cos_ref, sin_ref,
                ctx_ref, dq_ref, dk_ref, dv_ref, dk_acc, dv_acc, bias_ref):
    i, hp = pl.program_id(0), pl.program_id(1)
    kb = kb_ref[i]

    @pl.when(i == 0)
    def _():
        dk_acc[hp] = jnp.zeros(dk_acc.shape[1:], jnp.float32)
        dv_acc[hp] = jnp.zeros(dv_acc.shape[1:], jnp.float32)

    def body(blocks):
        w = blocks * QB
        k0 = pl.multiple_of(kb * QB, QB)

        @pl.when(hp == 0)
        def _():
            keys = lax.broadcasted_iota(jnp.int32, (w, QB), 0) + k0
            queries = lax.broadcasted_iota(jnp.int32, (w, QB), 1) + i * QB
            fine = (keys >= start_ref[...]) & (keys <= queries)
            bias_ref[:w] = jnp.where(fine, 0.0, -1e30)

        q, do = q_ref[...], do_ref[...]
        low = lax.broadcasted_iota(jnp.int32, q.shape, 1) < HD
        zero = jnp.zeros_like(q)
        k, v = k_ref[pl.ds(k0, w), :], v_ref[pl.ds(k0, w), :]
        kt, vt = k.T, v.T
        outs, dqs = [], []
        dk_new, dv_new = dk_acc[hp, pl.ds(k0, w), :], dv_acc[hp, pl.ds(k0, w), :]
        for head in range(2):
            qh = jnp.where(low, q, zero) if head == 0 else jnp.where(low, zero, q)
            doh = jnp.where(low, do, zero) if head == 0 else jnp.where(low, zero, do)
            s = mm(k, qh, NT) + bias_ref[:w]
            e = jnp.exp(s - jnp.max(s, axis=0, keepdims=True))
            p = e * (1.0 / jnp.sum(e, axis=0, keepdims=True))
            pb = p.astype(jnp.bfloat16)
            pd = p * mm(v, doh, NT)
            ds = (pd - p * jnp.sum(pd, axis=0, keepdims=True)).astype(jnp.bfloat16)
            dv_new = dv_new + mm(pb, doh)
            dk_new = dk_new + mm(ds, qh)
            outs.append(mm(vt[head * HD:(head + 1) * HD], pb))
            dqs.append(mm(kt[head * HD:(head + 1) * HD], ds))
        dk_acc[hp, pl.ds(k0, w), :] = dk_new
        dv_acc[hp, pl.ds(k0, w), :] = dv_new
        ctx_ref[...] = jnp.concatenate(outs, axis=0).T.astype(jnp.bfloat16)
        dq = jnp.concatenate(dqs, axis=0).T * 0.125
        dq_ref[...] = lane_turn(dq, cosq_ref[...], -sinq_ref[...]).astype(jnp.bfloat16)

    for blocks in range(1, 4):
        pl.when(i - kb + 1 == blocks)(partial(body, blocks))

    @pl.when(i == pl.num_programs(0) - 1)
    def _():
        dk_ref[...] = lane_turn(dk_acc[hp], cos_ref[...], -sin_ref[...]).astype(jnp.bfloat16)
        dv_ref[...] = dv_acc[hp].astype(jnp.bfloat16)


def attention(qkv, do, starts, cosines, sines):
    width = do.shape[1]
    pairs, steps = width // 128, SEQ // QB
    kb = starts[::QB] // QB
    last = steps - 1
    qspec = pl.BlockSpec((QB, 128), lambda i, h, kb: (i, h))
    kspec = pl.BlockSpec((SEQ, 128), lambda i, h, kb: (0, pairs + h))
    vspec = pl.BlockSpec((SEQ, 128), lambda i, h, kb: (0, 2 * pairs + h))
    outk = pl.BlockSpec((SEQ, 128), lambda i, h, kb: (0, jnp.where(i == last, h, 0)))
    shape = jax.ShapeDtypeStruct((SEQ, width), jnp.bfloat16)
    ctx, dq, dk, dv = pl.pallas_call(
        attn_kernel,
        grid_spec=pltpu.PrefetchScalarGridSpec(
            num_scalar_prefetch=1, grid=(steps, pairs),
            in_specs=[pl.BlockSpec((1, QB), lambda i, h, kb: (0, i)), qspec, kspec, vspec, qspec,
                      pl.BlockSpec((QB, 128), lambda i, h, kb: (i, 0)), pl.BlockSpec((QB, 128), lambda i, h, kb: (i, 0)),
                      pl.BlockSpec((SEQ, 128), lambda i, h, kb: (0, 0)), pl.BlockSpec((SEQ, 128), lambda i, h, kb: (0, 0))],
            out_specs=[qspec, qspec, outk, outk],
            scratch_shapes=[pltpu.VMEM((pairs, SEQ, 128), jnp.float32), pltpu.VMEM((pairs, SEQ, 128), jnp.float32),
                            pltpu.VMEM((3 * QB, QB), jnp.float32)]),
        out_shape=[shape] * 4,
        compiler_params=pltpu.CompilerParams(vmem_limit_bytes=63 << 20),
        cost_estimate=pl.CostEstimate(flops=30 << 30, bytes_accessed=16 << 20, transcendentals=8 << 20),
        name="attention",
    )(kb, starts[None], qkv, qkv, qkv, do, cosines, sines, cosines, sines)
    return ctx, (dq, dk, dv)


def lane_tables(positions):
    lanes = jnp.arange(128, dtype=jnp.int32) % HD
    exponents = (lanes // 2 * 2).astype(jnp.float32) / ROT
    angles = positions.astype(jnp.float32)[:, None] * jnp.power(10000.0, -exponents)
    turned = (lanes < ROT)[None]
    signs = jnp.where(lanes % 2 == 0, -1.0, 1.0)[None]
    return jnp.where(turned, jnp.cos(angles), 1.0), jnp.where(turned, jnp.sin(angles) * signs, 0.0)


def weight_block(ref):
    half = ref.shape[0] // 2
    rows = half * ref.shape[2]
    return jnp.concatenate(
        [ref[:half, 0].reshape(rows, 128), ref[half:, 0].reshape(rows, 128)], axis=1
    )


def qkv_kernel(x_ref, w_ref, cos_ref, sin_ref, o_ref):
    j = pl.program_id(0)
    out = mm(x_ref[...], weight_block(w_ref))

    @pl.when(j < 2)
    def _():
        cosines = jnp.concatenate([cos_ref[...]] * 2, axis=1)
        sines = jnp.concatenate([sin_ref[...]] * 2, axis=1)
        scale = jnp.where(j == 0, 0.125, 1.0)
        o_ref[...] = (lane_turn(out, cosines, sines).astype(jnp.bfloat16) * scale.astype(jnp.bfloat16))

    @pl.when(j == 2)
    def _():
        o_ref[...] = out.astype(jnp.bfloat16)


MESH_ID = pl.DeviceIdType.MESH
ZS, XS, YS, CS = 4, 2, 2, 2
G1_ROWS = 1024
G2_ROWS = 2064
SPLITS = ((0, 512), (512, 512))


def place_of(z, x, y, c):
    return (z * XS + x) * (YS * CS) + y * CS + c


def gather_kernel(x_ref, gain_ref, bias_ref, count_ref, g1_ref, grad_ref,
                  normed_ref, turned_ref, row_ref, grad_row, g1_out, counts_ref,
                  nv, tv, send_sem, recv_sem, own_sem, a2a_send, a2a_recv, row_sem, turn_sem, count_send, count_recv,
                  grad_send, grad_recv, grad_sem):
    dp, mp = lax.axis_index("dp"), lax.axis_index("mp")
    y, c, z, x = dp // CS, dp % CS, mp // XS, mp % XS
    members, own = ZS * XS, x_ref.shape[1]

    def device(z, x, y, c):
        return (y * CS + c, z * XS + x)

    barrier = pltpu.get_barrier_semaphore()
    others = [(dp, lax.rem(mp + k, members)) for k in range(1, members)]
    others += [(lax.rem(dp + k, YS * CS), mp) for k in range(1, YS * CS)]
    for other in others:
        pl.semaphore_signal(barrier, inc=1, device_id=other, device_id_type=MESH_ID)
    pl.semaphore_wait(barrier, len(others))

    copies = []

    def send(block, slot, piece, target, local=False):
        src, out = g1_ref, g1_out
        first, rows = SPLITS[block]
        spot = place_of(*piece)
        at = out.at[spot, pl.ds(first, rows)]
        copy = pltpu.make_async_remote_copy(
            src_ref=src.at[pl.ds(first, rows)] if local else at, dst_ref=at,
            send_sem=send_sem.at[block, slot], recv_sem=recv_sem.at[block, slot],
            device_id=device(*target), device_id_type=MESH_ID)
        copy.start()
        copies.append(copy)
        return copy

    recv = {}

    def hop(block, slot, piece, target, local=False):
        recv[block, slot] = send(block, slot, piece, target, local)

    flip = {"x": (z, 1 - x, y, c), "y": (z, x, 1 - y, c), "c": (z, x, y, 1 - c)}

    def orders(block):
        return ("x", "y") if block % 2 == 0 else ("y", "x")

    def begin(block):
        me = (z, x, y, c)
        for k in range(1, ZS):
            hop(block, k - 1, me, (lax.rem(z + k, ZS), x, y, c), True)
        one, two = orders(block)
        hop(block, 3, me, flip[one], True)
        hop(block, 7, me, flip[two], True)
        hop(block, 15, me, flip["c"], True)

    counts_ref[dp] = count_ref[...]
    count_copies = []
    for k in range(1, YS * CS):
        copy = pltpu.make_async_remote_copy(
            src_ref=count_ref, dst_ref=counts_ref.at[dp], send_sem=count_send.at[k], recv_sem=count_recv.at[k],
            device_id=(lax.rem(dp + k, YS * CS), mp), device_id_type=MESH_ID)
        copy.start()
        count_copies.append(copy)

    for block in range(2):
        begin(block)
    mine = pl.ds(pl.multiple_of(mp * own, own), own)
    grad_copies = []
    for k in range(1, members):
        row = lax.rem(mp + k, members)
        copy = pltpu.make_async_remote_copy(
            src_ref=grad_ref.at[row], dst_ref=grad_row.at[mine], send_sem=grad_send.at[k], recv_sem=grad_recv.at[k],
            device_id=(dp, row), device_id_type=MESH_ID)
        copy.start()
        grad_copies.append(copy)
    own_grad = pltpu.make_async_copy(grad_ref.at[mp], grad_row.at[mine], grad_sem.at[0])
    own_grad.start()
    me_spot = place_of(z, x, y, c)
    own_copies = [pltpu.make_async_copy(g1_ref, g1_out.at[me_spot], own_sem.at[0])]

    def normalise(k, carry):
        row = lax.rem(mp + k, members)
        value = x_ref[row].astype(jnp.float32)
        centred = value - jnp.mean(value, axis=-1, keepdims=True)
        inverse = lax.rsqrt(jnp.mean(centred * centred, axis=-1, keepdims=True) + EPSILON)
        nv[k] = (centred * inverse * gain_ref[...] + bias_ref[...]).astype(jnp.bfloat16)
        pltpu.make_async_copy(nv.at[k], normed_ref.at[row], row_sem.at[k]).start()
        return carry

    lax.fori_loop(0, members, normalise, 0)
    row_copies = []
    for k in range(1, members):
        row = lax.rem(mp + k, members)
        pltpu.make_async_copy(nv.at[k], normed_ref.at[row], row_sem.at[k]).wait()
        copy = pltpu.make_async_remote_copy(
            src_ref=normed_ref.at[row], dst_ref=row_ref.at[mine], send_sem=a2a_send.at[k], recv_sem=a2a_recv.at[k],
            device_id=(dp, row), device_id_type=MESH_ID)
        copy.start()
        row_copies.append(copy)
    pltpu.make_async_copy(nv.at[0], normed_ref.at[mp], row_sem.at[0]).wait()
    own_row = pltpu.make_async_copy(nv.at[0], row_ref.at[mine], row_sem.at[0])
    own_row.start()
    for copy in own_copies:
        copy.start()

    def turn(k, carry):
        row = lax.rem(mp + k, members)
        tv[:, pl.ds(pl.multiple_of(row * own, own), own)] = nv[k].T
        return carry

    lax.fori_loop(0, members, turn, 0)
    width = tv.shape[0] // (YS * CS)
    turn_copies = []
    for rel in range(YS * CS):
        yr, cr = rel % YS, rel // YS
        from_block = lax.rem(y + yr, YS) * CS + lax.rem(c + cr, CS)
        copy = pltpu.make_async_copy(
            tv.at[pl.ds(pl.multiple_of(from_block * width, width), width)], turned_ref.at[rel], turn_sem.at[rel])
        copy.start()
        turn_copies.append(copy)

    for blocks in ((0, 1),):
        for kz in range(1, ZS):
            for block in blocks:
                one, two = orders(block)
                recv[block, kz - 1].wait_recv()
                piece = (lax.rem(z + ZS - kz, ZS), x, y, c)
                hop(block, 3 + kz, piece, flip[one])
                hop(block, 7 + kz, piece, flip[two])
                hop(block, 15 + kz, piece, flip["c"])
        for kz in range(ZS):
            for block in blocks:
                one, two = orders(block)
                recv[block, 3 + kz].wait_recv()
                zz = lax.rem(z + ZS - kz, ZS)
                piece = (zz, 1 - x, y, c) if one == "x" else (zz, x, 1 - y, c)
                hop(block, 11 + kz, piece, flip[two])
                hop(block, 19 + kz, piece, flip["c"])
        for half in range(2):
            for kz in range(ZS):
                for block in blocks:
                    one, two = orders(block)
                    recv[block, 7 + half * ZS + kz].wait_recv()
                    zz = lax.rem(z + ZS - kz, ZS)
                    if half == 0:
                        piece = (zz, x, 1 - y, c) if two == "y" else (zz, 1 - x, y, c)
                    else:
                        piece = (zz, 1 - x, 1 - y, c)
                    hop(block, 23 + half * ZS + kz, piece, flip["c"])
    for block in range(2):
        for slot in range(15, 31):
            recv[block, slot].wait_recv()
    for copy in copies:
        copy.wait_send()
    for copy in own_copies + turn_copies:
        copy.wait()
    own_row.wait()
    own_grad.wait()
    for copy in row_copies + grad_copies + count_copies:
        copy.wait()


def gather_all(inputs, ln_gain, ln_bias, counts, g1, out_grad):
    rows, own, width = inputs.shape
    places = ZS * XS * YS * CS
    any_space = pl.BlockSpec(memory_space=pl.ANY)
    vmem = pl.BlockSpec(memory_space=pltpu.VMEM)
    shape = jax.ShapeDtypeStruct
    half = jnp.bfloat16
    dma = pltpu.SemaphoreType.DMA
    return pl.pallas_call(
        gather_kernel,
        in_specs=[vmem, vmem, vmem, vmem, any_space, any_space],
        out_specs=[pl.BlockSpec(memory_space=pltpu.HBM)] * 5 + [vmem],
        out_shape=[
            shape((rows, own, width), half),
            shape((YS * CS, width // (YS * CS), rows * own), half),
            shape((rows * own, width), half),
            shape((rows * own, width), half),
            shape((places,) + g1.shape, half),
            shape((YS * CS, 8, 128), jnp.float32),
        ],
        scratch_shapes=[
            pltpu.VMEM((rows, own, width), half), pltpu.VMEM((width, rows * own), half),
            dma((2, 31)), dma((2, 31)), dma((1,)), dma((rows,)), dma((rows,)), dma((rows,)), dma((YS * CS,)),
            dma((YS * CS,)), dma((YS * CS,)), dma((rows,)), dma((rows,)), dma((1,)),
        ],
        compiler_params=pltpu.CompilerParams(collective_id=0, has_side_effects=True, vmem_limit_bytes=63 << 20),
        name="gather_weights",
    )(inputs, ln_gain[None], ln_bias[None], counts, g1, out_grad)


PLACES = ZS * XS * YS * CS
PIECE = 256


def relative(dp, rel):
    return lax.rem(dp // CS + rel % YS, YS) * CS + lax.rem(dp % CS + rel // YS, CS)


def wide(ref, at, first, rows, count):
    return jnp.concatenate(
        [ref[at + (slice(first + b * rows, first + (b + 1) * rows),)] for b in range(count)], axis=-1
    )


def cotangent_kernel(place_ref, grad_ref, row_ref, weight_ref, piece_ref, branch_ref, turned_ref, row_turned_ref, ctx_ref,
                     w_ref, sum_ref):
    branch = (grad_ref[...].astype(jnp.float32) * weight_ref[...]).astype(jnp.bfloat16)
    branch_ref[...] = branch
    sum_ref[...] = jnp.sum(branch.astype(jnp.float32), axis=0, keepdims=True)
    for b in range(D // 128):
        w_ref[:, b * 128:(b + 1) * 128] = piece_ref[:, 0, b * 32:(b + 1) * 32, :].reshape(D, 128)
    branch_row = (row_ref[...].astype(jnp.float32) * weight_ref[...]).astype(jnp.bfloat16)
    ctx_ref[...] = mm(branch_row, w_ref[...], NT).astype(jnp.bfloat16)
    for rel in range(YS * CS):
        block = pl.ds(pl.multiple_of(relative(place_ref[0], rel) * PIECE, PIECE), PIECE)
        turned_ref[rel] = branch_ref[:, block].T
        row_turned_ref[rel] = (row_ref[:, block].astype(jnp.float32) * weight_ref[...]).astype(jnp.bfloat16).T


def cotangent(place, out_grad, grad_row, weight, g1):
    tokens = out_grad.shape[0]
    half = jnp.bfloat16
    shape = jax.ShapeDtypeStruct
    whole = lambda *dims: pl.BlockSpec(dims, lambda i, p: (0,) * len(dims), pipeline_mode=pl.Buffered(1))
    return pl.pallas_call(
        cotangent_kernel,
        grid_spec=pltpu.PrefetchScalarGridSpec(
            num_scalar_prefetch=1, grid=(1,),
            in_specs=[whole(tokens, D), whole(tokens, D), whole(1, 1),
                      pl.BlockSpec((PLACES, 1, 256, 128), lambda i, p: (0, 3, 0, 0))],
            out_specs=[whole(tokens, D), whole(4, PIECE, tokens), whole(4, PIECE, tokens), whole(tokens, D), whole(D, D),
                       whole(1, D)]),
        out_shape=[shape((tokens, D), half), shape((4, PIECE, tokens), half), shape((4, PIECE, tokens), half),
                   shape((tokens, D), half), shape((D, D), half), shape((1, D), jnp.float32)],
        compiler_params=pltpu.CompilerParams(vmem_limit_bytes=63 << 20),
        cost_estimate=pl.CostEstimate(flops=2 << 30, bytes_accessed=18 << 20, transcendentals=0),
        name="cotangent",
    )(place, out_grad, grad_row, weight, g1.reshape(PLACES, 4, 256, 128))


def project(rows, g1, cosines, sines):
    return pl.pallas_call(
        qkv_kernel,
        grid=(3, ZS),
        in_specs=[
            pl.BlockSpec((SEQ, D), lambda j, c: (0, 0)),
            pl.BlockSpec((8, 1, 256, 128), lambda j, c: (c, j, 0, 0)),
            pl.BlockSpec((SEQ, 128), lambda j, c: (0, 0)),
            pl.BlockSpec((SEQ, 128), lambda j, c: (0, 0)),
        ],
        out_specs=pl.BlockSpec((SEQ, 256), lambda j, c: (0, j * ZS + c)),
        out_shape=jax.ShapeDtypeStruct((SEQ, 3 * D), jnp.bfloat16),
        compiler_params=pltpu.CompilerParams(vmem_limit_bytes=63 << 20),
        cost_estimate=pl.CostEstimate(flops=6 << 30, bytes_accessed=14 << 20, transcendentals=0),
        name="qkv",
    )(rows, g1.reshape(PLACES, 4, 256, 128), cosines, sines)


def put_tiles(values, keep_ref, send_ref):
    for xr in range(XS):
        for yr in range(YS):
            keep_ref[yr, xr, 0] = values[xr][yr * PIECE:(yr + 1) * PIECE]
            send_ref[yr, xr, 0] = values[xr][(YS + yr) * PIECE:(YS + yr + 1) * PIECE]


def tile_specs(n, index):
    spec = pl.BlockSpec((YS, XS, 1, PIECE, n), index)
    return [spec, spec]


def tile_shapes(n):
    shape = jax.ShapeDtypeStruct((YS, XS, ZS, PIECE, n), jnp.bfloat16)
    return [shape, shape]


def by_x(value):
    return [value[:, :128], value[:, 128:]]


def back_kernel(place_ref, x_ref, w_ref, dq_ref, dk_ref, dv_ref, n_ref, keep_ref, send_ref, xt_ref, acc_ref):
    step = pl.program_id(0)

    @pl.when(step == 0)
    def _():
        for rel in range(YS * CS):
            block = relative(place_ref[0], rel)
            xt_ref[rel * PIECE:(rel + 1) * PIECE] = x_ref[:, pl.ds(pl.multiple_of(block * PIECE, PIECE), PIECE)].T
        acc_ref[...] = jnp.zeros_like(acc_ref)

    total = acc_ref[...]
    for j, d_ref in enumerate((dq_ref, dk_ref, dv_ref)):
        d = d_ref[...]
        total = total + mm(d, weight_block(w_ref.at[:, j:j + 1]), NT)
        values = by_x(mm(xt_ref[...], d).astype(jnp.bfloat16))
        lanes = pl.ds(j * 128, 128)
        put_tiles(values, keep_ref.at[..., lanes], send_ref.at[..., lanes])
    acc_ref[...] = total

    @pl.when(step == pl.num_programs(0) - 1)
    def _():
        n_ref[...] = acc_ref[...].astype(jnp.bfloat16)


def back(place, rows, g1, grads):
    return pl.pallas_call(
        back_kernel,
        grid_spec=pltpu.PrefetchScalarGridSpec(
            num_scalar_prefetch=1, grid=(ZS,),
            in_specs=[
                pl.BlockSpec((SEQ, D), lambda k, p: (0, 0), pipeline_mode=pl.Buffered(1)),
                pl.BlockSpec((8, 3, 256, 128), lambda k, p: (k, 0, 0, 0)),
            ]
            + [pl.BlockSpec((SEQ, 256), lambda k, p: (0, k))] * 3,
            out_specs=[pl.BlockSpec((SEQ, D), lambda k, p: (0, 0), pipeline_mode=pl.Buffered(1))]
            + tile_specs(384, lambda k, p: (0, 0, k, 0, 0)),
            scratch_shapes=[pltpu.VMEM((D, SEQ), jnp.bfloat16), pltpu.VMEM((SEQ, D), jnp.float32)]),
        out_shape=[jax.ShapeDtypeStruct((SEQ, D), jnp.bfloat16)] + tile_shapes(384),
        compiler_params=pltpu.CompilerParams(vmem_limit_bytes=63 << 20),
        cost_estimate=pl.CostEstimate(flops=12 << 30, bytes_accessed=22 << 20, transcendentals=0),
        name="attention_back",
    )(place, rows, g1.reshape(PLACES, 4, 256, 128), *grads)


HALF_PIECE = PIECE // 2
Z_ORDER = (2, 1, 3, 0)
BAND = 16


class Reduction:
    def __init__(self, keeps, sends, bufs):
        self.keeps, self.sends = keeps, sends
        (self.own, self.got, self.first, self.second, self.last, self.own_sem, self.core_send, self.core_recv,
         self.first_send, self.first_recv, self.second_send, self.second_recv, self.last_send, self.last_recv) = bufs
        dp, mp = lax.axis_index("dp"), lax.axis_index("mp")
        y, c, z, x = dp // CS, dp % CS, mp // XS, mp % XS
        self.x, self.z = x, z
        device = lambda z, x, y, c: (y * CS + c, z * XS + x)
        self.partner = device(z, x, y, 1 - c)
        self.axes = (device(z, 1 - x, y, c), device(z, x, 1 - y, c))
        self.line = [device(lax.rem(z + k, ZS), x, y, c) for k in range(ZS)]
        self.peers = [self.partner, *self.axes, *self.line[1:]]

    def parts(self):
        at = 0
        for s, ref in enumerate(self.keeps):
            for i in range(XS):
                yield s, i, pl.ds(at, ref.shape[-1])
            at += ref.shape[-1]

    def mine(self, s, i, k, lanes):
        return pltpu.make_async_copy(
            self.keeps[s].at[:, lax.rem(self.x + i, XS), lax.rem(self.z + k, ZS)], self.own.at[k, i, :, :, lanes],
            self.own_sem.at[s, i, k])

    def core(self, s, i, k, lanes):
        return pltpu.make_async_remote_copy(
            src_ref=self.sends[s].at[:, lax.rem(self.x + i, XS), lax.rem(self.z + k, ZS)],
            dst_ref=self.got.at[k, i, :, :, lanes],
            send_sem=self.core_send.at[s, i, k], recv_sem=self.core_recv.at[s, i, k],
            device_id=self.partner, device_id_type=MESH_ID)

    def load(self):
        for k in Z_ORDER:
            for s, i, lanes in self.parts():
                self.mine(s, i, k, lanes).start()

    def begin(self):
        for k in Z_ORDER:
            for s, i, lanes in self.parts():
                self.core(s, i, k, lanes).start()

    def half_of(self, ref, k, half, away, other):
        yy, xx = (other, away) if half == 0 else (away, other)
        return ref.at[k, xx, yy, pl.ds(half * HALF_PIECE, HALF_PIECE)]

    def one(self, k, half, other):
        return pltpu.make_async_remote_copy(
            src_ref=self.half_of(self.own, k, half, 1, other), dst_ref=self.first.at[k, half, other],
            send_sem=self.first_send.at[k, half, other], recv_sem=self.first_recv.at[k, half, other],
            device_id=self.axes[half], device_id_type=MESH_ID)

    def two(self, k, half):
        return pltpu.make_async_remote_copy(
            src_ref=self.half_of(self.own, k, half, 0, 1), dst_ref=self.second.at[k, half],
            send_sem=self.second_send.at[k, half], recv_sem=self.second_recv.at[k, half],
            device_id=self.axes[1 - half], device_id_type=MESH_ID)

    def three(self, k, half):
        return pltpu.make_async_remote_copy(
            src_ref=self.half_of(self.own, k, half, 0, 0), dst_ref=self.last.at[k, half],
            send_sem=self.last_send.at[k, half], recv_sem=self.last_recv.at[k, half],
            device_id=self.line[k], device_id_type=MESH_ID)

    def add(self, refs, write):
        def body(i, carry):
            band = pl.ds(pl.multiple_of(i * BAND, BAND), BAND)
            value = refs[0][band].astype(jnp.float32)
            for ref in refs[1:]:
                value = value + ref[band].astype(jnp.float32)
            write(band, value)
            return carry

        lax.fori_loop(0, HALF_PIECE // BAND, body, 0)

    def store(self, k, half, away, other, *extra):
        own = self.half_of(self.own, k, half, away, other)

        def write(band, value):
            own[band] = value.astype(jnp.bfloat16)

        self.add((own, self.half_of(self.got, k, half, away, other), *extra), write)

    def stage_one(self, k):
        for s, i, lanes in self.parts():
            self.mine(s, i, k, lanes).wait()
            self.core(s, i, k, lanes).wait_recv()
        for other in (1, 0):
            for half in range(2):
                self.store(k, half, 1, other)
                self.one(k, half, other).start()

    def stage_two(self, k):
        for half in range(2):
            self.one(k, half, 1).wait_recv()
            self.store(k, half, 0, 1, self.first.at[k, half, 1])
            self.two(k, half).start()

    def stage_three(self, k):
        for half in range(2):
            self.one(k, half, 0).wait_recv()
            self.two(k, half).wait_recv()
            if k:
                self.store(k, half, 0, 0, self.first.at[k, half, 0], self.second.at[k, half])
                self.three(k, half).start()

    def finish(self, out_ref):
        self.stage_three(0)
        for half in range(2):
            for k in range(1, ZS):
                self.three(k, half).wait_recv()
            out = out_ref.at[pl.ds(half * HALF_PIECE, HALF_PIECE)]

            def write(band, value):
                out[band] = value

            self.add(
                [self.half_of(self.own, 0, half, 0, 0), self.half_of(self.got, 0, half, 0, 0), self.first.at[0, half, 0],
                 self.second.at[0, half]] + [self.last.at[k, half] for k in range(1, ZS)], write)
        for k in range(ZS):
            for s, i, lanes in self.parts():
                self.core(s, i, k, lanes).wait_send()
            for half in range(2):
                for other in range(2):
                    self.one(k, half, other).wait_send()
                self.two(k, half).wait_send()
                if k:
                    self.three(k, half).wait_send()


def greet(others):
    barrier = pltpu.get_barrier_semaphore()
    for other in others:
        pl.semaphore_signal(barrier, inc=1, device_id=other, device_id_type=MESH_ID)
    pl.semaphore_wait(barrier, len(others))


def reduction_scratch(sets, width):
    half, dma = jnp.bfloat16, pltpu.SemaphoreType.DMA
    tiles = pltpu.VMEM((ZS, XS, YS, PIECE, width), half)
    lines = pltpu.VMEM((ZS, 2, HALF_PIECE, width), half)
    return [tiles, tiles, pltpu.VMEM((ZS, 2, 2, HALF_PIECE, width), half), lines, lines,
            dma((sets, XS, ZS)), dma((sets, XS, ZS)), dma((sets, XS, ZS)), dma((ZS, 2, 2)), dma((ZS, 2, 2)),
            dma((ZS, 2)), dma((ZS, 2)), dma((ZS, 2)), dma((ZS, 2))]


REDUCTION_REFS = 14


NORM_BAND = 128


def reduce_kernel(sets, *refs):
    keeps, sends, small_ref = refs[:sets], refs[sets:2 * sets], refs[2 * sets]
    refs = refs[2 * sets + 1:]
    token_refs, (gain_ref, bias_ref, weight_ref) = refs[:8], refs[8:11]
    out_ref, small_out, sums_out, grad_hbm, layer_hbm = refs[11:16]
    work = Reduction(keeps, sends, refs[16:16 + REDUCTION_REFS])
    refs = refs[16 + REDUCTION_REFS:]
    token_bufs, (grad_buf, layer_buf, sums_buf, sums_got, small_got, small_send, small_recv, small_sem, sums_send, sums_recv,
                 token_sem) = refs[:8], refs[8:]
    dp, mp = lax.axis_index("dp"), lax.axis_index("mp")
    groups, members = YS * CS, ZS * XS
    everyone = [(lax.rem(dp + a, groups), lax.rem(mp + b, members))
                for a in range(groups) for b in range(members) if (a, b) != (0, 0)]
    work.load()
    loads = [pltpu.make_async_copy(ref, buf, token_sem.at[i]) for i, (ref, buf) in enumerate(zip(token_refs, token_bufs))]
    for copy in loads:
        copy.start()
    greet(everyone)
    work.begin()
    small_local = pltpu.make_async_copy(small_ref.at[dp * members + mp], small_got.at[0], small_sem.at[0])
    small_local.start()
    small_copies = []
    for i, (a, b) in enumerate(everyone):
        copy = pltpu.make_async_remote_copy(
            src_ref=small_ref.at[a * members + b], dst_ref=small_got.at[i + 1], send_sem=small_send.at[i],
            recv_sem=small_recv.at[i], device_id=(a, b), device_id_type=MESH_ID)
        copy.start()
        small_copies.append(copy)
    order = Z_ORDER
    work.stage_one(order[0])
    work.stage_one(order[1])

    for copy in loads:
        copy.wait()
    sums_buf[...] = jnp.zeros_like(sums_buf)

    def norm_back(i, carry):
        band = pl.ds(pl.multiple_of(i * NORM_BAND, NORM_BAND), NORM_BAND)
        x, g, a, m0, m1, ao, mo0, mo1 = [buf[band].astype(jnp.float32) for buf in token_bufs]
        layer_buf[band] = (x + bias_ref[...].astype(jnp.float32) + ao + (mo0 + mo1)).astype(jnp.bfloat16)
        centred = x - jnp.mean(x, axis=-1, keepdims=True)
        inverse = lax.rsqrt(jnp.mean(centred * centred, axis=-1, keepdims=True) + EPSILON)
        standard = centred * inverse
        grad = a + (m0 + m1)
        scaled = grad * gain_ref[...]
        part = inverse * (
            scaled
            - jnp.mean(scaled, axis=-1, keepdims=True)
            - standard * jnp.mean(scaled * standard, axis=-1, keepdims=True)
        )
        grad_buf[band] = (g * weight_ref[...] + part).astype(jnp.bfloat16)
        sums_buf[...] += jnp.concatenate(
            [jnp.sum(grad * standard, axis=0, keepdims=True), jnp.sum(grad, axis=0, keepdims=True)], axis=0)
        return carry

    lax.fori_loop(0, x_bands(token_bufs[0]), norm_back, 0)
    results = [pltpu.make_async_copy(grad_buf, grad_hbm, token_sem.at[8]),
               pltpu.make_async_copy(layer_buf, layer_hbm, token_sem.at[9])]
    for copy in results:
        copy.start()
    sums_copies = []
    for i, (a, b) in enumerate(everyone):
        copy = pltpu.make_async_remote_copy(
            src_ref=sums_buf, dst_ref=sums_got.at[i], send_sem=sums_send.at[i],
            recv_sem=sums_recv.at[i], device_id=(a, b), device_id_type=MESH_ID)
        copy.start()
        sums_copies.append(copy)

    work.stage_two(order[0])
    work.stage_one(order[2])
    work.stage_three(order[0])
    work.stage_two(order[1])
    work.stage_one(order[3])
    work.stage_three(order[1])
    work.stage_two(order[2])
    work.stage_three(order[2])
    work.stage_two(order[3])
    small_local.wait()
    for copy in small_copies + sums_copies:
        copy.wait_recv()
    summed, sums = small_got[0], sums_buf[...]
    for i in range(1, PLACES):
        summed = summed + small_got[i]
        sums = sums + sums_got[i - 1]
    small_out[...] = summed
    sums_out[...] = sums
    work.finish(out_ref)
    for copy in small_copies + sums_copies:
        copy.wait_send()
    for copy in results:
        copy.wait()


def x_bands(ref):
    return ref.shape[0] // NORM_BAND


def reduce_tiles(keeps, sends, small, token_args, ln_gain, b_out, weight):
    width, sets = sum(keep.shape[-1] for keep in keeps), len(keeps)
    any_space, vmem = pl.BlockSpec(memory_space=pl.ANY), pl.BlockSpec(memory_space=pltpu.VMEM)
    dma, full = pltpu.SemaphoreType.DMA, jnp.float32
    tokens = jax.ShapeDtypeStruct(token_args[0].shape, jnp.bfloat16)
    buffer = lambda array: pltpu.VMEM(array.shape, array.dtype)
    return pl.pallas_call(
        partial(reduce_kernel, sets),
        in_specs=[any_space] * (2 * sets + 1 + len(token_args)) + [vmem] * 3,
        out_specs=[vmem, vmem, vmem, any_space, any_space],
        out_shape=[jax.ShapeDtypeStruct((PIECE, width), full), jax.ShapeDtypeStruct((8, 128), full),
                   jax.ShapeDtypeStruct((2, D), full), tokens, tokens],
        scratch_shapes=reduction_scratch(sets, width) + [buffer(array) for array in token_args] + [
            buffer(tokens), buffer(tokens), pltpu.VMEM((2, D), full), pltpu.VMEM((PLACES - 1, 2, D), full),
            pltpu.VMEM((PLACES, 8, 128), full), dma((PLACES,)), dma((PLACES,)), dma((1,)), dma((PLACES,)), dma((PLACES,)),
            dma((10,))],
        compiler_params=pltpu.CompilerParams(collective_id=1, has_side_effects=True, vmem_limit_bytes=63 << 20),
        name="reduce_tiles",
    )(*keeps, *sends, small, *token_args, ln_gain[None], b_out[None], weight)


C0 = math.sqrt(2.0 / math.pi)


def mlp_kernel(sets, x_ref, xt_ref, g_ref, gt_ref, wa_ref, wb_ref, *refs):
    out_ref, dn_ref, keep_ref, send_ref, bsum_ref, sum_ref = refs[2 * sets:2 * sets + 6]
    work = Reduction(refs[:sets], refs[sets:2 * sets], refs[2 * sets + 6:])
    step = pl.program_id(0)
    order = Z_ORDER

    @pl.when(step == 0)
    def _():
        work.load()
        greet(work.peers)
        work.begin()
        out_ref[...] = jnp.zeros_like(out_ref)
        dn_ref[...] = jnp.zeros_like(dn_ref)

    def stages(at, *calls):
        @pl.when(step == at)
        def _():
            for stage, i in calls:
                stage(order[i])

    one, two, three = work.stage_one, work.stage_two, work.stage_three
    stages(1, (one, 1), (one, 2))
    stages(2, (two, 1))
    stages(3, (two, 3), (three, 1))
    w_in = jnp.concatenate([wide(r, (0, p, 0), 0, 128, 8) for r in (wa_ref, wb_ref) for p in range(CS)], axis=0)
    w_out = jnp.concatenate([wide(r, (0, p, 0), 1024, 128, 8) for r in (wa_ref, wb_ref) for p in range(CS)], axis=0)
    bias = jnp.concatenate([r[0, p, 0, 2048:2049] for r in (wa_ref, wb_ref) for p in range(CS)], axis=1)
    x = mm(x_ref[...], w_in, NT) + bias.astype(jnp.float32)
    squared = x * x
    tanh = jnp.tanh(C0 * x * (1.0 + 0.044715 * squared))
    half = 0.5 * (1.0 + tanh)
    act = (x * half).astype(jnp.bfloat16)
    slope = half + 0.5 * x * (1.0 - tanh * tanh) * (C0 * (1.0 + 3 * 0.044715 * squared))
    hid = (mm(g_ref[...], w_out, NT) * slope).astype(jnp.bfloat16)
    stages(0, (one, 0))
    stages(1, (two, 0), (one, 3))
    stages(2, (three, 0), (two, 2))
    stages(3, (three, 2))
    out_ref[...] += mm(act, w_out)
    dn_ref[...] += mm(hid, w_in)
    bsum_ref[0] = jnp.sum(hid.astype(jnp.float32), axis=0, keepdims=True)
    out_part = mm(gt_ref[...], act).astype(jnp.bfloat16)
    in_part = mm(xt_ref[...], hid).astype(jnp.bfloat16)
    put_tiles(
        [jnp.concatenate([out_part[:, a * 256:(a + 1) * 256], in_part[:, a * 256:(a + 1) * 256]], axis=1)
         for a in range(XS)], keep_ref, send_ref)

    @pl.when(step == pl.num_programs(0) - 1)
    def _():
        work.finish(sum_ref)


def mlp_half(h, normed, normed_turned, branch, branch_turned, g2, keeps, sends):
    tokens, sets, width = normed.shape[0], len(keeps), sum(keep.shape[-1] for keep in keeps)
    one = lambda *dims: pl.BlockSpec(dims, lambda k: (0,) * len(dims), pipeline_mode=pl.Buffered(1))
    weight = lambda x: pl.BlockSpec((1, CS, 1, G2_ROWS, 128), lambda k: (h, 0, k * XS + x, 0, 0))
    views = g2.reshape(YS, CS, ZS * XS, G2_ROWS, 128)
    full = jax.ShapeDtypeStruct((tokens, D), jnp.float32)
    return pl.pallas_call(
        partial(mlp_kernel, sets),
        grid=(ZS,),
        in_specs=[one(tokens, D), one(D, tokens), one(tokens, D), one(D, tokens), weight(0), weight(1)]
        + [pl.BlockSpec(memory_space=pl.ANY)] * (2 * sets),
        out_specs=[one(tokens, D), one(tokens, D)] + tile_specs(512, lambda k: (0, 0, k, 0, 0))
        + [pl.BlockSpec((1, 1, 512), lambda k: (k, 0, 0)), one(PIECE, width)],
        scratch_shapes=reduction_scratch(sets, width),
        out_shape=[full, full] + tile_shapes(512)
        + [jax.ShapeDtypeStruct((ZS, 1, 512), jnp.float32), jax.ShapeDtypeStruct((PIECE, width), jnp.float32)],
        compiler_params=pltpu.CompilerParams(collective_id=2 + h, has_side_effects=True, vmem_limit_bytes=63 << 20),
        cost_estimate=pl.CostEstimate(flops=26 << 30, bytes_accessed=30 << 20, transcendentals=2 << 20),
        name="mlp",
    )(normed, normed_turned.reshape(D, tokens), branch, branch_turned.reshape(D, tokens), views, views, *keeps, *sends)


def output_kernel(ctx_ref, w_ref, gt_ref, out_ref, keep_ref, send_ref, acc_ref):
    step = pl.program_id(0)
    ctx = ctx_ref[...]

    @pl.when(step == 0)
    def _():
        acc_ref[...] = jnp.zeros_like(acc_ref)

    acc_ref[...] += mm(ctx, w_ref[...])
    put_tiles(by_x(mm(gt_ref[...], ctx).astype(jnp.bfloat16)), keep_ref, send_ref)

    @pl.when(step == pl.num_programs(0) - 1)
    def _():
        out_ref[...] = acc_ref[...].astype(jnp.bfloat16)


def row_output(context, w_output, branch_turned):
    tokens = context.shape[0]
    whole = lambda *dims: pl.BlockSpec(dims, lambda k: (0,) * len(dims), pipeline_mode=pl.Buffered(1))
    return pl.pallas_call(
        output_kernel,
        grid=(ZS,),
        in_specs=[
            pl.BlockSpec((tokens, 256), lambda k: (0, k)),
            pl.BlockSpec((256, D), lambda k: (k, 0)),
            whole(D, tokens),
        ],
        out_specs=[whole(tokens, D)] + tile_specs(128, lambda k: (0, 0, k, 0, 0)),
        scratch_shapes=[pltpu.VMEM((tokens, D), jnp.float32)],
        out_shape=[jax.ShapeDtypeStruct((tokens, D), jnp.bfloat16)] + tile_shapes(128),
        compiler_params=pltpu.CompilerParams(vmem_limit_bytes=63 << 20),
        cost_estimate=pl.CostEstimate(flops=4 << 30, bytes_accessed=12 << 20, transcendentals=0),
        name="row_output",
    )(context, w_output, branch_turned.reshape(D, tokens))


def on_device_rows(
    inputs,
    seg_lengths,
    group_counts,
    out_grad,
    ln_gain,
    ln_bias,
    w_query,
    w_key,
    w_value,
    w_output,
    w_in,
    b_in,
    w_out,
    b_out,
):
    row_count, own_tokens = inputs.shape[0], inputs.shape[1]
    tokens = row_count * own_tokens
    group, member = lax.axis_index("dp"), lax.axis_index("mp")
    place = jnp.stack([group, member]).astype(jnp.int32)

    def quarter(matrix, axis):
        size = matrix.shape[axis] // (YS * CS)
        return lax.dynamic_slice_in_dim(matrix, group * size, size, axis)

    def narrow(matrix):
        return matrix.reshape(matrix.shape[0], D // 128, 128).transpose(1, 0, 2).reshape(-1, 128)

    def exchange(tensor):
        blocks = tensor.reshape(row_count, own_tokens, D)
        return lax.all_to_all(blocks, "mp", 0, 0, tiled=True).reshape(tokens, D)

    counts = jnp.broadcast_to(group_counts.astype(jnp.float32)[:, None], (8, 128))
    g1 = jnp.concatenate(
        [quarter(w_query, 0), quarter(w_key, 0), quarter(w_value, 0), narrow(quarter(w_output, 0))], axis=0)
    bias_rows = jnp.pad(quarter(b_in, 0)[None], ((0, G2_ROWS - 2049), (0, 0)))
    g2 = jnp.concatenate([narrow(quarter(w_in, 0)), narrow(quarter(w_out, 0)), bias_rows], axis=0)
    normed, normed_turned, normed_row, grad_row, g1_all, counts_all = gather_all(
        inputs, ln_gain, ln_bias, counts, g1, out_grad)
    g2, normed_row = lax.optimization_barrier((g2, normed_row))
    g2_all = lax.all_gather(g2, ("dp", "mp"))
    normed = normed.reshape(tokens, D)
    weight = (YS * CS * counts_all[group, 0, 0] / jnp.sum(counts_all[:, 0, 0])).reshape(1, 1)

    flat_grad = out_grad.reshape(tokens, D)
    branch, branch_turned, row_turned, ctx_grad_row, w_output_all, out_sum = cotangent(
        place, flat_grad, grad_row, weight, g1_all)
    own_row = lax.dynamic_index_in_dim(seg_lengths, member, 0, keepdims=True)
    _, positions = segment_layout(own_row)
    positions = positions[0]
    cosines, sines = lane_tables(positions)
    starts = jnp.arange(SEQ, dtype=jnp.int32) - positions
    qkv = project(normed_row, g1_all, cosines, sines)
    context_row, qkv_grad = attention(qkv, ctx_grad_row, starts, cosines, sines)
    out_row, keep_o, send_o = row_output(context_row, w_output_all, row_turned)
    attn_out = exchange(out_row)
    normed_row_grad, keep_a, send_a = back(place, normed_row, g1_all, qkv_grad)
    out0, grad0, keep0, send0, bsum0, grads_a = mlp_half(
        0, normed, normed_turned, branch, branch_turned, g2_all, (keep_a, keep_o), (send_a, send_o))
    normed_row_grad, keep0 = lax.optimization_barrier((normed_row_grad, keep0))
    attn_grad = exchange(normed_row_grad)
    out1, grad1, keep1, send1, bsum1, grads0 = mlp_half(
        1, normed, normed_turned, branch, branch_turned, g2_all, (keep0,), (send0,))
    bsums = jnp.stack([bsum0, bsum1]).reshape(YS, ZS * XS, CS, 128)
    bsums = bsums.transpose(1, 0, 2, 3).reshape(ZS * XS, 4, 128)
    own = D // PLACES
    vectors = jnp.pad(out_sum.reshape(PLACES, 1, own), ((0, 0), (0, 3), (0, 128 - own)))
    small = jnp.concatenate([jnp.tile(bsums, (YS * CS, 1, 1)), vectors], axis=1)
    grads1, small, sums, input_grad, layer_out = reduce_tiles(
        (keep1,), (send1,), small, (inputs.reshape(tokens, D), flat_grad, attn_grad, grad0, grad1, attn_out, out0, out1),
        ln_gain, b_out, weight)
    sums = lax.dynamic_slice_in_dim(sums, (group * (ZS * XS) + member) * own, own, 1)
    shape = (row_count, own_tokens, D)
    return (
        layer_out.reshape(shape),
        input_grad.reshape(shape),
        sums[0],
        sums[1],
        grads_a[:, :128],
        grads_a[:, 128:256],
        grads_a[:, 256:384],
        grads_a[:, 384:].T,
        jnp.concatenate([grads0[:, 256:], grads1[:, 256:]], axis=1).T,
        small[:4].reshape(512),
        jnp.concatenate([grads0[:, :256], grads1[:, :256]], axis=1).T,
        small[4, :own],
    )


def solution(mesh):
    placed = (
        P("dp", "mp", None),
        P("dp", None),
        P("dp"),
        P("dp", "mp", None),
        P(),
        P(),
        P(None, "mp"),
        P(None, "mp"),
        P(None, "mp"),
        P("mp", None),
        P("mp", None),
        P("mp"),
        P("mp", None),
        P(),
    )
    sizes = (mesh.shape["dp"], mesh.shape["mp"])

    def on_device(*args):
        if sizes == (YS * CS, ZS * XS) and args[0].shape[0] == ZS * XS:
            return on_device_rows(*args)
        return on_device_gathered(*args)

    return jax.shard_map(
        on_device,
        mesh=mesh,
        in_specs=placed,
        out_specs=(
            P("dp", "mp", None),
            P("dp", "mp", None),
            P(("dp", "mp")),
            P(("dp", "mp")),
            P("dp", "mp"),
            P("dp", "mp"),
            P("dp", "mp"),
            P("mp", "dp"),
            P("mp", "dp"),
            P("mp"),
            P("mp", "dp"),
            P(("dp", "mp")),
        ),
        check_vma=False,
    )
```
